32 devices in a mesh: rep: 8 (over y, x, core), shard: 4 (over z).
Axes of the slice: x: 2, y: 2, z: 4, core: 2. Of those that a mesh axis runs over, the one named last changes fastest.
Arguments:
- tokens: bfloat16 [32, 512, 1024], P(('rep', 'shard')), may hold values from -6 to 6
- segments: int32 [32, 512], P(('rep', 'shard')), may hold values from 0 to 25, as said below
- lengths: int32 [32], P(('rep', 'shard')), may hold values from 449 to 512, as said below
- cotangent: bfloat16 [32, 512, 1024], P(('rep', 'shard')), may hold values from -6 to 6
- w_qkv: bfloat16 [1024, 3072], P('shard'), may hold values from -0.1875 to 0.1875
- b_qv: bfloat16 [2048], P('shard'), may hold values from -4 to 4
- w_out: bfloat16 [1024, 1024], P('shard'), may hold values from -0.5 to 0.5
- b_out: bfloat16 [1024], P('shard'), may hold values from -4 to 4
- gain_one: bfloat16 [1024], P('shard'), may hold values from 0.5 to 1.5
- shift_one: bfloat16 [1024], P('shard'), may hold values from -4 to 4
- w_in: bfloat16 [1024, 4096], P('shard'), may hold values from -0.1875 to 0.1875
- b_in: bfloat16 [4096], P('shard'), may hold values from -4 to 4
- w_down: bfloat16 [4096, 1024], P('shard'), may hold values from -0.09375 to 0.09375
- b_down: bfloat16 [1024], P('shard'), may hold values from -4 to 4
- gain_two: bfloat16 [1024], P('shard'), may hold values from 0.5 to 1.5
- shift_two: bfloat16 [1024], P('shard'), may hold values from -4 to 4
Outputs:
- layer_out: bfloat16 [32, 512, 1024], P(('rep', 'shard'))
- grad_tokens: float32 [32, 512, 1024], P(('rep', 'shard'))
- grad_w_qkv: float32 [1024, 3072], P('shard')
- grad_b_qv: float32 [2048], P('shard')
- grad_w_out: float32 [1024, 1024], P('shard')
- grad_b_out: float32 [1024], P('shard')
- grad_gain_one: float32 [1024], P('shard')
- grad_shift_one: float32 [1024], P('shard')
- grad_w_in: float32 [1024, 4096], P('shard')
- grad_b_in: float32 [4096], P('shard')
- grad_w_down: float32 [4096, 1024], P('shard')
- grad_b_down: float32 [1024], P('shard')
- grad_gain_two: float32 [1024], P('shard')
- grad_shift_two: float32 [1024], P('shard')
The draws below stay inside these ranges and needn't reach their ends.
Inputs may be any that keep to these rules, and one draw needn't show every extreme that they name: `segments`: within a sequence the document numbers start at 0 and never fall; every document spans 20 to 200 positions unless the sequence's end cuts it; the first sequence is made of documents of 20 positions. `lengths`: positions from a sequence's length on are padding; the first sequence has none, the second has the most.
All inputs are finite; a program needn't handle non-finite values.
Results may differ from the reference program's by a relative error of at most 0.019.
Values may be sent and summed in bfloat16 or wider, within the bound.
No kernel may reach another device: no remote copies, remote signals or barrier semaphores. Data moves between devices by JAX's collectives and lax.ppermute only.
A program may use at most 192 MiB of HBM per device.

```python
import jax
import jax.numpy as jnp
from jax import lax

D = 1024
HEAD_DIM = 64
FF = 4096
LEN = 512
SEQS = 32


def packing(key):
    base = jax.random.fold_in(key, 7)
    first_key = jax.random.fold_in(base, 1)
    second_key = jax.random.fold_in(base, 2)
    max_docs = LEN // 20 + 1
    doc_sizes = jax.random.randint(first_key, (SEQS, max_docs), 20, 201)
    doc_sizes = jnp.where(jnp.arange(SEQS)[:, None] == 0, 20, doc_sizes)
    doc_ends = jnp.cumsum(doc_sizes, axis=1)
    positions = jnp.arange(LEN)
    doc_ids = jnp.sum((positions[None, :, None] >= doc_ends[:, None, :]).astype(jnp.int32), axis=2)
    padding = jax.random.randint(second_key, (SEQS,), 0, LEN // 8)
    seq_index = jnp.arange(SEQS)
    padding = jnp.where(seq_index == 0, 0, padding)
    padding = jnp.where(seq_index == 1, LEN // 8 - 1, padding)
    return (doc_ids.astype(jnp.int32), (LEN - padding).astype(jnp.int32))


def draw_segments(key, part):
    return packing(key)[0]


def draw_lengths(key, part):
    return packing(key)[1]


def shard_levels(own_key, shape, cuts, smallest, top_value):
    loudness, own = 1.0, jax.random.fold_in(own_key, 6)
    for dim, shards_of in cuts:
        draws = jnp.exp(jax.random.uniform(jax.random.fold_in(own, dim), (shards_of,), jnp.float32, smallest / len(cuts), top_value / len(cuts)))
        loudness = loudness * jnp.repeat(draws, shape[dim] // shards_of).reshape([-1 if axis == dim else 1 for axis in range(len(shape))])
    return loudness


def normal_values(own_key, shape, deviation, bound, split=(), dtype=jnp.bfloat16):
    values = jax.random.normal(own_key, shape, jnp.float32) * deviation
    if len(split) > 0:
        values = shard_levels(own_key, shape, split, -0.22, 0.18) * values
    return jnp.clip(values, min=-bound, max=bound).astype(dtype)


def setup_inputs(seed: int = 0) -> dict:
    streams_of = jax.random.split(jax.random.key(seed), 17)
    tokens = normal_values(streams_of[0], (SEQS, LEN, D), 1.0, 6.0, ((0, 32),))
    segments = draw_segments(jax.random.fold_in(streams_of[16], 71), 0)
    lengths = draw_lengths(jax.random.fold_in(streams_of[16], 71), 0)
    cotangent = normal_values(streams_of[3], (SEQS, LEN, D), 1.0, 6.0, ((0, 32),))
    w_qkv = normal_values(streams_of[4], (D, 3 * D), D ** -0.5, 0.1875, ((0, 4),))
    b_qv = normal_values(streams_of[5], (2 * D,), 0.3, 4.0, ((0, 4),))
    w_out = normal_values(streams_of[6], (D, D), (D // 8) ** -0.5, 0.5, ((0, 4),))
    b_out = normal_values(streams_of[7], (D,), 0.3, 4.0, ((0, 4),))
    gain_one = jnp.clip(1.0 + 0.1 * jax.random.normal(streams_of[8], (D,), jnp.float32), 0.5, 1.5).astype(jnp.bfloat16)
    shift_one = normal_values(streams_of[9], (D,), 0.3, 4.0, ((0, 4),))
    w_in = normal_values(streams_of[10], (D, FF), D ** -0.5, 0.1875, ((0, 4),))
    b_in = normal_values(streams_of[11], (FF,), 0.3, 4.0, ((0, 4),))
    w_down = normal_values(streams_of[12], (FF, D), FF ** -0.5, 0.09375, ((0, 4),))
    b_down = normal_values(streams_of[13], (D,), 0.3, 4.0, ((0, 4),))
    gain_two = jnp.clip(1.0 + 0.1 * jax.random.normal(streams_of[14], (D,), jnp.float32), 0.5, 1.5).astype(jnp.bfloat16)
    shift_two = normal_values(streams_of[15], (D,), 0.3, 4.0, ((0, 4),))
    return dict(tokens=tokens, segments=segments, lengths=lengths, cotangent=cotangent, w_qkv=w_qkv, b_qv=b_qv, w_out=w_out, b_out=b_out, gain_one=gain_one, shift_one=shift_one, w_in=w_in, b_in=b_in, w_down=w_down, b_down=b_down, gain_two=gain_two, shift_two=shift_two)


@jax.custom_vjp
def low(v):
    return lax.optimization_barrier(v.astype(jnp.bfloat16)).astype(jnp.float32)

@jax.custom_vjp
def low_back(v):
    return v

def low_keep(v):
    return (low(v), None)

def low_pass(kept, grad):
    return (grad,)

def back_keep(v):
    return (v, None)

def back_low(kept, grad):
    return (low(grad),)
low.defvjp(low_keep, low_pass)
low_back.defvjp(back_keep, back_low)

def matmul(left, right):
    return jnp.dot(left, right, precision=lax.Precision.HIGHEST)

def layer_norm(hidden, norm_gain, norm_shift):
    average = lax.optimization_barrier(jnp.mean(hidden, axis=-1, keepdims=True))
    centred = hidden - average
    variance = lax.optimization_barrier(jnp.mean(centred * centred, axis=-1, keepdims=True))
    return centred * lax.rsqrt(variance + 1e-06) * norm_gain + norm_shift

def layer_forward(params, inputs, doc_ids, length):
    w_qkv, b_qv, w_out, b_out, gain_one, shift_one, w_in, b_in, w_down, b_down, gain_two, shift_two = params
    num_heads = D // HEAD_DIM
    projected = matmul(inputs, w_qkv)
    queries = low(low_back(projected[:, :D] + b_qv[:D]))
    key_rows = low(low_back(projected[:, D:2 * D]))
    value_rows = low(low_back(projected[:, 2 * D:] + b_qv[D:]))
    query_heads = queries.reshape(LEN, num_heads, HEAD_DIM)
    key_heads = key_rows.reshape(LEN, num_heads, HEAD_DIM)
    value_heads = value_rows.reshape(LEN, num_heads, HEAD_DIM)
    positions = jnp.arange(LEN)
    is_valid = positions < length
    allowed = (doc_ids[:, None] == doc_ids[None, :]) & (is_valid[:, None] == is_valid[None, :])
    scores = jnp.einsum('qhd,khd->hqk', query_heads, key_heads, precision=lax.Precision.HIGHEST) * HEAD_DIM ** (-0.5)
    scores = low_back(scores)
    scores = jnp.where(allowed[None], scores, -1e+30)
    attn_probs = low(jax.nn.softmax(scores, axis=-1))
    context = jnp.einsum('hqk,khd->qhd', attn_probs, value_heads, precision=lax.Precision.HIGHEST).reshape(LEN, D)
    context = low(low_back(context))
    attn_out = low_back(matmul(context, w_out) + b_out)
    first_sum = inputs + attn_out
    normed_one = layer_norm(first_sum, gain_one, shift_one)
    inner = low_back(matmul(low(normed_one), w_in) + b_in)
    activated = low(jax.nn.gelu(inner, approximate=False))
    branch = low_back(matmul(activated, w_down) + b_down)
    return layer_norm(normed_one + branch, gain_two, shift_two)

def reference(tokens, segments, lengths, cotangent, w_qkv, b_qv, w_out, b_out, gain_one, shift_one, w_in, b_in, w_down, b_down, gain_two, shift_two):
    params = tuple((weight.astype(jnp.float32) for weight in (w_qkv, b_qv, w_out, b_out, gain_one, shift_one, w_in, b_in, w_down, b_down, gain_two, shift_two)))

    def one_sequence(carry, items):
        seq_tokens, doc_ids, length, seq_cot = items

        def forward(*inputs):
            return layer_forward(inputs[:-1], inputs[-1], doc_ids, length)
        result, back_fn = jax.vjp(forward, *params, seq_tokens.astype(jnp.float32))
        grads = back_fn(seq_cot.astype(jnp.float32))
        carry = tuple((left + right for left, right in zip(carry, grads[:-1])))
        return (carry, (result.astype(jnp.bfloat16), grads[-1]))
    zeros = tuple((jnp.zeros_like(weight) for weight in params))
    sums, (results, grad_inputs) = lax.scan(one_sequence, zeros, (tokens, segments, lengths, cotangent))
    return (results, grad_inputs, sums[0], sums[1], sums[2], sums[3], sums[4], sums[5], sums[6], sums[7], sums[8], sums[9], sums[10], sums[11])
```

```python
from functools import partial

import jax
import jax.numpy as jnp
from jax import lax
from jax.sharding import Mesh
from jax.sharding import PartitionSpec as P

HEAD_DIM = 64
REP = ("chip", "core")
ALL = ("chip", "core", "shard")


def layer_norm(hidden, norm_gain, norm_shift):
    average = jnp.mean(hidden, axis=-1, keepdims=True)
    centred = hidden - average
    variance = jnp.mean(centred * centred, axis=-1, keepdims=True)
    return centred * lax.rsqrt(variance + 1e-06) * norm_gain + norm_shift


def matmul(left, right):
    return jnp.dot(left, right, preferred_element_type=jnp.float32)


def project_back(left, right):
    return lax.dot_general(
        left, right, (((1,), (1,)), ((), ())), preferred_element_type=jnp.float32
    )


def outer_sum(left, right):
    return lax.dot_general(
        left, right, (((0,), (0,)), ((), ())), preferred_element_type=jnp.float32
    )


def column_sum(values):
    return jnp.sum(values.astype(jnp.float32), axis=0)


def allowed_pairs(doc_ids, length):
    positions = jnp.arange(doc_ids.shape[0])
    is_valid = positions < length
    return (doc_ids[:, None] == doc_ids[None, :]) & (is_valid[:, None] == is_valid[None, :])


def attend(query_heads, key_heads, value_heads, allowed):
    scale = HEAD_DIM ** (-0.5)
    scores = (
        jnp.einsum("qhd,khd->hqk", query_heads, key_heads, preferred_element_type=jnp.float32)
        * scale
    )
    scores = jnp.where(allowed[None], scores, -1e30)
    maxima = jnp.max(scores, axis=2, keepdims=True)
    expo = jnp.exp(scores - maxima)
    totals = jnp.sum(expo, axis=2, keepdims=True)
    attn_probs = (expo / totals).astype(jnp.bfloat16)
    context = jnp.einsum(
        "hqk,khd->qhd", attn_probs, value_heads, preferred_element_type=jnp.float32
    )
    return (context.astype(jnp.bfloat16), maxima + jnp.log(totals))


def attend_back(query_heads, key_heads, value_heads, grad_context, allowed, log_totals):
    scale = HEAD_DIM ** (-0.5)
    scores = (
        jnp.einsum("qhd,khd->hqk", query_heads, key_heads, preferred_element_type=jnp.float32)
        * scale
    )
    scores = jnp.where(allowed[None], scores, -1e30)
    attn_probs = jnp.exp(scores - log_totals)
    grad_probs = jnp.einsum(
        "qhd,khd->hqk", grad_context, value_heads, preferred_element_type=jnp.float32
    )
    grad_scores = attn_probs * (
        grad_probs - jnp.sum(attn_probs * grad_probs, axis=2, keepdims=True)
    )
    grad_low = grad_scores.astype(jnp.bfloat16)
    grad_query = (
        jnp.einsum("hqk,khd->qhd", grad_low, key_heads, preferred_element_type=jnp.float32) * scale
    )
    grad_key = (
        jnp.einsum("hqk,qhd->khd", grad_low, query_heads, preferred_element_type=jnp.float32)
        * scale
    )
    grad_value = jnp.einsum(
        "hqk,qhd->khd",
        attn_probs.astype(jnp.bfloat16),
        grad_context,
        preferred_element_type=jnp.float32,
    )
    return (
        grad_query.astype(jnp.bfloat16),
        grad_key.astype(jnp.bfloat16),
        grad_value.astype(jnp.bfloat16),
    )


def local(
    chips,
    group,
    tokens,
    segments,
    lengths,
    cotangent,
    w_qkv,
    b_qv,
    w_out,
    b_out,
    gain_one,
    shift_one,
    w_in,
    b_in,
    w_down,
    b_down,
    gain_two,
    shift_two,
):
    reps = 2 * chips
    core = lax.axis_index("core")
    rank = lax.axis_index("chip") * 2 + core
    own = lax.axis_index("shard")
    _, seq_len, model_width = tokens.shape
    num_heads = model_width // HEAD_DIM
    split_shape = (seq_len, num_heads, HEAD_DIM)
    ff_rows = w_down.shape[0]
    ff_width = w_in.shape[1]
    qkv_width = w_qkv.shape[1]

    def from_shard(value, step):
        return lax.ppermute(value, "shard", [(i, (i - step) % group) for i in range(group)])

    def to_shard(value, step):
        return lax.ppermute(value, "shard", [(i, (i + step) % group) for i in range(group)])

    def sibling(value):
        return lax.ppermute(value, "core", [(0, 1), (1, 0)])

    def roll_left(value, width):
        twice = jnp.concatenate([value, value], axis=1)
        return lax.dynamic_slice_in_dim(twice, own * width, value.shape[1], axis=1)

    def roll_right(value, width):
        twice = jnp.concatenate([value, value], axis=1)
        start = ((group - own) % group) * width
        return lax.dynamic_slice_in_dim(twice, start, value.shape[1], axis=1)

    vectors = (b_qv, b_out, gain_one, shift_one, b_in, b_down, gain_two, shift_two)
    sizes = [v.shape[0] for v in vectors]
    w_one = jnp.concatenate([w_qkv, w_out], axis=1)
    part = w_one.shape[1] // reps
    rows = w_one.shape[0]
    packed = jnp.concatenate(vectors)
    extra = -(-packed.shape[0] // (16 * part)) * 16
    packed = jnp.pad(packed, (0, extra * part - packed.shape[0])).reshape(extra, part)
    piece_one = jnp.concatenate(
        [lax.dynamic_slice_in_dim(w_one, rank * part, part, axis=1), packed], axis=0
    )
    part_in = ff_width // reps
    piece_in = lax.dynamic_slice_in_dim(w_in, rank * part_in, part_in, axis=1)
    part_down = ff_rows // reps
    piece_down = lax.dynamic_slice_in_dim(w_down, rank * part_down, part_down, axis=0)

    got_one = [from_shard(piece_one, s) for s in range(1, group)]
    got_in = [from_shard(piece_in, s) for s in range(1, group)]
    got_down = [from_shard(piece_down, s) for s in range(1, group)]
    rest_one = lax.all_gather(
        jnp.concatenate([g[:rows] for g in got_one], axis=0), REP, axis=1, tiled=True
    )
    rest_in = lax.all_gather(jnp.concatenate(got_in, axis=0), REP, axis=1, tiled=True)
    rest_down = lax.all_gather(jnp.stack(got_down), REP, axis=1, tiled=True)
    rest_down = rest_down.reshape(-1, model_width)

    relative = jnp.stack([packed.reshape(-1)] + [g[rows:].reshape(-1) for g in got_one])
    natural = jnp.concatenate([relative, relative], axis=0)
    natural = lax.dynamic_slice_in_dim(natural, (group - own) % group, group, axis=0)
    full, start = [], 0
    for size in sizes:
        full.append(natural[:, start : start + size].reshape(-1).astype(jnp.float32))
        start += size
    bias_qv, bias_out, norm_gone, norm_sone, bias_in, bias_down, norm_gtwo, norm_stwo = full

    own_qkv, own_out = w_qkv, w_out
    rest_qkv, rest_out = rest_one[:, :qkv_width], rest_one[:, qkv_width:]

    flat_in = tokens[0]
    in_rel = roll_left(flat_in, rows)
    projected = matmul(in_rel[:, :rows], own_qkv) + matmul(in_rel[:, rows:], rest_qkv)
    queries = (projected[:, :model_width] + bias_qv[:model_width]).astype(jnp.bfloat16)
    key_rows = projected[:, model_width : 2 * model_width].astype(jnp.bfloat16)
    value_rows = (projected[:, 2 * model_width :] + bias_qv[model_width:]).astype(jnp.bfloat16)
    query_heads = queries.reshape(split_shape)
    key_heads = key_rows.reshape(split_shape)
    value_heads = value_rows.reshape(split_shape)
    allowed = allowed_pairs(segments[0], lengths[0])
    context, log_totals = attend(query_heads, key_heads, value_heads, allowed)
    context_rel = roll_left(context.reshape(-1, model_width), rows)
    attn_out = (
        matmul(context_rel[:, :rows], own_out)
        + matmul(context_rel[:, rows:], rest_out)
        + bias_out
    )
    first_sum = flat_in.astype(jnp.float32) + attn_out
    normed_one = layer_norm(first_sum, norm_gone, norm_sone)
    normed_rel = roll_left(normed_one.astype(jnp.bfloat16), rows)
    inner = matmul(normed_rel[:, :rows], w_in) + matmul(normed_rel[:, rows:], rest_in) + bias_in
    activated = jax.nn.gelu(inner, approximate=False)
    act_rel = roll_left(activated.astype(jnp.bfloat16), ff_rows)
    branch = (
        matmul(act_rel[:, :ff_rows], w_down) + matmul(act_rel[:, ff_rows:], rest_down) + bias_down
    )
    second_sum = normed_one + branch
    output_rows = layer_norm(second_sum, norm_gtwo, norm_stwo)

    def half(value, width, which):
        split = value.reshape(seq_len, -1, 2, width)
        return lax.dynamic_index_in_dim(split, which, axis=2, keepdims=False).reshape(seq_len, -1)

    def pair(value, width):
        return half(value, width, core), sibling(half(value, width, 1 - core))

    def both(left, right):
        return outer_sum(left[0], right[0]) + outer_sum(left[1], right[1])

    in_pair = (in_rel, sibling(in_rel))
    context_pair = (context_rel, sibling(context_rel))
    normed_pair = (normed_rel, sibling(normed_rel))
    act_pair = pair(act_rel, part_down)

    def own_sum(parts):
        total = parts[0].astype(jnp.float32)
        for s in range(1, group):
            total = total + to_shard(parts[s], s).astype(jnp.float32)
        return total.astype(jnp.bfloat16)

    def scatter_columns(grad):
        share = lax.psum_scatter(
            grad.astype(jnp.bfloat16), "chip", scatter_dimension=1, tiled=True
        )
        share = own_sum(share.reshape(group, rows, -1))
        return lax.all_gather(share, REP, axis=1, tiled=True).astype(jnp.float32)

    grad_rows = cotangent[0].astype(jnp.float32)
    _, norm_two_back = jax.vjp(layer_norm, second_sum, norm_gtwo, norm_stwo)
    grad_second, grad_gtwo, grad_stwo = norm_two_back(grad_rows)
    grad_branch = grad_second.astype(jnp.bfloat16)
    branch_pair = (grad_branch, sibling(grad_branch))
    grad_bdown = column_sum(grad_branch)
    grad_down = both(act_pair, branch_pair).astype(jnp.bfloat16)
    grad_down = lax.psum_scatter(
        grad_down.reshape(group, chips * part_down, model_width),
        "chip",
        scatter_dimension=1,
        tiled=True,
    )
    grad_wdown = lax.all_gather(own_sum(grad_down), REP, axis=0, tiled=True).astype(jnp.float32)

    grad_act = jnp.concatenate(
        [project_back(grad_branch, w_down), project_back(grad_branch, rest_down)], axis=1
    )
    grad_act = roll_right(grad_act, ff_rows)
    _, gelu_back = jax.vjp(partial(jax.nn.gelu, approximate=False), inner)
    grad_inner = gelu_back(grad_act)[0].astype(jnp.bfloat16)
    grad_win = scatter_columns(both(normed_pair, pair(grad_inner, part_in)))
    grad_bin = column_sum(grad_inner)
    back_in = jnp.concatenate(
        [project_back(grad_inner, w_in), project_back(grad_inner, rest_in)], axis=1
    )
    grad_normed = grad_second + roll_right(back_in, rows)
    _, norm_one_back = jax.vjp(layer_norm, first_sum, norm_gone, norm_sone)
    grad_first, grad_gone, grad_sone = norm_one_back(grad_normed)
    grad_attn = grad_first.astype(jnp.bfloat16)
    half_out = both(context_pair, pair(grad_attn, part))
    grad_bout = column_sum(grad_attn)
    grad_context = jnp.concatenate(
        [project_back(grad_attn, own_out), project_back(grad_attn, rest_out)], axis=1
    ).astype(jnp.bfloat16)
    grad_context = roll_right(grad_context, rows).reshape(split_shape)
    grad_query, grad_key, grad_value = attend_back(
        query_heads, key_heads, value_heads, grad_context, allowed, log_totals
    )
    grad_query = grad_query.reshape(-1, model_width)
    grad_key = grad_key.reshape(-1, model_width)
    grad_value = grad_value.reshape(-1, model_width)
    grad_proj = jnp.concatenate([grad_query, grad_key, grad_value], axis=1)
    half_qkv = both(in_pair, pair(grad_proj, part))
    grad_one = scatter_columns(jnp.concatenate([half_qkv, half_out], axis=1))
    back_proj = jnp.concatenate(
        [project_back(grad_proj, own_qkv), project_back(grad_proj, rest_qkv)], axis=1
    )
    grad_input = grad_first + roll_right(back_proj, rows)

    small = (
        jnp.concatenate([column_sum(grad_query), column_sum(grad_value)]),
        grad_bout,
        grad_gone,
        grad_sone,
        grad_bin,
        grad_bdown,
        grad_gtwo,
        grad_stwo,
    )
    small = jnp.concatenate([v.reshape(group, -1) for v in small], axis=1)
    small = lax.psum(small, ALL)
    small = lax.dynamic_index_in_dim(small, own, axis=0, keepdims=False)
    vecs, start = [], 0
    for size in sizes:
        vecs.append(small[start : start + size])
        start += size

    return (
        output_rows.astype(jnp.bfloat16).reshape(tokens.shape),
        grad_input.reshape(tokens.shape),
        grad_one[:, :qkv_width],
        vecs[0],
        grad_one[:, qkv_width:],
        vecs[1],
        vecs[2],
        vecs[3],
        grad_win,
        vecs[4],
        grad_wdown,
        vecs[5],
        vecs[6],
        vecs[7],
    )


def solution(mesh):
    reps, group = mesh.devices.shape
    fine = Mesh(mesh.devices.reshape(reps // 2, 2, group), ALL)
    rows = P(ALL, None, None)
    matrix = P("shard", None)
    vector = P("shard")
    in_specs = (
        rows,
        P(ALL, None),
        P(ALL),
        rows,
        matrix,
        vector,
        matrix,
        vector,
        vector,
        vector,
        matrix,
        vector,
        matrix,
        vector,
        vector,
        vector,
    )
    out_specs = (
        rows,
        rows,
        matrix,
        vector,
        matrix,
        vector,
        vector,
        vector,
        matrix,
        vector,
        matrix,
        vector,
        vector,
        vector,
    )
    return jax.shard_map(
        partial(local, reps // 2, group),
        mesh=fine,
        in_specs=in_specs,
        out_specs=out_specs,
        check_vma=False,
    )
```

```python
from functools import partial

import jax
import jax.numpy as jnp
from jax import lax
from jax.experimental import pallas as pl
from jax.experimental.pallas import tpu as pltpu
from jax.sharding import Mesh
from jax.sharding import PartitionSpec as P

HEAD_DIM = 64
REP = ("chip", "core")
ALL = ("chip", "core", "shard")
F32 = jnp.float32
BF16 = jnp.bfloat16
VMEM_LIMIT = 60 * 1024 * 1024


def dot(left, right):
    return jnp.dot(left, right, preferred_element_type=F32)


def dot_t(left, right):
    return lax.dot_general(left, right, (((1,), (1,)), ((), ())), preferred_element_type=F32)


def t_dot(left, right):
    return lax.dot_general(left, right, (((0,), (0,)), ((), ())), preferred_element_type=F32)


def call(body, grid, ins, outs, out_shape, scratch=(), flops=0, moved=0):
    return pl.pallas_call(
        body,
        grid_spec=pltpu.PrefetchScalarGridSpec(
            num_scalar_prefetch=1,
            grid=grid,
            in_specs=ins,
            out_specs=outs,
            scratch_shapes=list(scratch),
        ),
        out_shape=out_shape,
        compiler_params=pltpu.CompilerParams(
            dimension_semantics=("arbitrary",) * len(grid), vmem_limit_bytes=VMEM_LIMIT
        ),
        cost_estimate=pl.CostEstimate(flops=flops, bytes_accessed=moved, transcendentals=0),
    )


def spec(shape, index):
    return pl.BlockSpec(shape, index)


def fixed(shape):
    zeros = (0,) * len(shape)
    return pl.BlockSpec(shape, lambda *_: zeros)


def struct(shape, dtype):
    return jax.ShapeDtypeStruct(shape, dtype)


def natural(where, step, group):
    return lax.rem(where[0] + step, group)


def normalise(hidden):
    average = jnp.mean(hidden, axis=-1, keepdims=True)
    centred = hidden - average
    variance = jnp.mean(centred * centred, axis=-1, keepdims=True)
    inverse = lax.rsqrt(variance + 1e-06)
    return centred * inverse, inverse


def normalise_back(grad, unit, inverse, gain):
    scaled = grad * gain
    first = jnp.mean(scaled, axis=-1, keepdims=True)
    second = jnp.mean(scaled * unit, axis=-1, keepdims=True)
    return inverse * (scaled - first - unit * second)


def rows_sum(value):
    return jnp.sum(value, axis=0, keepdims=True)


def qkv_kernel(group, where, x, own, rest, bias, out, rolled):
    rows = own.shape[0]

    @pl.when(pl.program_id(0) == 0)
    def _():
        for s in range(group):
            start = pl.multiple_of(natural(where, s, group) * rows, 128)
            rolled[:, s * rows : (s + 1) * rows] = x[:, pl.ds(start, rows)]

    total = dot(rolled[:, :rows], own[...]) + dot(rolled[:, rows:], rest[...])
    out[...] = (total + bias[...]).astype(BF16)


def qkv(where, x, w_qkv, rest_one, bias, group):
    seq, width = x.shape
    rows, columns = w_qkv.shape
    block = 512
    return call(
        partial(qkv_kernel, group),
        (columns // block,),
        [
            fixed((seq, width)),
            spec((rows, block), lambda j, w: (0, j)),
            spec((width - rows, block), lambda j, w: (0, j)),
            spec((1, block), lambda j, w: (0, j)),
        ],
        spec((seq, block), lambda j, w: (0, j)),
        struct((seq, columns), BF16),
        [pltpu.VMEM((seq, width), BF16)],
        flops=2 * seq * width * columns,
        moved=2 * (width * columns + seq * columns),
    )(where, x, w_qkv, rest_one, bias)


def attend_kernel(where, q, k, v, column, row, out, log_totals, bias):
    step = pl.program_id(0)
    seq = q.shape[0]

    @pl.when(step == 0)
    def _():
        bias[...] = jnp.where(column[...] == row[...], 0.0, -1e30)
        log_totals[...] = jnp.zeros_like(log_totals)

    lanes = lax.broadcasted_iota(jnp.int32, (1, 128), 1)
    heads = q.shape[1] // HEAD_DIM
    for h in range(heads):
        part = slice(h * HEAD_DIM, (h + 1) * HEAD_DIM)
        scores = dot_t(q[:, part] * BF16(HEAD_DIM**-0.5), k[:, part]) + bias[...]
        maxima = jnp.max(scores, axis=1, keepdims=True)
        expo = jnp.exp(scores - maxima)
        totals = jnp.sum(expo, axis=1, keepdims=True)
        probs = (expo * (1.0 / totals)).astype(BF16)
        out[:, part] = dot(probs, v[:, part]).astype(BF16)
        log_totals[...] = jnp.where(
            lanes == step * heads + h, maxima + jnp.log(totals), log_totals[...]
        )


def attention(where, projected, column, row, width):
    seq = projected.shape[0]
    block = 2 * HEAD_DIM
    count = width // block
    return call(
        attend_kernel,
        (count,),
        [
            spec((seq, block), lambda h, w: (0, h)),
            spec((seq, block), lambda h, w: (0, count + h)),
            spec((seq, block), lambda h, w: (0, 2 * count + h)),
            fixed((seq, 1)),
            fixed((1, seq)),
        ],
        [spec((seq, block), lambda h, w: (0, h)), fixed((seq, 128))],
        [struct((seq, width), BF16), struct((seq, 128), F32)],
        [pltpu.VMEM((seq, seq), F32)],
        flops=4 * seq * seq * width,
        moved=8 * seq * width,
    )(where, projected, projected, projected, column, row)


def attend_back_kernel(where, q, k, v, grad, log_totals, column, row, out, sums, bias):
    step = pl.program_id(0)

    @pl.when(step == 0)
    def _():
        bias[...] = jnp.where(column[...] == row[...], 0.0, -1e30)

    lanes = lax.broadcasted_iota(jnp.int32, (1, 128), 1)
    heads = q.shape[1] // HEAD_DIM
    for h in range(heads):
        part = slice(h * HEAD_DIM, (h + 1) * HEAD_DIM)
        picked = jnp.where(lanes == step * heads + h, log_totals[...], 0.0)
        logs = jnp.sum(picked, axis=1, keepdims=True)
        query = q[:, part] * BF16(HEAD_DIM**-0.5)
        scores = dot_t(query, k[:, part]) + bias[...]
        probs = jnp.exp(scores - logs)
        grad_probs = dot_t(grad[:, part], v[:, part])
        weighted = probs * grad_probs
        low = (weighted - probs * jnp.sum(weighted, axis=1, keepdims=True)).astype(BF16)
        grad_q = (dot(low, k[:, part]) * (HEAD_DIM**-0.5)).astype(BF16)
        grad_k = t_dot(low, query).astype(BF16)
        grad_v = t_dot(probs.astype(BF16), grad[:, part]).astype(BF16)
        out[0, :, part] = grad_q
        out[1, :, part] = grad_k
        out[2, :, part] = grad_v
        sums[0, :, part] = rows_sum(grad_q.astype(F32))
        sums[1, :, part] = rows_sum(grad_k.astype(F32))
        sums[2, :, part] = rows_sum(grad_v.astype(F32))


def attention_back(where, projected, grad, log_totals, column, row):
    seq, width = grad.shape
    block = 2 * HEAD_DIM
    count = width // block
    return call(
        attend_back_kernel,
        (count,),
        [
            spec((seq, block), lambda h, w: (0, h)),
            spec((seq, block), lambda h, w: (0, count + h)),
            spec((seq, block), lambda h, w: (0, 2 * count + h)),
            spec((seq, block), lambda h, w: (0, h)),
            fixed((seq, 128)),
            fixed((seq, 1)),
            fixed((1, seq)),
        ],
        [
            spec((3, seq, block), lambda h, w: (0, 0, h)),
            spec((3, 1, block), lambda h, w: (0, 0, h)),
        ],
        [struct((3, seq, width), BF16), struct((3, 1, width), F32)],
        [pltpu.VMEM((seq, seq), F32)],
        flops=10 * seq * seq * width,
        moved=14 * seq * width,
    )(where, projected, projected, projected, grad, log_totals, column, row)


def out_kernel(group, where, context, x, own, rest, bias, gain, shift, hidden, low):
    rows = own.shape[0]
    total = bias[...] + x[...].astype(F32)
    for s in range(group):
        start = pl.multiple_of(natural(where, s, group) * rows, 128)
        weight = own[...] if s == 0 else rest[(s - 1) * rows : s * rows, :]
        total = total + dot(context[:, pl.ds(start, rows)], weight)
    hidden[...] = total
    unit, _ = normalise(total)
    low[...] = (unit * gain[...] + shift[...]).astype(BF16)


def out_norm(where, context, x, w_out, rest_one, bias, gain, shift, group):
    seq, width = x.shape
    rows = w_out.shape[0]
    last = rest_one.shape[1] // width - 1
    block = seq // 2
    vector = fixed((1, width))
    return call(
        partial(out_kernel, group),
        (seq // block,),
        [
            spec((block, width), lambda i, w: (i, 0)),
            spec((block, width), lambda i, w: (i, 0)),
            fixed((rows, width)),
            spec((width - rows, width), lambda i, w: (0, last)),
            vector,
            vector,
            vector,
        ],
        [spec((block, width), lambda i, w: (i, 0))] * 2,
        [struct((seq, width), F32), struct((seq, width), BF16)],
        flops=2 * seq * width * width,
        moved=2 * width * width + 10 * seq * width,
    )(where, context, x, w_out, rest_one, bias, gain, shift)


def inner_kernel(group, where, x, own, rest, bias, act, slope, rolled):
    rows = own.shape[0]

    @pl.when(pl.program_id(0) == 0)
    def _():
        for s in range(group):
            start = pl.multiple_of(natural(where, s, group) * rows, 128)
            rolled[:, s * rows : (s + 1) * rows] = x[:, pl.ds(start, rows)]

    total = dot(rolled[:, :rows], own[...]) + dot(rolled[:, rows:], rest[...])
    total = total + bias[...]
    below = 0.5 + 0.5 * lax.erf(total * (0.5**0.5))
    act[...] = (total * below).astype(BF16)
    density = jnp.exp(-0.5 * total * total) * ((2.0 * jnp.pi) ** -0.5)
    slope[...] = (below + total * density).astype(BF16)


def inner(where, x, w_in, rest_in, bias, group):
    seq, width = x.shape
    rows, columns = w_in.shape
    block = 512
    return call(
        partial(inner_kernel, group),
        (columns // block,),
        [
            fixed((seq, width)),
            spec((rows, block), lambda j, w: (0, j)),
            spec((width - rows, block), lambda j, w: (0, j)),
            spec((1, block), lambda j, w: (0, j)),
        ],
        [spec((seq, block), lambda j, w: (0, j))] * 2,
        [struct((seq, columns), BF16)] * 2,
        [pltpu.VMEM((seq, width), BF16)],
        flops=2 * seq * width * columns,
        moved=2 * (width * columns + 2 * seq * columns),
    )(where, x, w_in, rest_in, bias)


def outer_kernel(
    group,
    where,
    act,
    own,
    rest,
    hidden,
    cotangent,
    gain_one,
    shift_one,
    bias,
    gain_two,
    shift_two,
    out,
    grad,
    low,
    sums,
    total,
):
    step = pl.program_id(0)

    @pl.when(step == 0)
    def _():
        total[...] = dot(act[...], own[...])

    @pl.when(step > 0)
    def _():
        total[...] += dot(act[...], rest[...])

    @pl.when(step == group - 1)
    def _():
        unit_one, _ = normalise(hidden[...])
        second = unit_one * gain_one[...] + shift_one[...] + total[...] + bias[...]
        unit, inverse = normalise(second)
        out[...] = (unit * gain_two[...] + shift_two[...]).astype(BF16)
        given = cotangent[...].astype(F32)
        back = normalise_back(given, unit, inverse, gain_two[...])
        grad[...] = back
        rounded = back.astype(BF16)
        low[...] = rounded
        sums[0:1, :] = rows_sum(given * unit)
        sums[1:2, :] = rows_sum(given)
        sums[2:3, :] = rows_sum(rounded.astype(F32))


def outer(where, act, w_down, rest_down, hidden, cotangent, vectors, group):
    seq, width = hidden.shape
    rows = w_down.shape[0]
    full = fixed((seq, width))
    vector = fixed((1, width))
    return call(
        partial(outer_kernel, group),
        (group,),
        [
            spec((seq, rows), lambda s, w: (0, natural(w, s, group))),
            fixed((rows, width)),
            spec((rows, width), lambda s, w: (jnp.maximum(s - 1, 0), 0)),
            full,
            full,
        ]
        + [vector] * 5,
        [full, full, full, fixed((8, width))],
        [
            struct((seq, width), BF16),
            struct((seq, width), F32),
            struct((seq, width), BF16),
            struct((8, width), F32),
        ],
        [pltpu.VMEM((seq, width), F32)],
        flops=2 * seq * width * rows * group,
        moved=2 * width * rows * group + 14 * seq * width,
    )(where, act, w_down, rest_down, hidden, cotangent, *vectors)


def inner_back_kernel(
    group,
    where,
    low,
    own_down,
    rest_down,
    slope,
    own_in,
    rest_in,
    grad_two,
    hidden,
    gain,
    own_out,
    rest_out,
    grad_inner,
    bias_sums,
    grad_one,
    low_one,
    grad_context,
    sums,
    total,
):
    step = pl.program_id(0)
    rows = own_in.shape[0]

    def place(s):
        return pl.ds(pl.multiple_of(natural(where, s, group) * rows, 128), rows)

    def finish(back):
        value = (back * slope[...].astype(F32)).astype(BF16)
        grad_inner[...] = value
        bias_sums[...] = rows_sum(value.astype(F32))

    @pl.when(step == 0)
    def _():
        finish(dot_t(low[...], own_down[...]))
        total[...] = grad_two[...]

    @pl.when(step > 0)
    def _():
        finish(dot_t(low[...], rest_down[...]))

    value = grad_inner[...]
    total[:, place(0)] += dot_t(value, own_in[...])
    for s in range(1, group):
        total[:, place(s)] += dot_t(value, rest_in[(s - 1) * rows : s * rows, :])

    @pl.when(step == group - 1)
    def _():
        unit, inverse = normalise(hidden[...])
        given = total[...]
        back = normalise_back(given, unit, inverse, gain[...])
        grad_one[...] = back
        rounded = back.astype(BF16)
        low_one[...] = rounded
        sums[0:1, :] = rows_sum(given * unit)
        sums[1:2, :] = rows_sum(given)
        sums[2:3, :] = rows_sum(rounded.astype(F32))
        grad_context[:, place(0)] = dot_t(rounded, own_out[...]).astype(BF16)
        for s in range(1, group):
            weight = rest_out[(s - 1) * rows : s * rows, :]
            grad_context[:, place(s)] = dot_t(rounded, weight).astype(BF16)


def inner_back(
    where, low, w_down, rest_down, slope, w_in, rest_in, grad_two, hidden, gain, w_out, rest_one, group
):
    seq, width = hidden.shape
    ff_rows = w_down.shape[0]
    rows, columns = w_in.shape
    last = rest_one.shape[1] // width - 1
    full = fixed((seq, width))

    def block(rows_of):
        return spec((rows_of, ff_rows), lambda s, w: (0, natural(w, s, group)))

    return call(
        partial(inner_back_kernel, group),
        (group,),
        [
            full,
            fixed((ff_rows, width)),
            spec((ff_rows, width), lambda s, w: (jnp.maximum(s - 1, 0), 0)),
            block(seq),
            block(rows),
            block(width - rows),
            full,
            full,
            fixed((1, width)),
            fixed((rows, width)),
            spec((width - rows, width), lambda s, w: (0, last)),
        ],
        [block(seq), block(1), full, full, full, fixed((8, width))],
        [
            struct((seq, columns), BF16),
            struct((1, columns), F32),
            struct((seq, width), F32),
            struct((seq, width), BF16),
            struct((seq, width), BF16),
            struct((8, width), F32),
        ],
        [pltpu.VMEM((seq, width), F32)],
        flops=4 * seq * width * columns + 2 * seq * width * width,
        moved=4 * width * columns + 4 * seq * columns + 18 * seq * width,
    )(where, low, w_down, rest_down, slope, w_in, rest_in, grad_two, hidden, gain, w_out, rest_one)


def input_back_kernel(where, grad, first, own, rest, out):
    def result(weight):
        width = grad.shape[2]
        total = first[...]
        for m in range(3):
            total = total + dot_t(grad[m], weight[:, m * width : (m + 1) * width])
        out[...] = total

    @pl.when(pl.program_id(0) == 0)
    def _():
        result(own)

    @pl.when(pl.program_id(0) > 0)
    def _():
        result(rest)


def input_back(where, grad, first, w_qkv, rest_one, group):
    _, seq, width = grad.shape
    rows, columns = w_qkv.shape
    block = spec((seq, rows), lambda s, w: (0, natural(w, s, group)))
    return call(
        input_back_kernel,
        (group,),
        [
            fixed((3, seq, width)),
            block,
            fixed((rows, columns)),
            spec((rows, columns), lambda s, w: (jnp.maximum(s - 1, 0), 0)),
        ],
        block,
        struct((seq, width), F32),
        flops=2 * seq * width * columns,
        moved=2 * (width * columns + seq * columns) + 8 * seq * width,
    )(where, grad, first, w_qkv, rest_one)


def down_grad_kernel(where, act, act_other, low, low_other, out):
    out[...] = (t_dot(act[...], low[...]) + t_dot(act_other[...], low_other[...])).astype(BF16)


def down_grad(where, act, act_other, low, low_other, rows, group):
    seq, columns = act.shape
    half = low.shape[1] // 2
    left = spec((seq, rows), lambda s, w: (0, natural(w, s, group)))
    right = spec((seq, half), lambda s, w: (0, w[1]))
    return call(
        down_grad_kernel,
        (group,),
        [left, left, right, right],
        spec((rows, half), lambda s, w: (s, 0)),
        struct((columns, half), BF16),
        flops=4 * seq * columns * half,
        moved=2 * (2 * seq * columns + columns * half),
    )(where, act, act_other, low, low_other)


def in_grad_kernel(group, where, x, x_other, grad, grad_other, out):
    width = x.shape[1]
    rows = width // group
    for s in range(group):
        place = pl.ds(pl.multiple_of(natural(where, s, group) * rows, 128), rows)
        value = t_dot(x[:, place], grad[...]) + t_dot(x_other[:, place], grad_other[...])
        out[0, s * rows : (s + 1) * rows, :] = value.astype(BF16)


def in_grad(where, x, x_other, grad, grad_other, chips, group):
    seq, width = x.shape
    part = grad.shape[1] // (2 * chips)
    full = fixed((seq, width))
    right = spec((seq, part), lambda p, w: (0, 2 * p + w[1]))
    return call(
        partial(in_grad_kernel, group),
        (chips,),
        [full, full, right, right],
        spec((1, width, part), lambda p, w: (p, 0, 0)),
        struct((chips, width, part), BF16),
        flops=4 * seq * width * part * chips,
        moved=2 * (4 * seq * width + width * part * chips),
    )(where, x, x_other, grad, grad_other)


def first_grad_kernel(group, split, where, x, x_other, c, c_other, g, g_other, a, a_other, out):
    width = x.shape[1]
    rows = width // group

    def result(left, left_other, right, right_other):
        for s in range(group):
            place = pl.ds(pl.multiple_of(natural(where, s, group) * rows, 128), rows)
            value = t_dot(left[:, place], right) + t_dot(left_other[:, place], right_other)
            out[0, s * rows : (s + 1) * rows, :] = value.astype(BF16)

    @pl.when(pl.program_id(0) < split)
    def _():
        result(x, x_other, g[0], g_other[0])

    @pl.when(pl.program_id(0) >= split)
    def _():
        result(c, c_other, a[...], a_other[...])


def first_grad(where, x, x_other, c, c_other, g, g_other, a, a_other, chips, group):
    seq, width = x.shape
    part = 4 * width // (2 * chips)
    each = width // part
    split = 3 * chips // 4
    full = fixed((seq, width))

    def proj_block(p, w):
        block = jnp.minimum(2 * p + w[1], 3 * each - 1)
        return (block // each, 0, lax.rem(block, each))

    def attn_block(p, w):
        return (0, jnp.maximum(2 * p + w[1] - 3 * each, 0))

    proj = spec((1, seq, part), proj_block)
    attn = spec((seq, part), attn_block)
    return call(
        partial(first_grad_kernel, group, split),
        (chips,),
        [full, full, full, full, proj, proj, attn, attn],
        spec((1, width, part), lambda p, w: (p, 0, 0)),
        struct((chips, width, part), BF16),
        flops=4 * seq * width * part * chips,
        moved=2 * (8 * seq * width + width * part * chips),
    )(where, x, x_other, c, c_other, g, g_other, a, a_other)


def local(
    chips,
    group,
    tokens,
    segments,
    lengths,
    cotangent,
    w_qkv,
    b_qv,
    w_out,
    b_out,
    gain_one,
    shift_one,
    w_in,
    b_in,
    w_down,
    b_down,
    gain_two,
    shift_two,
):
    reps = 2 * chips
    core = lax.axis_index("core")
    rank = lax.axis_index("chip") * 2 + core
    own = lax.axis_index("shard")
    _, seq_len, model_width = tokens.shape
    ff_rows = w_down.shape[0]
    ff_width = w_in.shape[1]
    qkv_width = w_qkv.shape[1]

    def from_shard(value, step):
        return lax.ppermute(value, "shard", [(i, (i - step) % group) for i in range(group)])

    def to_shard(value, step):
        return lax.ppermute(value, "shard", [(i, (i + step) % group) for i in range(group)])

    def sibling(value):
        return lax.ppermute(value, "core", [(0, 1), (1, 0)])

    vectors = (b_qv, b_out, gain_one, shift_one, b_in, b_down, gain_two, shift_two)
    sizes = [v.shape[0] for v in vectors]
    w_one = jnp.concatenate([w_qkv, w_out], axis=1)
    part = w_one.shape[1] // reps
    rows = w_one.shape[0]
    packed = jnp.concatenate(vectors)
    extra = -(-packed.shape[0] // (16 * part)) * 16
    packed = jnp.pad(packed, (0, extra * part - packed.shape[0])).reshape(extra, part)
    piece_one = jnp.concatenate(
        [lax.dynamic_slice_in_dim(w_one, rank * part, part, axis=1), packed], axis=0
    )
    part_in = ff_width // reps
    piece_in = lax.dynamic_slice_in_dim(w_in, rank * part_in, part_in, axis=1)
    part_down = ff_rows // reps
    piece_down = lax.dynamic_slice_in_dim(w_down, rank * part_down, part_down, axis=0)

    got_one = [from_shard(piece_one, s) for s in range(1, group)]
    got_in = [from_shard(piece_in, s) for s in range(1, group)]
    got_down = [from_shard(piece_down, s) for s in range(1, group)]
    rest_one = lax.all_gather(
        jnp.concatenate([g[:rows] for g in got_one], axis=0), REP, axis=1, tiled=True
    )
    rest_in = lax.all_gather(jnp.concatenate(got_in, axis=0), REP, axis=1, tiled=True)
    rest_down = lax.all_gather(jnp.stack(got_down), REP, axis=1, tiled=True)
    rest_down = rest_down.reshape(-1, model_width)

    relative = jnp.stack([packed.reshape(-1)] + [g[rows:].reshape(-1) for g in got_one])
    ordered = jnp.concatenate([relative, relative], axis=0)
    ordered = lax.dynamic_slice_in_dim(ordered, (group - own) % group, group, axis=0)
    full, start = [], 0
    for size in sizes:
        full.append(ordered[:, start : start + size].reshape(1, -1).astype(F32))
        start += size
    bias_qv, bias_out, norm_gone, norm_sone, bias_in, bias_down, norm_gtwo, norm_stwo = full

    where = jnp.stack([own, core]).astype(jnp.int32)
    none = jnp.zeros((1, model_width), F32)
    bias_qkv = jnp.concatenate([bias_qv[:, :model_width], none, bias_qv[:, model_width:]], axis=1)
    kind = segments[0] * 2 + (jnp.arange(seq_len) < lengths[0]).astype(jnp.int32)
    column, row = kind[:, None], kind[None, :]

    flat_in = tokens[0]
    projected = qkv(where, flat_in, w_qkv, rest_one, bias_qkv, group)
    context, log_totals = attention(where, projected, column, row, model_width)
    hidden, normed = out_norm(
        where, context, flat_in, w_out, rest_one, bias_out, norm_gone, norm_sone, group
    )
    act, slope = inner(where, normed, w_in, rest_in, bias_in, group)
    in_other, context_other = sibling(flat_in), sibling(context)
    normed_other, act_other = sibling(normed), sibling(act)
    output_rows, grad_second, grad_branch, sums_two = outer(
        where,
        act,
        w_down,
        rest_down,
        hidden,
        cotangent[0],
        (norm_gone, norm_sone, bias_down, norm_gtwo, norm_stwo),
        group,
    )

    def own_sum(parts):
        total = parts[0].astype(F32)
        for s in range(1, group):
            total = total + to_shard(parts[s], s).astype(F32)
        return total.astype(BF16)

    def scatter_columns(grad):
        flat = grad.reshape(-1, grad.shape[2])
        share = lax.psum_scatter(flat, "chip", scatter_dimension=0, tiled=True)
        share = own_sum(share.reshape(group, rows, -1))
        return lax.all_gather(share, REP, axis=1, tiled=True).astype(F32)

    grad_down = down_grad(
        where, act, act_other, grad_branch, sibling(grad_branch), ff_rows, group
    )
    half = model_width // 2
    grad_down = lax.psum_scatter(
        grad_down.reshape(group, ff_rows, half), "chip", scatter_dimension=1, tiled=True
    )
    grad_down = lax.all_gather(own_sum(grad_down), REP, axis=0, tiled=False)
    grad_down = grad_down.reshape(chips, 2, ff_rows // chips, half).transpose(0, 2, 1, 3)
    grad_wdown = grad_down.reshape(ff_rows, model_width).astype(F32)

    grad_inner, sums_in, grad_first, grad_attn, grad_context, sums_one = inner_back(
        where,
        grad_branch,
        w_down,
        rest_down,
        slope,
        w_in,
        rest_in,
        grad_second,
        hidden,
        norm_gone,
        w_out,
        rest_one,
        group,
    )
    grad_win = scatter_columns(
        in_grad(where, normed, normed_other, grad_inner, sibling(grad_inner), chips, group)
    )
    grad_proj, sums_proj = attention_back(
        where, projected, grad_context, log_totals, column, row
    )
    grad_one = scatter_columns(
        first_grad(
            where,
            flat_in,
            in_other,
            context,
            context_other,
            grad_proj,
            sibling(grad_proj),
            grad_attn,
            sibling(grad_attn),
            chips,
            group,
        )
    )
    grad_input = input_back(where, grad_proj, grad_first, w_qkv, rest_one, group)

    small = (
        jnp.concatenate([sums_proj[0, 0], sums_proj[2, 0]]),
        sums_one[2],
        sums_one[0],
        sums_one[1],
        sums_in[0],
        sums_two[2],
        sums_two[0],
        sums_two[1],
    )
    small = jnp.concatenate([v.reshape(group, -1) for v in small], axis=1)
    small = lax.psum(small, ALL)
    small = lax.dynamic_index_in_dim(small, own, axis=0, keepdims=False)
    vecs, start = [], 0
    for size in sizes:
        vecs.append(small[start : start + size])
        start += size

    return (
        output_rows.reshape(tokens.shape),
        grad_input.reshape(tokens.shape),
        grad_one[:, :qkv_width],
        vecs[0],
        grad_one[:, qkv_width:],
        vecs[1],
        vecs[2],
        vecs[3],
        grad_win,
        vecs[4],
        grad_wdown,
        vecs[5],
        vecs[6],
        vecs[7],
    )


def solution(mesh):
    reps, group = mesh.devices.shape
    fine = Mesh(mesh.devices.reshape(reps // 2, 2, group), ALL)
    rows = P(ALL, None, None)
    matrix = P("shard", None)
    vector = P("shard")
    in_specs = (
        rows,
        P(ALL, None),
        P(ALL),
        rows,
        matrix,
        vector,
        matrix,
        vector,
        vector,
        vector,
        matrix,
        vector,
        matrix,
        vector,
        vector,
        vector,
    )
    out_specs = (
        rows,
        rows,
        matrix,
        vector,
        matrix,
        vector,
        vector,
        vector,
        matrix,
        vector,
        matrix,
        vector,
        vector,
        vector,
    )
    return jax.shard_map(
        partial(local, reps // 2, group),
        mesh=fine,
        in_specs=in_specs,
        out_specs=out_specs,
        check_vma=False,
    )
```

```python
from functools import partial

import jax
import jax.numpy as jnp
from jax import lax
from jax.experimental import pallas as pl
from jax.experimental.pallas import tpu as pltpu
from jax.sharding import Mesh
from jax.sharding import PartitionSpec as P

HEAD_DIM = 64
REP = ("chip", "core")
ALL = ("chip", "core", "shard")
F32 = jnp.float32
BF16 = jnp.bfloat16
MIB = 1024 * 1024
HINT = 3690000


def dot(left, right):
    return jnp.dot(left, right, preferred_element_type=F32)


def dot_t(left, right):
    return lax.dot_general(left, right, (((1,), (1,)), ((), ())), preferred_element_type=F32)


def t_dot(left, right):
    return lax.dot_general(left, right, (((0,), (0,)), ((), ())), preferred_element_type=F32)


def call(body, grid, ins, outs, out_shape, scratch=(), micros=1, limit=63, aliases=None):
    return pl.pallas_call(
        body,
        grid_spec=pltpu.PrefetchScalarGridSpec(
            num_scalar_prefetch=1,
            grid=grid,
            in_specs=ins,
            out_specs=outs,
            scratch_shapes=list(scratch),
        ),
        out_shape=out_shape,
        compiler_params=pltpu.CompilerParams(
            dimension_semantics=("arbitrary",) * len(grid), vmem_limit_bytes=limit * MIB
        ),
        input_output_aliases=aliases or {},
        cost_estimate=pl.CostEstimate(
            flops=0, bytes_accessed=int(micros * HINT), transcendentals=0
        ),
    )


def spec(shape, index):
    return pl.BlockSpec(shape, index)


def fixed(shape):
    zeros = (0,) * len(shape)
    return pl.BlockSpec(shape, lambda *_: zeros)


def struct(shape, dtype):
    return jax.ShapeDtypeStruct(shape, dtype)


def natural(where, step, group):
    return lax.rem(where[0] + step, group)


def block_of(where, unit, chips):
    return 2 * where[2 + unit] + jnp.where(unit < chips, where[1], 1 - where[1])


def part_specs(parts, first=0):
    half, steps, rows, columns = parts[0].shape

    def given(index):
        return spec(
            (1, steps, rows, columns),
            lambda u, w: (jnp.clip(u - first - index * half, 0, half - 1), 0, 0, 0),
        )

    return [given(index) for index in range(4)]


def load_weight(unit, half, own, parts, weight):
    rows = own.shape[0]
    weight[:rows, :] = own[...]
    for index, part in enumerate(parts):

        @pl.when(unit // half == index)
        def _(part=part):
            weight[rows:, :] = part[0].reshape(-1, part.shape[3])


def normalise(hidden):
    average = jnp.mean(hidden, axis=-1, keepdims=True)
    centred = hidden - average
    variance = jnp.mean(centred * centred, axis=-1, keepdims=True)
    inverse = lax.rsqrt(variance + 1e-06)
    return centred * inverse, inverse


def normalise_back(grad, unit, inverse, gain):
    scaled = grad * gain
    first = jnp.mean(scaled, axis=-1, keepdims=True)
    second = jnp.mean(scaled * unit, axis=-1, keepdims=True)
    return inverse * (scaled - first - unit * second)


def rows_sum(value):
    return jnp.sum(value, axis=0, keepdims=True)


def roll_into(rolled, x, where, rows, group):
    for s in range(group):
        start = pl.multiple_of(natural(where, s, group) * rows, 128)
        rolled[:, s * rows : (s + 1) * rows] = x[:, pl.ds(start, rows)]


def qkv_kernel(dims, where, x, own, a, b, c, d, bias, out, rest_out, rolled, weight):
    group, half, qkv_width = dims
    unit = pl.program_id(0)
    rows, columns = own.shape

    @pl.when(unit == 0)
    def _():
        roll_into(rolled, x, where, rows, group)

    load_weight(unit, half, own, (a, b, c, d), weight)
    start = block_of(where, unit, 2 * half) * columns

    @pl.when(start < qkv_width)
    def _():
        out[...] = (dot(rolled[...], weight[...]) + bias[...]).astype(BF16)

    @pl.when(start >= qkv_width)
    def _():
        place = pl.ds(pl.multiple_of(start - qkv_width, 128), columns)
        rest_out[:, place] = weight[rows:, :]


def qkv(where, x, w_qkv, parts, bias, group):
    seq, width = x.shape
    rows, qkv_width = w_qkv.shape
    half, _, _, block = parts[0].shape
    chips = 2 * half
    total = 2 * chips * block
    top = qkv_width // block - 1
    return call(
        partial(qkv_kernel, (group, half, qkv_width)),
        (2 * chips,),
        [
            fixed((seq, width)),
            spec((rows, block), lambda u, w: (0, jnp.minimum(block_of(w, u, chips), top))),
        ]
        + part_specs(parts)
        + [spec((1, block), lambda u, w: (0, block_of(w, u, chips)))],
        [
            spec((seq, block), lambda u, w: (0, block_of(w, u, chips))),
            fixed((width - rows, total - qkv_width)),
        ],
        [struct((seq, total), BF16), struct((width - rows, total - qkv_width), BF16)],
        [pltpu.VMEM((seq, width), BF16), pltpu.VMEM((width, block), BF16)],
        micros=12,
    )(where, x, w_qkv, *parts, bias)


def attend_kernel(first, where, q, k, v, x, column, row, *refs):
    out, turned, log_totals, bias = refs[-4:]
    step = pl.program_id(0)
    turned[0] = x[...].T

    @pl.when(step == 0)
    def _():
        bias[...] = jnp.where(column[...] == row[...], 0.0, -1e30)
        log_totals[...] = jnp.zeros_like(log_totals)

    lanes = lax.broadcasted_iota(jnp.int32, (1, 128), 1)
    heads = q.shape[1] // HEAD_DIM
    for h in range(heads):
        part = slice(h * HEAD_DIM, (h + 1) * HEAD_DIM)
        scores = dot_t(q[:, part] * BF16(HEAD_DIM**-0.5), k[:, part]) + bias[...]
        maxima = jnp.max(scores, axis=1, keepdims=True)
        expo = jnp.exp(scores - maxima)
        totals = jnp.sum(expo, axis=1, keepdims=True)
        probs = (expo * (1.0 / totals)).astype(BF16)
        out[:, part] = dot(probs, v[:, part]).astype(BF16)
        log_totals[...] = jnp.where(
            lanes == (first + step) * heads + h, maxima + jnp.log(totals), log_totals[...]
        )
    turned[1] = out[...].T


def attention(where, projected, x, column, row, first, count, before=()):
    seq, width = x.shape
    block = 2 * HEAD_DIM
    each = width // block
    anywhere = pl.BlockSpec(memory_space=pl.ANY)
    return call(
        partial(attend_kernel, first),
        (count,),
        [
            spec((seq, block), lambda h, w: (0, first + h)),
            spec((seq, block), lambda h, w: (0, each + first + h)),
            spec((seq, block), lambda h, w: (0, 2 * each + first + h)),
            spec((seq, block), lambda h, w: (0, first + h)),
            fixed((seq, 1)),
            fixed((1, seq)),
        ]
        + [anywhere] * len(before),
        [
            spec((seq, block), lambda h, w: (0, first + h)),
            spec((2, block, seq), lambda h, w: (0, first + h, 0)),
            fixed((seq, 128)),
        ],
        [
            struct((seq, width), BF16),
            struct((2, width, seq), BF16),
            struct((seq, 128), F32),
        ],
        [pltpu.VMEM((seq, seq), F32)],
        micros=11,
        aliases={7: 0, 8: 1} if before else None,
    )(where, projected, projected, projected, x, column, row, *before)


def attend_back_kernel(dims, where, q, k, v, grad, logs_a, logs_b, attn, column, row, *refs):
    out, sums, bias = refs
    mine, per = dims
    step = pl.program_id(0)
    pair = pair_of(where, step, mine, per)
    out[3] = attn[...]

    @pl.when(step == 0)
    def _():
        bias[...] = jnp.where(column[...] == row[...], 0.0, -1e30)

    lanes = lax.broadcasted_iota(jnp.int32, (1, 128), 1)
    heads = q.shape[1] // HEAD_DIM
    for h in range(heads):
        part = slice(h * HEAD_DIM, (h + 1) * HEAD_DIM)
        picked = jnp.where(lanes == pair * heads + h, logs_a[...] + logs_b[...], 0.0)
        logs = jnp.sum(picked, axis=1, keepdims=True)
        query = q[:, part] * BF16(HEAD_DIM**-0.5)
        scores = dot_t(query, k[:, part]) + bias[...]
        probs = jnp.exp(scores - logs)
        grad_probs = dot_t(grad[:, part], v[:, part])
        weighted = probs * grad_probs
        low = (weighted - probs * jnp.sum(weighted, axis=1, keepdims=True)).astype(BF16)
        grad_q = (dot(low, k[:, part]) * (HEAD_DIM**-0.5)).astype(BF16)
        grad_k = t_dot(low, query).astype(BF16)
        grad_v = t_dot(probs.astype(BF16), grad[:, part]).astype(BF16)
        for m, value in enumerate((grad_q, grad_k, grad_v)):
            out[m, :, part] = value
            sums[m, :, part] = rows_sum(value.astype(F32))


def pair_of(where, step, mine, per):
    parity = where[1] if mine else 1 - where[1]
    return (2 * (step // per) + parity) * per + lax.rem(step, per)


def attention_back(where, projected, grad, logs, attn, column, row, mine, part):
    seq, width = grad.shape
    block = 2 * HEAD_DIM
    each = width // block
    per = part // block

    def pairs(first):
        return spec((seq, block), lambda h, w: (0, first + pair_of(w, h, mine, per)))

    return call(
        partial(attend_back_kernel, (mine, per)),
        (each // 2,),
        [
            pairs(0),
            pairs(each),
            pairs(2 * each),
            pairs(0),
            fixed((seq, 128)),
            fixed((seq, 128)),
            pairs(0),
            fixed((seq, 1)),
            fixed((1, seq)),
        ],
        [
            spec((4, seq, block), lambda h, w: (0, 0, h)),
            spec((3, 1, block), lambda h, w: (0, 0, h)),
        ],
        [struct((4, seq, width // 2), BF16), struct((3, 1, width // 2), F32)],
        [pltpu.VMEM((seq, seq), F32)],
        micros=13,
    )(where, projected, projected, projected, grad, *logs, attn, column, row)


def out_kernel(group, where, context, x, own, rest, bias, gain, shift, hidden, low, turned):
    rows = own.shape[0]
    total = bias[...] + x[...].astype(F32)
    for s in range(group):
        start = pl.multiple_of(natural(where, s, group) * rows, 128)
        weight = own[...] if s == 0 else rest[(s - 1) * rows : s * rows, :]
        total = total + dot(context[:, pl.ds(start, rows)], weight)
    hidden[...] = total
    unit, _ = normalise(total)
    value = (unit * gain[...] + shift[...]).astype(BF16)
    low[...] = value
    turned[...] = value.T


def out_norm(where, context, x, w_out, rest_out, bias, gain, shift, group):
    seq, width = x.shape
    rows = w_out.shape[0]
    block = seq // 2
    vector = fixed((1, width))
    return call(
        partial(out_kernel, group),
        (seq // block,),
        [
            spec((block, width), lambda i, w: (i, 0)),
            spec((block, width), lambda i, w: (i, 0)),
            fixed((rows, width)),
            fixed((width - rows, width)),
            vector,
            vector,
            vector,
        ],
        [spec((block, width), lambda i, w: (i, 0))] * 2
        + [spec((width, block), lambda i, w: (0, i))],
        [
            struct((seq, width), F32),
            struct((seq, width), BF16),
            struct((width, seq), BF16),
        ],
        micros=6,
    )(where, context, x, w_out, rest_out, bias, gain, shift)


def inner_kernel(dims, where, x, own, a, b, c, d, bias, act, turned, slope, rolled, weight):
    group, half = dims
    unit = pl.program_id(0)

    @pl.when(unit == 0)
    def _():
        roll_into(rolled, x, where, own.shape[0], group)

    load_weight(unit, half, own, (a, b, c, d), weight)
    total = dot(rolled[...], weight[...]) + bias[...]
    below = 0.5 + 0.5 * lax.erf(total * (0.5**0.5))
    value = (total * below).astype(BF16)
    act[...] = value
    turned[...] = value.T
    density = jnp.exp(-0.5 * total * total) * ((2.0 * jnp.pi) ** -0.5)
    slope[...] = (below + total * density).astype(BF16)


def inner(where, x, w_in, parts, bias, group):
    seq, width = x.shape
    rows, columns = w_in.shape
    half, _, _, block = parts[0].shape
    chips = 2 * half

    def columns_at(height):
        return spec((height, block), lambda u, w: (0, block_of(w, u, chips)))

    return call(
        partial(inner_kernel, (group, half)),
        (2 * chips,),
        [fixed((seq, width)), columns_at(rows)] + part_specs(parts) + [columns_at(1)],
        [
            columns_at(seq),
            spec((block, seq), lambda u, w: (block_of(w, u, chips), 0)),
            columns_at(seq),
        ],
        [
            struct((seq, columns), BF16),
            struct((columns, seq), BF16),
            struct((seq, columns), BF16),
        ],
        [pltpu.VMEM((seq, width), BF16), pltpu.VMEM((width, block), BF16)],
        micros=16,
    )(where, x, w_in, *parts, bias)


def outer_kernel(
    dims,
    where,
    act,
    own,
    a,
    b,
    c,
    d,
    hidden,
    cotangent,
    gain_one,
    shift_one,
    bias,
    gain_two,
    shift_two,
    out,
    grad,
    low,
    low_other,
    sums,
    total,
    picked,
):
    group, half = dims
    step = pl.program_id(0)
    ff_rows = own.shape[0]
    rows = a.shape[2]

    @pl.when(step == 0)
    def _():
        start = pl.multiple_of(where[0] * ff_rows, 128)
        total[...] = dot(act[:, pl.ds(start, ff_rows)], own[...])

    for index, part in enumerate((a, b, c, d)):

        @pl.when(step == index + 1)
        def _(index=index, part=part):
            at = 0
            for i in range(half):
                block = block_of(where, index * half + i, 2 * half)
                for s in range(1, group):
                    start = natural(where, s, group) * ff_rows + block * rows
                    picked[:, at : at + rows] = act[:, pl.ds(pl.multiple_of(start, rows), rows)]
                    at += rows
            total[...] += dot(picked[...], part[...].reshape(-1, part.shape[3]))

    @pl.when(step == 4)
    def _():
        unit_one, _ = normalise(hidden[...])
        second = unit_one * gain_one[...] + shift_one[...] + total[...] + bias[...]
        unit, inverse = normalise(second)
        out[...] = (unit * gain_two[...] + shift_two[...]).astype(BF16)
        given = cotangent[...].astype(F32)
        back = normalise_back(given, unit, inverse, gain_two[...])
        grad[...] = back
        rounded = back.astype(BF16)
        low[...] = rounded
        size = low_other.shape[1]
        start = pl.multiple_of((1 - where[1]) * size, 128)
        low_other[...] = low[:, pl.ds(start, size)]
        sums[0:1, :] = rows_sum(given * unit)
        sums[1:2, :] = rows_sum(given)
        sums[2:3, :] = rows_sum(rounded.astype(F32))


def outer(where, act, w_down, parts, hidden, cotangent, vectors, group):
    seq, width = hidden.shape
    rows = w_down.shape[0]
    half, steps, size, _ = parts[0].shape
    full = fixed((seq, width))
    vector = fixed((1, width))
    return call(
        partial(outer_kernel, (group, half)),
        (5,),
        [fixed(act.shape), fixed((rows, width))]
        + [fixed(parts[0].shape)] * 4
        + [full, full]
        + [vector] * 5,
        [full, full, full, fixed((seq, width // 2)), fixed((8, width))],
        [
            struct((seq, width), BF16),
            struct((seq, width), F32),
            struct((seq, width), BF16),
            struct((seq, width // 2), BF16),
            struct((8, width), F32),
        ],
        [pltpu.VMEM((seq, width), F32), pltpu.VMEM((seq, half * steps * size), BF16)],
        micros=60,
    )(where, act, w_down, *parts, hidden, cotangent, *vectors)


def slope_kernel(dims, where, low, own, a, b, c, d, slope, grad, grad_other, sums):
    group, half, width = dims
    step = pl.program_id(0)
    ff_rows = own.shape[0]
    rows = a.shape[2]

    def finish(back, start, size):
        place = pl.ds(pl.multiple_of(start, size), size)
        value = (back * slope[:, place].astype(F32)).astype(BF16)
        grad[:, place] = value
        sums[:, place] = rows_sum(value.astype(F32))
        piece = min(size, width)
        for at in range(0, size, piece):
            block = (start + at) // width
            inside = start + at - block * width

            @pl.when(lax.rem(block, 2) != where[1])
            def _(at=at, block=block, inside=inside):
                there = pl.multiple_of((block // 2) * width + inside, piece)
                grad_other[:, pl.ds(there, piece)] = value[:, at : at + piece]

    @pl.when(step == 0)
    def _():
        finish(dot_t(low[...], own[...]), where[0] * ff_rows, ff_rows)

    for index, part in enumerate((a, b, c, d)):

        @pl.when(step == index + 1)
        def _(index=index, part=part):
            back = dot_t(low[...], part[...].reshape(-1, part.shape[3]))
            at = 0
            for i in range(half):
                block = block_of(where, index * half + i, 2 * half)
                for s in range(1, group):
                    start = natural(where, s, group) * ff_rows + block * rows
                    finish(back[:, at : at + rows], start, rows)
                    at += rows


def slope_back(where, low, w_down, parts, slope, part, group):
    seq, width = low.shape
    rows = w_down.shape[0]
    half = parts[0].shape[0]
    columns = slope.shape[1]
    return call(
        partial(slope_kernel, (group, half, part)),
        (5,),
        [fixed((seq, width)), fixed((rows, width))]
        + [fixed(parts[0].shape)] * 4
        + [fixed((seq, columns))],
        [fixed((seq, columns)), fixed((seq, columns // 2)), fixed((1, columns))],
        [
            struct((seq, columns), BF16),
            struct((seq, columns // 2), BF16),
            struct((1, columns), F32),
        ],
        micros=14,
    )(where, low, w_down, *parts, slope)


def inner_back_kernel(
    dims,
    where,
    grad_inner,
    own,
    a,
    b,
    c,
    d,
    grad_two,
    hidden,
    gain,
    own_out,
    rest_out,
    grad_one,
    low_one,
    grad_context,
    sums,
    total,
    weight,
):
    group, half = dims
    unit = pl.program_id(0)
    rows = own.shape[0]

    def place(s):
        return pl.ds(pl.multiple_of(natural(where, s, group) * rows, 128), rows)

    load_weight(unit, half, own, (a, b, c, d), weight)
    value = dot_t(grad_inner[...], weight[...])

    @pl.when(unit == 0)
    def _():
        total[...] = value

    @pl.when(unit > 0)
    def _():
        total[...] += value

    @pl.when(unit == 4 * half - 1)
    def _():
        unit_one, inverse = normalise(hidden[...])
        for s in range(group):
            grad_one[:, place(s)] = total[:, s * rows : (s + 1) * rows]
        given = grad_one[...] + grad_two[...]
        back = normalise_back(given, unit_one, inverse, gain[...])
        grad_one[...] = back
        rounded = back.astype(BF16)
        low_one[...] = rounded
        sums[0:1, :] = rows_sum(given * unit_one)
        sums[1:2, :] = rows_sum(given)
        sums[2:3, :] = rows_sum(rounded.astype(F32))
        grad_context[:, place(0)] = dot_t(rounded, own_out[...]).astype(BF16)
        for s in range(1, group):
            piece = rest_out[(s - 1) * rows : s * rows, :]
            grad_context[:, place(s)] = dot_t(rounded, piece).astype(BF16)


def inner_back(where, grad_inner, w_in, parts, grad_two, hidden, gain, w_out, rest_out, group):
    seq, width = hidden.shape
    rows, columns = w_in.shape
    half, _, _, block = parts[0].shape
    chips = 2 * half
    full = fixed((seq, width))

    def columns_at(height):
        return spec((height, block), lambda u, w: (0, block_of(w, u, chips)))

    return call(
        partial(inner_back_kernel, (group, half)),
        (2 * chips,),
        [columns_at(seq), columns_at(rows)]
        + part_specs(parts)
        + [full, full, fixed((1, width)), fixed((rows, width)), fixed((width - rows, width))],
        [full, full, full, fixed((8, width))],
        [
            struct((seq, width), F32),
            struct((seq, width), BF16),
            struct((seq, width), BF16),
            struct((8, width), F32),
        ],
        [pltpu.VMEM((seq, width), F32), pltpu.VMEM((width, block), BF16)],
        micros=19,
    )(where, grad_inner, w_in, *parts, grad_two, hidden, gain, w_out, rest_out)


def input_back_kernel(dims, where, mine, others, own, a, b, c, d, first, out, total, weight):
    group, half, qkv_width = dims
    unit = pl.program_id(0)
    rows, columns = own.shape

    @pl.when(unit == 0)
    def _():
        total[...] = jnp.zeros_like(total)

    block = block_of(where, unit, 2 * half)
    inside = block * columns < qkv_width
    same = lax.rem(block, 2) == where[1]

    @pl.when(inside)
    def _():
        load_weight(unit, half, own, (a, b, c, d), weight)

    @pl.when(inside & same)
    def _():
        total[...] += dot_t(mine[0], weight[...])

    @pl.when(inside & ~same)
    def _():
        total[...] += dot_t(others[0], weight[...])

    @pl.when(unit == 4 * half - 1)
    def _():
        for s in range(group):
            place = pl.ds(pl.multiple_of(natural(where, s, group) * rows, 128), rows)
            out[:, place] = first[:, place] + total[:, s * rows : (s + 1) * rows]


def input_back(where, mine, others, first, w_qkv, parts, group):
    seq, width = first.shape
    rows, qkv_width = w_qkv.shape
    half, _, _, block = parts[0].shape
    chips = 2 * half
    each = width // block
    top = qkv_width // block - 1

    def plane(u, w):
        n = jnp.minimum(block_of(w, u, chips), top)
        return (n // each, 0, lax.rem(n, each) // 2)

    return call(
        partial(input_back_kernel, (group, half, qkv_width)),
        (2 * chips,),
        [
            spec((1, seq, block), plane),
            spec((1, seq, block), plane),
            spec((rows, block), lambda u, w: (0, jnp.minimum(block_of(w, u, chips), top))),
        ]
        + part_specs(parts)
        + [fixed((seq, width))],
        fixed((seq, width)),
        struct((seq, width), F32),
        [pltpu.VMEM((seq, width), F32), pltpu.VMEM((width, block), BF16)],
        micros=12,
    )(where, mine, others, w_qkv, *parts, first)


def widen_kernel(dims, where, *refs):
    parts, outs = refs[:4], refs[4:]
    phases, by_rows = dims
    chips = 1 << phases
    half = chips // 2
    for side in range(2):
        core = where[1] if side == 0 else 1 - where[1]
        for order in range(chips):
            value = parts[2 * side + order // half][order % half].astype(F32)
            rows, columns = value.shape
            chip = where[2 + side * chips + order]
            if by_rows:
                outs[0][
                    pl.ds(pl.multiple_of(chip * rows, 8), rows),
                    pl.ds(pl.multiple_of(core * columns, 128), columns),
                ] = value
                continue
            start = (2 * chip + core) * columns
            base = 0
            for out in outs:
                size = out.shape[1]
                inside = (start >= base) & (start < base + size)

                @pl.when(inside)
                def _(out=out, start=start, base=base, value=value):
                    out[:, pl.ds(pl.multiple_of(start - base, 128), columns)] = value

                base += size


def widen(where, parts, phases, by_rows, shapes):
    return call(
        partial(widen_kernel, (phases, by_rows)),
        (1,),
        [fixed(part.shape) for part in parts],
        [fixed(shape) for shape in shapes],
        [struct(shape, F32) for shape in shapes],
        micros=4,
    )(where, *parts)


def grads_kernel(dims, where, *refs):
    orders, adds, last, group = dims
    units = len(orders)
    step = pl.program_id(0)
    at = 0
    outs = refs[units * (4 + adds) :]
    for u in range(units):
        left, left_other, right, right_other = refs[at : at + 4]
        value = dot(left[0], right[0]) + dot(left_other[0], right_other[0])
        for add in refs[at + 4 : at + 4 + adds]:
            value = value + add[0].astype(F32)
        at += 4 + adds
        value = value.astype(BF16)
        if not last:
            outs[0][u] = value
            continue
        for s in range(group):

            @pl.when(step == s)
            def _(s=s, value=value):
                outs[s][...] = value


def grads(where, left, right, maps, shape, units, received, group):
    rows, columns = shape
    seq = left[0].shape[2]
    left_map, right_map, other_map = maps
    last = units == [0]
    ins, args = [], []
    for order in units:
        lefts = spec((1, rows, seq), partial(left_map, order))
        rights = spec((1, seq, columns), partial(right_map, order))
        others = spec((1, seq, columns), partial(other_map, order))
        ins += [lefts, lefts, rights, others]
        args += [left[0], left[1], right[0], right[1]]
        for phase, value in enumerate(received):
            index = order >> (phase + 1)
            ins.append(spec((1, rows, columns), lambda s, w, index=index: (index, s, 0)))
            args.append(value)
    count = len(units)
    if last:
        outs = [fixed((rows, columns))] * group
        out_shape = [struct((rows, columns), BF16)] * group
    else:
        outs = [spec((count, rows, columns), lambda s, w: (0, s, 0))]
        out_shape = [struct((count, group * rows, columns), BF16)]
    return call(
        partial(grads_kernel, (units, len(received), last, group)),
        (group,),
        ins,
        outs,
        out_shape,
        micros=6,
    )(where, *args)


def after(value, *others):
    return lax.optimization_barrier((value, others))[0]


def local(
    chips,
    group,
    tokens,
    segments,
    lengths,
    cotangent,
    w_qkv,
    b_qv,
    w_out,
    b_out,
    gain_one,
    shift_one,
    w_in,
    b_in,
    w_down,
    b_down,
    gain_two,
    shift_two,
):
    reps = 2 * chips
    phases = chips.bit_length() - 1
    core = lax.axis_index("core")
    chip = lax.axis_index("chip")
    rank = chip * 2 + core
    own = lax.axis_index("shard")
    _, seq_len, model_width = tokens.shape
    ff_rows = w_down.shape[0]
    ff_width = w_in.shape[1]
    qkv_width = w_qkv.shape[1]

    def from_shard(value, step):
        return lax.ppermute(value, "shard", [(i, (i - step) % group) for i in range(group)])

    def to_shard(value, step):
        return lax.ppermute(value, "shard", [(i, (i + step) % group) for i in range(group)])

    def sibling(value):
        return lax.ppermute(value, "core", [(0, 1), (1, 0)])

    def bit(phase, which):
        return 1 << ((phase + which) % phases)

    def swap(value, phase):
        pairs = [
            (q * 2 + c, (q ^ bit(phase, c)) * 2 + c) for q in range(chips) for c in range(2)
        ]
        return lax.ppermute(value, REP, pairs)

    def table(which):
        orders = []
        for order in range(chips):
            mask = sum(bit(f, which) for f in range(phases) if order >> f & 1)
            orders.append(mask)
        return orders

    masks = jnp.where(core == 0, jnp.array(table(0)), jnp.array(table(1)))
    masks_other = jnp.where(core == 0, jnp.array(table(1)), jnp.array(table(0)))
    where = jnp.concatenate(
        [jnp.stack([own, core]), chip ^ masks, chip ^ masks_other]
    ).astype(jnp.int32)

    def gather(value, *gates):
        for phase in range(phases - 1):
            value = jnp.concatenate([value, swap(value, phase)], axis=0)
        rest = swap(value, phases - 1)
        return value, rest, sibling(after(value, gates)), sibling(rest)

    w_one = jnp.concatenate([w_qkv, w_out], axis=1)
    part = w_one.shape[1] // reps
    rows = w_one.shape[0]
    piece_one = lax.dynamic_slice_in_dim(w_one, rank * part, part, axis=1)
    part_in = ff_width // reps
    piece_in = lax.dynamic_slice_in_dim(w_in, rank * part_in, part_in, axis=1)
    part_down = ff_rows // reps
    piece_down = lax.dynamic_slice_in_dim(w_down, rank * part_down, part_down, axis=0)

    class Gather:

        def __init__(self, value):
            self.value = value
            self.first = swap(value, 0)

        def step(self, *gates):
            other = self.first
            for phase in range(phases - 1):
                self.value = after(jnp.concatenate([self.value, other], axis=0), gates)
                other = swap(self.value, phase + 1)
            self.rest = other
            self.side = sibling(self.value)

        def finish(self, *gates):
            self.parts = (self.value, self.rest, self.side, sibling(after(self.rest, gates)))

    got_one = [from_shard(piece_one, s) for s in range(1, group)]
    got_in = [from_shard(piece_in, s) for s in range(1, group)]

    vectors = (b_qv, b_out, gain_one, shift_one, b_in, b_down, gain_two, shift_two)
    sizes = [v.shape[0] for v in vectors]
    packed = jnp.concatenate(after(vectors, piece_one))
    got_packed = [from_shard(packed, s) for s in range(1, group)]

    parts_one = gather(jnp.stack(got_one)[None], got_packed)
    parts_in = Gather(jnp.stack(got_in)[None])
    parts_in.step()
    got_down = [from_shard(after(piece_down, got_in), s) for s in range(1, group)]

    relative = jnp.stack([packed] + got_packed)
    ordered = jnp.concatenate([relative, relative], axis=0)
    ordered = lax.dynamic_slice_in_dim(ordered, (group - own) % group, group, axis=0)
    full, start = [], 0
    for size in sizes:
        full.append(ordered[:, start : start + size].reshape(1, -1).astype(F32))
        start += size
    bias_qv, bias_out, norm_gone, norm_sone, bias_in, bias_down, norm_gtwo, norm_stwo = full
    none = jnp.zeros((1, model_width), F32)
    bias_qkv = jnp.concatenate(
        [bias_qv[:, :model_width], none, bias_qv[:, model_width:], none], axis=1
    )
    kind = segments[0] * 2 + (jnp.arange(seq_len) < lengths[0]).astype(jnp.int32)
    column, row = kind[:, None], kind[None, :]

    flat_in = tokens[0]
    projected, rest_out = qkv(where, after(flat_in, parts_in.rest), w_qkv, parts_one, bias_qkv, group)
    parts_in.finish()
    count = model_width // (4 * HEAD_DIM)
    context, turned, logs_a = attention(where, projected, flat_in, column, row, 0, count)
    parts_down = Gather(jnp.stack(got_down)[None])
    context, turned, logs_b = attention(
        where,
        projected,
        flat_in,
        column,
        row,
        count,
        count,
        (context, turned),
    )
    first_left = (turned, sibling(turned))
    parts_down.step(logs_b)
    hidden, normed, normed_turned = out_norm(
        where,
        after(context, parts_down.value),
        flat_in,
        w_out,
        rest_out,
        bias_out,
        norm_gone,
        norm_sone,
        group,
    )
    parts_in = parts_in.parts
    in_left = (normed_turned[None], sibling(normed_turned)[None])
    act, act_turned, slope = inner(where, normed, w_in, parts_in, bias_in, group)
    parts_down.finish(act)
    parts_down = parts_down.parts
    down_left = (act_turned[None], sibling(act_turned)[None])
    where_down = where
    if part_down % 128:
        merged = jnp.zeros((group - 1, ff_rows, model_width), BF16)
        for unit in range(reps):
            piece = parts_down[2 * unit // chips][unit % (chips // 2)]
            at = block_of(where, unit, chips) * part_down
            merged = lax.dynamic_update_slice_in_dim(merged, piece, at, axis=1)
        fourth = ff_rows // 4
        parts_down = [
            merged[:, b * fourth : (b + 1) * fourth][None] for b in (0, 2, 1, 3)
        ]
        where_down = jnp.stack([own, 0, 0, 1, 0, 1]).astype(jnp.int32)
    output_rows, grad_second, grad_branch, branch_other, sums_two = outer(
        where_down,
        act,
        w_down,
        parts_down,
        hidden,
        cotangent[0],
        (norm_gone, norm_sone, bias_down, norm_gtwo, norm_stwo),
        group,
    )

    class Scatter:

        def __init__(self, left, right, maps, shape):
            self.fixed = (where, left, right, maps, shape)
            self.received = []

        def send(self, *gates):
            phase = len(self.received)
            units = list(range(1 << phase, chips, 2 << phase))
            received = after(self.received, gates) if phase else []
            sent = grads(*self.fixed, units, received, group)[0]
            self.received.append(swap(sent, phase))
            return sent

        def send_rest(self, *gates):
            while len(self.received) < phases:
                sent = self.send(*gates)
            return sent

        def finish(self, *gates):
            received = after(self.received, gates)
            parts = grads(*self.fixed, [0], received, group)
            self.own = parts[0]
            self.given = [to_shard(parts[s], s) for s in range(1, group)]
            return parts[0]

        def total(self):
            total = self.own.astype(F32)
            for value in self.given:
                total = total + value.astype(F32)
            return total.astype(BF16)

    half = model_width // 2
    part_rows = ff_rows // chips
    down_maps = (
        lambda o, s, w: (0, natural(w, s, group) * chips + w[2 + o], 0),
        lambda o, s, w: (0, 0, w[1]),
        lambda o, s, w: (0, 0, 0),
    )
    down_right = (grad_branch[None], sibling(branch_other)[None])
    down = Scatter(down_left, down_right, down_maps, (part_rows, half))
    sent = down.send()
    grad_inner, inner_other, sums_in = slope_back(
        where_down, after(grad_branch, sent), w_down, parts_down, slope, part_in, group
    )
    grad_first, grad_attn, grad_context, sums_one = inner_back(
        where,
        after(grad_inner, in_left),
        w_in,
        parts_in,
        grad_second,
        hidden,
        norm_gone,
        w_out,
        rest_out,
        group,
    )
    in_other = sibling(inner_other)
    sent = down.send_rest(grad_first, first_left)
    logs = (logs_a, logs_b)
    others, sums_others = attention_back(
        where, projected, after(grad_context, sent), logs, grad_attn, column, row, False, part
    )
    in_maps = (
        lambda o, s, w: (0, natural(w, s, group), 0),
        lambda o, s, w: (0, 0, 2 * w[2 + o] + w[1]),
        lambda o, s, w: (0, 0, w[2 + o]),
    )
    in_right = after((grad_inner[None], in_other[None]), down.received, others)
    inward = Scatter(in_left, in_right, in_maps, (rows, part_in))
    sent = inward.send()
    done = down.finish(sent)
    other_proj = sibling(others)
    mine, sums_mine = attention_back(
        where, projected, after(grad_context, done), logs, grad_attn, column, row, True, part
    )
    each = model_width // part

    def plane(order, w):
        return 2 * w[2 + order] + w[1]

    def compact(o, s, w):
        return (plane(o, w) // each, 0, lax.rem(plane(o, w), each) // 2)

    first_maps = (
        lambda o, s, w: (plane(o, w) // (3 * each), natural(w, s, group), 0),
        compact,
        compact,
    )
    first = Scatter(first_left, (mine, other_proj), first_maps, (rows, part))
    sent = first.send()
    sent = inward.send_rest(sent)
    share_down = down.total()[None]
    grad_input = input_back(
        where, after(mine, sent), others, grad_first, w_qkv, parts_one, group
    )
    done = inward.finish(grad_input)
    sent = first.send_rest(done)
    share_in = inward.total()[None]
    def blocks(core_parity):
        value = jnp.where(core == core_parity, sums_mine, sums_others)
        return value.reshape(3, -1, 1, part)

    sums_proj = jnp.concatenate([blocks(0), blocks(1)], axis=2).reshape(3, model_width)
    small = (
        jnp.concatenate([sums_proj[0], sums_proj[2]]),
        sums_one[2],
        sums_one[0],
        sums_one[1],
        sums_in[0],
        sums_two[2],
        sums_two[0],
        sums_two[1],
    )
    small = jnp.concatenate([v.reshape(group, -1) for v in small], axis=1)
    done = first.finish(sent, share_in)
    shares = jnp.stack([share_down.reshape(share_in.shape), share_in], axis=1)
    shares = after(shares, done)
    gathered = Gather(shares)
    share_one = after(first.total()[None], gathered.first)
    gathered.step(share_one)
    gathered.finish()
    final_parts = gather(share_one)
    small = after(small, done)
    small = small + sibling(small)
    for phase in range(phases):
        small = small + swap(small, phase)
    small = jnp.concatenate([small, small], axis=0)
    small = lax.dynamic_slice_in_dim(small, own, group, axis=0)
    small = after(small, final_parts)
    total = small[0]
    for s in range(1, group):
        total = total + to_shard(small[s], s)
    down_parts = [
        value[:, 0].reshape(-1, *share_down.shape[1:]) for value in gathered.parts
    ]
    in_parts = [value[:, 1] for value in gathered.parts]
    (grad_wdown,) = widen(where, down_parts, phases, True, [(ff_rows, model_width)])
    (grad_win,) = widen(where, in_parts, phases, False, [(rows, ff_width)])
    grad_wqkv, grad_wout = widen(
        where,
        final_parts,
        phases,
        False,
        [(rows, qkv_width), (rows, model_width)],
    )

    vecs, start = [], 0
    for size in sizes:
        vecs.append(total[start : start + size])
        start += size

    return (
        output_rows.reshape(tokens.shape),
        grad_input.reshape(tokens.shape),
        grad_wqkv,
        vecs[0],
        grad_wout,
        vecs[1],
        vecs[2],
        vecs[3],
        grad_win,
        vecs[4],
        grad_wdown,
        vecs[5],
        vecs[6],
        vecs[7],
    )


def solution(mesh):
    reps, group = mesh.devices.shape
    fine = Mesh(mesh.devices.reshape(reps // 2, 2, group), ALL)
    rows = P(ALL, None, None)
    matrix = P("shard", None)
    vector = P("shard")
    in_specs = (
        rows,
        P(ALL, None),
        P(ALL),
        rows,
        matrix,
        vector,
        matrix,
        vector,
        vector,
        vector,
        matrix,
        vector,
        matrix,
        vector,
        vector,
        vector,
    )
    out_specs = (
        rows,
        rows,
        matrix,
        vector,
        matrix,
        vector,
        vector,
        vector,
        matrix,
        vector,
        matrix,
        vector,
        vector,
        vector,
    )
    return jax.shard_map(
        partial(local, reps // 2, group),
        mesh=fine,
        in_specs=in_specs,
        out_specs=out_specs,
        check_vma=False,
    )
```

```python
from functools import partial

import jax
import jax.numpy as jnp
from jax import lax
from jax.experimental import pallas as pl
from jax.experimental.pallas import tpu as pltpu
from jax.sharding import Mesh
from jax.sharding import PartitionSpec as P

HEAD_DIM = 64
REP = ("chip", "core")
ALL = ("chip", "core", "shard")
F32 = jnp.float32
BF16 = jnp.bfloat16
MIB = 1024 * 1024
HINT = 3690000


def dot(left, right):
    return jnp.dot(left, right, preferred_element_type=F32)


def dot_t(left, right):
    return lax.dot_general(left, right, (((1,), (1,)), ((), ())), preferred_element_type=F32)


def t_dot(left, right):
    return lax.dot_general(left, right, (((0,), (0,)), ((), ())), preferred_element_type=F32)


def call(body, grid, ins, outs, out_shape, scratch=(), micros=1, limit=63, aliases=None):
    return pl.pallas_call(
        body,
        grid_spec=pltpu.PrefetchScalarGridSpec(
            num_scalar_prefetch=1,
            grid=grid,
            in_specs=ins,
            out_specs=outs,
            scratch_shapes=list(scratch),
        ),
        out_shape=out_shape,
        compiler_params=pltpu.CompilerParams(
            dimension_semantics=("arbitrary",) * len(grid), vmem_limit_bytes=limit * MIB
        ),
        input_output_aliases=aliases or {},
        cost_estimate=pl.CostEstimate(
            flops=0, bytes_accessed=int(micros * HINT), transcendentals=0
        ),
    )


def spec(shape, index):
    return pl.BlockSpec(shape, index)


def fixed(shape):
    zeros = (0,) * len(shape)
    return pl.BlockSpec(shape, lambda *_: zeros)


def struct(shape, dtype):
    return jax.ShapeDtypeStruct(shape, dtype)


def natural(where, step, group):
    return lax.rem(where[0] + step, group)


def block_of(where, unit, chips):
    return 2 * where[2 + unit] + jnp.where(unit < chips, where[1], 1 - where[1])


def part_specs(parts, first=0):
    half, steps, rows, columns = parts[0].shape

    def given(index):
        return spec(
            (1, steps, rows, columns),
            lambda u, w: (jnp.clip(u - first - index * half, 0, half - 1), 0, 0, 0),
        )

    return [given(index) for index in range(4)]


def load_weight(unit, half, own, parts, weight):
    rows = own.shape[0]
    weight[:rows, :] = own[...]
    for index, part in enumerate(parts):

        @pl.when(unit // half == index)
        def _(part=part):
            weight[rows:, :] = part[0].reshape(-1, part.shape[3])


def normalise(hidden):
    average = jnp.mean(hidden, axis=-1, keepdims=True)
    centred = hidden - average
    variance = jnp.mean(centred * centred, axis=-1, keepdims=True)
    inverse = lax.rsqrt(variance + 1e-06)
    return centred * inverse, inverse


def normalise_back(grad, unit, inverse, gain):
    scaled = grad * gain
    first = jnp.mean(scaled, axis=-1, keepdims=True)
    second = jnp.mean(scaled * unit, axis=-1, keepdims=True)
    return inverse * (scaled - first - unit * second)


def rows_sum(value):
    return jnp.sum(value, axis=0, keepdims=True)


def roll_into(rolled, x, where, rows, group):
    for s in range(group):
        start = pl.multiple_of(natural(where, s, group) * rows, 128)
        rolled[:, s * rows : (s + 1) * rows] = x[:, pl.ds(start, rows)]


def qkv_kernel(dims, where, x, own, a, b, c, d, bias, out, rest_out, rolled, weight):
    group, half, qkv_width = dims
    unit = pl.program_id(0)
    rows, columns = own.shape

    @pl.when(unit == 0)
    def _():
        roll_into(rolled, x, where, rows, group)

    load_weight(unit, half, own, (a, b, c, d), weight)
    start = block_of(where, unit, 2 * half) * columns

    @pl.when(start < qkv_width)
    def _():
        out[...] = (dot(rolled[...], weight[...]) + bias[...]).astype(BF16)

    @pl.when(start >= qkv_width)
    def _():
        place = pl.ds(pl.multiple_of(start - qkv_width, 128), columns)
        rest_out[:, place] = weight[rows:, :]


def qkv(where, x, w_qkv, parts, bias, group):
    seq, width = x.shape
    rows, qkv_width = w_qkv.shape
    half, _, _, block = parts[0].shape
    chips = 2 * half
    total = 2 * chips * block
    top = qkv_width // block - 1
    return call(
        partial(qkv_kernel, (group, half, qkv_width)),
        (2 * chips,),
        [
            fixed((seq, width)),
            spec((rows, block), lambda u, w: (0, jnp.minimum(block_of(w, u, chips), top))),
        ]
        + part_specs(parts)
        + [spec((1, block), lambda u, w: (0, block_of(w, u, chips)))],
        [
            spec((seq, block), lambda u, w: (0, block_of(w, u, chips))),
            fixed((width - rows, total - qkv_width)),
        ],
        [struct((seq, total), BF16), struct((width - rows, total - qkv_width), BF16)],
        [pltpu.VMEM((seq, width), BF16), pltpu.VMEM((width, block), BF16)],
        micros=12,
    )(where, x, w_qkv, *parts, bias)


def attend_kernel(first, where, q, k, v, x, column, row, *refs):
    out, turned, log_totals, bias = refs[-4:]
    step = pl.program_id(0)
    turned[0] = x[...].T

    @pl.when(step == 0)
    def _():
        bias[...] = jnp.where(column[...] == row[...], 0.0, -1e30)
        log_totals[...] = jnp.zeros_like(log_totals)

    lanes = lax.broadcasted_iota(jnp.int32, (1, 128), 1)
    heads = q.shape[1] // HEAD_DIM
    for h in range(heads):
        part = slice(h * HEAD_DIM, (h + 1) * HEAD_DIM)
        scores = dot_t(q[:, part] * BF16(HEAD_DIM**-0.5), k[:, part]) + bias[...]
        maxima = jnp.max(scores, axis=1, keepdims=True)
        expo = jnp.exp(scores - maxima)
        totals = jnp.sum(expo, axis=1, keepdims=True)
        probs = (expo * (1.0 / totals)).astype(BF16)
        out[:, part] = dot(probs, v[:, part]).astype(BF16)
        log_totals[...] = jnp.where(
            lanes == (first + step) * heads + h, maxima + jnp.log(totals), log_totals[...]
        )
    turned[1] = out[...].T


def attention(where, projected, x, column, row, first, count, before=()):
    seq, width = x.shape
    block = 2 * HEAD_DIM
    each = width // block
    anywhere = pl.BlockSpec(memory_space=pl.ANY)
    return call(
        partial(attend_kernel, first),
        (count,),
        [
            spec((seq, block), lambda h, w: (0, first + h)),
            spec((seq, block), lambda h, w: (0, each + first + h)),
            spec((seq, block), lambda h, w: (0, 2 * each + first + h)),
            spec((seq, block), lambda h, w: (0, first + h)),
            fixed((seq, 1)),
            fixed((1, seq)),
        ]
        + [anywhere] * len(before),
        [
            spec((seq, block), lambda h, w: (0, first + h)),
            spec((2, block, seq), lambda h, w: (0, first + h, 0)),
            fixed((seq, 128)),
        ],
        [
            struct((seq, width), BF16),
            struct((2, width, seq), BF16),
            struct((seq, 128), F32),
        ],
        [pltpu.VMEM((seq, seq), F32)],
        micros=11,
        aliases={7: 0, 8: 1} if before else None,
    )(where, projected, projected, projected, x, column, row, *before)


def attend_back_kernel(dims, where, q, k, v, grad, logs_a, logs_b, attn, column, row, *refs):
    out, sums, bias = refs
    mine, per = dims
    step = pl.program_id(0)
    pair = pair_of(where, step, mine, per)
    out[3] = attn[...]

    @pl.when(step == 0)
    def _():
        bias[...] = jnp.where(column[...] == row[...], 0.0, -1e30)

    lanes = lax.broadcasted_iota(jnp.int32, (1, 128), 1)
    heads = q.shape[1] // HEAD_DIM
    for h in range(heads):
        part = slice(h * HEAD_DIM, (h + 1) * HEAD_DIM)
        picked = jnp.where(lanes == pair * heads + h, logs_a[...] + logs_b[...], 0.0)
        logs = jnp.sum(picked, axis=1, keepdims=True)
        query = q[:, part] * BF16(HEAD_DIM**-0.5)
        scores = dot_t(query, k[:, part]) + bias[...]
        probs = jnp.exp(scores - logs)
        grad_probs = dot_t(grad[:, part], v[:, part])
        weighted = probs * grad_probs
        low = (weighted - probs * jnp.sum(weighted, axis=1, keepdims=True)).astype(BF16)
        grad_q = (dot(low, k[:, part]) * (HEAD_DIM**-0.5)).astype(BF16)
        grad_k = t_dot(low, query).astype(BF16)
        grad_v = t_dot(probs.astype(BF16), grad[:, part]).astype(BF16)
        for m, value in enumerate((grad_q, grad_k, grad_v)):
            out[m, :, part] = value
            sums[m, :, part] = rows_sum(value.astype(F32))


def pair_of(where, step, mine, per):
    parity = where[1] if mine else 1 - where[1]
    return (2 * (step // per) + parity) * per + lax.rem(step, per)


def attention_back(where, projected, grad, logs, attn, column, row, mine, part):
    seq, width = grad.shape
    block = 2 * HEAD_DIM
    each = width // block
    per = part // block

    def pairs(first):
        return spec((seq, block), lambda h, w: (0, first + pair_of(w, h, mine, per)))

    return call(
        partial(attend_back_kernel, (mine, per)),
        (each // 2,),
        [
            pairs(0),
            pairs(each),
            pairs(2 * each),
            pairs(0),
            fixed((seq, 128)),
            fixed((seq, 128)),
            pairs(0),
            fixed((seq, 1)),
            fixed((1, seq)),
        ],
        [
            spec((4, seq, block), lambda h, w: (0, 0, h)),
            spec((3, 1, block), lambda h, w: (0, 0, h)),
        ],
        [struct((4, seq, width // 2), BF16), struct((3, 1, width // 2), F32)],
        [pltpu.VMEM((seq, seq), F32)],
        micros=13,
    )(where, projected, projected, projected, grad, *logs, attn, column, row)


def out_kernel(group, where, context, x, own, rest, bias, gain, shift, hidden, low, turned):
    rows = own.shape[0]
    total = bias[...] + x[...].astype(F32)
    for s in range(group):
        start = pl.multiple_of(natural(where, s, group) * rows, 128)
        weight = own[...] if s == 0 else rest[(s - 1) * rows : s * rows, :]
        total = total + dot(context[:, pl.ds(start, rows)], weight)
    hidden[...] = total
    unit, _ = normalise(total)
    value = (unit * gain[...] + shift[...]).astype(BF16)
    low[...] = value
    turned[...] = value.T


def out_norm(where, context, x, w_out, rest_out, bias, gain, shift, group):
    seq, width = x.shape
    rows = w_out.shape[0]
    block = seq // 2
    vector = fixed((1, width))
    return call(
        partial(out_kernel, group),
        (seq // block,),
        [
            spec((block, width), lambda i, w: (i, 0)),
            spec((block, width), lambda i, w: (i, 0)),
            fixed((rows, width)),
            fixed((width - rows, width)),
            vector,
            vector,
            vector,
        ],
        [spec((block, width), lambda i, w: (i, 0))] * 2
        + [spec((width, block), lambda i, w: (0, i))],
        [
            struct((seq, width), F32),
            struct((seq, width), BF16),
            struct((width, seq), BF16),
        ],
        micros=6,
    )(where, context, x, w_out, rest_out, bias, gain, shift)


def inner_kernel(dims, where, x, own, a, b, c, d, bias, act, early, late, slope, rolled, weight):
    group, half = dims
    unit = pl.program_id(0)

    @pl.when(unit == 0)
    def _():
        roll_into(rolled, x, where, own.shape[0], group)

    load_weight(unit, half, own, (a, b, c, d), weight)
    total = dot(rolled[...], weight[...]) + bias[...]
    below = 0.5 + 0.5 * lax.erf(total * (0.5**0.5))
    value = (total * below).astype(BF16)
    act[...] = value
    half_seq = early.shape[1]
    early[...] = value[:half_seq].T
    late[...] = value[half_seq:].T
    density = jnp.exp(-0.5 * total * total) * ((2.0 * jnp.pi) ** -0.5)
    slope[...] = (below + total * density).astype(BF16)


def inner(where, x, w_in, parts, bias, group):
    seq, width = x.shape
    rows, columns = w_in.shape
    half, _, _, block = parts[0].shape
    chips = 2 * half

    def columns_at(height):
        return spec((height, block), lambda u, w: (0, block_of(w, u, chips)))

    return call(
        partial(inner_kernel, (group, half)),
        (2 * chips,),
        [fixed((seq, width)), columns_at(rows)] + part_specs(parts) + [columns_at(1)],
        [
            columns_at(seq),
            spec((block, seq // 2), lambda u, w: (block_of(w, u, chips), 0)),
            spec((block, seq // 2), lambda u, w: (block_of(w, u, chips), 0)),
            columns_at(seq),
        ],
        [
            struct((seq, columns), BF16),
            struct((columns, seq // 2), BF16),
            struct((columns, seq // 2), BF16),
            struct((seq, columns), BF16),
        ],
        [pltpu.VMEM((seq, width), BF16), pltpu.VMEM((width, block), BF16)],
        micros=16,
    )(where, x, w_in, *parts, bias)


def outer_kernel(
    dims,
    where,
    act,
    own,
    a,
    b,
    c,
    d,
    hidden,
    cotangent,
    gain_one,
    shift_one,
    bias,
    gain_two,
    shift_two,
    out,
    grad,
    low,
    low_other,
    sums,
    total,
    picked,
):
    group, half = dims
    step = pl.program_id(0)
    ff_rows = own.shape[0]
    rows = a.shape[2]

    @pl.when(step == 0)
    def _():
        start = pl.multiple_of(where[0] * ff_rows, 128)
        total[...] = dot(act[:, pl.ds(start, ff_rows)], own[...])

    for index, part in enumerate((a, b, c, d)):

        @pl.when(step == index + 1)
        def _(index=index, part=part):
            at = 0
            for i in range(half):
                block = block_of(where, index * half + i, 2 * half)
                for s in range(1, group):
                    start = natural(where, s, group) * ff_rows + block * rows
                    picked[:, at : at + rows] = act[:, pl.ds(pl.multiple_of(start, rows), rows)]
                    at += rows
            total[...] += dot(picked[...], part[...].reshape(-1, part.shape[3]))

    @pl.when(step == 4)
    def _():
        unit_one, _ = normalise(hidden[...])
        second = unit_one * gain_one[...] + shift_one[...] + total[...] + bias[...]
        unit, inverse = normalise(second)
        out[...] = (unit * gain_two[...] + shift_two[...]).astype(BF16)
        given = cotangent[...].astype(F32)
        back = normalise_back(given, unit, inverse, gain_two[...])
        grad[...] = back
        rounded = back.astype(BF16)
        low[...] = rounded
        size = low_other.shape[1]
        start = pl.multiple_of((1 - where[1]) * size, 128)
        low_other[...] = low[:, pl.ds(start, size)]
        sums[0:1, :] = rows_sum(given * unit)
        sums[1:2, :] = rows_sum(given)
        sums[2:3, :] = rows_sum(rounded.astype(F32))


def outer(where, act, w_down, parts, hidden, cotangent, vectors, group):
    seq, width = hidden.shape
    rows = w_down.shape[0]
    half, steps, size, _ = parts[0].shape
    full = fixed((seq, width))
    vector = fixed((1, width))
    return call(
        partial(outer_kernel, (group, half)),
        (5,),
        [fixed(act.shape), fixed((rows, width))]
        + [fixed(parts[0].shape)] * 4
        + [full, full]
        + [vector] * 5,
        [full, full, full, fixed((seq, width // 2)), fixed((8, width))],
        [
            struct((seq, width), BF16),
            struct((seq, width), F32),
            struct((seq, width), BF16),
            struct((seq, width // 2), BF16),
            struct((8, width), F32),
        ],
        [pltpu.VMEM((seq, width), F32), pltpu.VMEM((seq, half * steps * size), BF16)],
        micros=60,
    )(where, act, w_down, *parts, hidden, cotangent, *vectors)


def slope_kernel(dims, where, low, own, a, b, c, d, slope, grad, grad_other, sums):
    group, half, width = dims
    step = pl.program_id(0)
    ff_rows = own.shape[0]
    rows = a.shape[2]

    def finish(back, start, size):
        place = pl.ds(pl.multiple_of(start, size), size)
        value = (back * slope[:, place].astype(F32)).astype(BF16)
        grad[:, place] = value
        sums[:, place] = rows_sum(value.astype(F32))
        piece = min(size, width)
        for at in range(0, size, piece):
            block = (start + at) // width
            inside = start + at - block * width

            @pl.when(lax.rem(block, 2) != where[1])
            def _(at=at, block=block, inside=inside):
                there = pl.multiple_of((block // 2) * width + inside, piece)
                grad_other[:, pl.ds(there, piece)] = value[:, at : at + piece]

    @pl.when(step == 0)
    def _():
        finish(dot_t(low[...], own[...]), where[0] * ff_rows, ff_rows)

    for index, part in enumerate((a, b, c, d)):

        @pl.when(step == index + 1)
        def _(index=index, part=part):
            back = dot_t(low[...], part[...].reshape(-1, part.shape[3]))
            at = 0
            for i in range(half):
                block = block_of(where, index * half + i, 2 * half)
                for s in range(1, group):
                    start = natural(where, s, group) * ff_rows + block * rows
                    finish(back[:, at : at + rows], start, rows)
                    at += rows


def slope_back(where, low, w_down, parts, slope, part, group):
    seq, width = low.shape
    rows = w_down.shape[0]
    half = parts[0].shape[0]
    columns = slope.shape[1]
    return call(
        partial(slope_kernel, (group, half, part)),
        (5,),
        [fixed((seq, width)), fixed((rows, width))]
        + [fixed(parts[0].shape)] * 4
        + [fixed((seq, columns))],
        [fixed((seq, columns)), fixed((seq, columns // 2)), fixed((1, columns))],
        [
            struct((seq, columns), BF16),
            struct((seq, columns // 2), BF16),
            struct((1, columns), F32),
        ],
        micros=14,
    )(where, low, w_down, *parts, slope)


def inner_back_kernel(
    dims,
    where,
    grad_inner,
    own,
    a,
    b,
    c,
    d,
    grad_two,
    hidden,
    gain,
    own_out,
    rest_out,
    grad_one,
    low_one,
    grad_context,
    sums,
    total,
    weight,
):
    group, half = dims
    unit = pl.program_id(0)
    rows = own.shape[0]

    def place(s):
        return pl.ds(pl.multiple_of(natural(where, s, group) * rows, 128), rows)

    load_weight(unit, half, own, (a, b, c, d), weight)
    value = dot_t(grad_inner[...], weight[...])

    @pl.when(unit == 0)
    def _():
        total[...] = value

    @pl.when(unit > 0)
    def _():
        total[...] += value

    @pl.when(unit == 4 * half - 1)
    def _():
        unit_one, inverse = normalise(hidden[...])
        for s in range(group):
            grad_one[:, place(s)] = total[:, s * rows : (s + 1) * rows]
        given = grad_one[...] + grad_two[...]
        back = normalise_back(given, unit_one, inverse, gain[...])
        grad_one[...] = back
        rounded = back.astype(BF16)
        low_one[...] = rounded
        sums[0:1, :] = rows_sum(given * unit_one)
        sums[1:2, :] = rows_sum(given)
        sums[2:3, :] = rows_sum(rounded.astype(F32))
        grad_context[:, place(0)] = dot_t(rounded, own_out[...]).astype(BF16)
        for s in range(1, group):
            piece = rest_out[(s - 1) * rows : s * rows, :]
            grad_context[:, place(s)] = dot_t(rounded, piece).astype(BF16)


def inner_back(where, grad_inner, w_in, parts, grad_two, hidden, gain, w_out, rest_out, group):
    seq, width = hidden.shape
    rows, columns = w_in.shape
    half, _, _, block = parts[0].shape
    chips = 2 * half
    full = fixed((seq, width))

    def columns_at(height):
        return spec((height, block), lambda u, w: (0, block_of(w, u, chips)))

    return call(
        partial(inner_back_kernel, (group, half)),
        (2 * chips,),
        [columns_at(seq), columns_at(rows)]
        + part_specs(parts)
        + [full, full, fixed((1, width)), fixed((rows, width)), fixed((width - rows, width))],
        [full, full, full, fixed((8, width))],
        [
            struct((seq, width), F32),
            struct((seq, width), BF16),
            struct((seq, width), BF16),
            struct((8, width), F32),
        ],
        [pltpu.VMEM((seq, width), F32), pltpu.VMEM((width, block), BF16)],
        micros=19,
    )(where, grad_inner, w_in, *parts, grad_two, hidden, gain, w_out, rest_out)


def input_back_kernel(dims, where, mine, others, own, a, b, c, d, first, out, total, weight):
    group, half, qkv_width = dims
    unit = pl.program_id(0)
    rows, columns = own.shape

    @pl.when(unit == 0)
    def _():
        total[...] = jnp.zeros_like(total)

    block = block_of(where, unit, 2 * half)
    inside = block * columns < qkv_width
    same = lax.rem(block, 2) == where[1]

    @pl.when(inside)
    def _():
        load_weight(unit, half, own, (a, b, c, d), weight)

    @pl.when(inside & same)
    def _():
        total[...] += dot_t(mine[0], weight[...])

    @pl.when(inside & ~same)
    def _():
        total[...] += dot_t(others[0], weight[...])

    @pl.when(unit == 4 * half - 1)
    def _():
        for s in range(group):
            place = pl.ds(pl.multiple_of(natural(where, s, group) * rows, 128), rows)
            out[:, place] = first[:, place] + total[:, s * rows : (s + 1) * rows]


def input_back(where, mine, others, first, w_qkv, parts, group):
    seq, width = first.shape
    rows, qkv_width = w_qkv.shape
    half, _, _, block = parts[0].shape
    chips = 2 * half
    each = width // block
    top = qkv_width // block - 1

    def plane(u, w):
        n = jnp.minimum(block_of(w, u, chips), top)
        return (n // each, 0, lax.rem(n, each) // 2)

    return call(
        partial(input_back_kernel, (group, half, qkv_width)),
        (2 * chips,),
        [
            spec((1, seq, block), plane),
            spec((1, seq, block), plane),
            spec((rows, block), lambda u, w: (0, jnp.minimum(block_of(w, u, chips), top))),
        ]
        + part_specs(parts)
        + [fixed((seq, width))],
        fixed((seq, width)),
        struct((seq, width), F32),
        [pltpu.VMEM((seq, width), F32), pltpu.VMEM((width, block), BF16)],
        micros=12,
    )(where, mine, others, w_qkv, *parts, first)


def widen_rows_kernel(phases, where, a, b, c, d, out):
    parts = (a, b, c, d)
    chips = 1 << phases
    half = chips // 2
    for side in range(2):
        core = where[1] if side == 0 else 1 - where[1]
        for order in range(chips):
            value = parts[2 * side + order // half][order % half].astype(F32)
            rows, columns = value.shape
            out[
                pl.ds(pl.multiple_of(where[2 + side * chips + order] * rows, 8), rows),
                pl.ds(pl.multiple_of(core * columns, 128), columns),
            ] = value


def widen_rows(where, parts, phases, shape):
    return call(
        partial(widen_rows_kernel, phases),
        (1,),
        [fixed(part.shape) for part in parts],
        fixed(shape),
        struct(shape, F32),
        micros=4,
    )(where, *parts)


def widen_kernel(dims, where, *refs):
    parts, outs, extra = refs[:4], refs[4:-1], refs[-1]
    phases, kinds = dims
    chips = 1 << phases
    half = chips // 2
    summed = jnp.zeros(extra.shape, F32)
    for side in range(2):
        core = where[1] if side == 0 else 1 - where[1]
        for order in range(chips):
            start = 2 * where[2 + side * chips + order] + core
            given = parts[2 * side + order // half].at[order % half]
            at, row = 0, 0
            for count in kinds:
                rows = outs[at].shape[0]
                value = given[row : row + rows, :].astype(F32)
                row += rows
                columns = value.shape[1]
                base = 0
                for out in outs[at : at + count]:
                    size = out.shape[1]
                    first = start * columns - base

                    @pl.when((first >= 0) & (first < size))
                    def _(out=out, first=first, value=value, columns=columns):
                        out[:, pl.ds(pl.multiple_of(first, 128), columns)] = value

                    base += size
                at += count
            summed = summed + given[row:, :].astype(F32)
    extra[...] = summed


def widen(where, parts, phases, kinds):
    shapes = [shape for given in kinds for shape in given]
    rows = sum(given[0][0] for given in kinds)
    shapes.append((parts[0].shape[1] - rows, parts[0].shape[2]))
    return call(
        partial(widen_kernel, (phases, [len(given) for given in kinds])),
        (1,),
        [fixed(part.shape) for part in parts],
        [fixed(shape) for shape in shapes],
        [struct(shape, F32) for shape in shapes],
        micros=4,
    )(where, *parts)


def grads_kernel(dims, where, *refs):
    orders, adds, last, group, cuts, extra = dims
    units = len(orders)
    step = pl.program_id(0)
    at = 0
    outs = refs[units * (2 + 2 * cuts + adds) + extra :]
    for u in range(units):
        right, right_other = refs[at : at + 2]
        at += 2
        value = 0.0
        for given in (right, right_other):
            size = given.shape[1] // cuts
            for i in range(cuts):
                value = value + dot(refs[at][0], given[0, i * size : (i + 1) * size, :])
                at += 1
        for add in refs[at : at + adds]:
            value = value + add[0].astype(F32)
        at += adds
        value = value.astype(BF16)
        if not last:
            outs[0][u] = value
            continue
        for s in range(group):

            @pl.when(step == s)
            def _(s=s, value=value):
                outs[s][: value.shape[0], :] = value
                if extra:
                    outs[s][value.shape[0] :, :] = refs[-group - 1][s]


def grads(where, left, right, maps, shape, units, received, group, extra=None):
    rows, columns = shape
    cuts = len(left[0])
    seq = left[0][0].shape[2]
    left_map, right_map, other_map = maps
    last = units == [0]
    ins, args = [], []
    for order in units:
        lefts = spec((1, rows, seq), partial(left_map, order))
        ins.append(spec((1, seq * cuts, columns), partial(right_map, order)))
        ins.append(spec((1, seq * cuts, columns), partial(other_map, order)))
        ins += [lefts] * (2 * cuts)
        args += [right[0], right[1], *left[0], *left[1]]
        for phase, value in enumerate(received):
            index = order >> (phase + 1)
            ins.append(spec((1, rows, columns), lambda s, w, index=index: (index, s, 0)))
            args.append(value)
    count = len(units)
    more = 0 if extra is None else extra.shape[1]
    if more:
        ins.append(fixed(extra.shape))
        args.append(extra)
    if last:
        outs = [fixed((rows + more, columns))] * group
        out_shape = [struct((rows + more, columns), BF16)] * group
    else:
        outs = [spec((count, rows, columns), lambda s, w: (0, s, 0))]
        out_shape = [struct((count, group * rows, columns), BF16)]
    return call(
        partial(grads_kernel, (units, len(received), last, group, cuts, int(more > 0))),
        (group,),
        ins,
        outs,
        out_shape,
        micros=6,
    )(where, *args)


def after(value, *others):
    return lax.optimization_barrier((value, others))[0]


def local(
    chips,
    group,
    tokens,
    segments,
    lengths,
    cotangent,
    w_qkv,
    b_qv,
    w_out,
    b_out,
    gain_one,
    shift_one,
    w_in,
    b_in,
    w_down,
    b_down,
    gain_two,
    shift_two,
):
    reps = 2 * chips
    phases = chips.bit_length() - 1
    core = lax.axis_index("core")
    chip = lax.axis_index("chip")
    rank = chip * 2 + core
    own = lax.axis_index("shard")
    _, seq_len, model_width = tokens.shape
    ff_rows = w_down.shape[0]
    ff_width = w_in.shape[1]
    qkv_width = w_qkv.shape[1]

    def from_shard(value, step):
        return lax.ppermute(value, "shard", [(i, (i - step) % group) for i in range(group)])

    def to_shard(value, step):
        return lax.ppermute(value, "shard", [(i, (i + step) % group) for i in range(group)])

    def sibling(value):
        return lax.ppermute(value, "core", [(0, 1), (1, 0)])

    def bit(phase, which):
        return 1 << ((phase + which) % phases)

    def swap(value, phase):
        pairs = [
            (q * 2 + c, (q ^ bit(phase, c)) * 2 + c) for q in range(chips) for c in range(2)
        ]
        return lax.ppermute(value, REP, pairs)

    def table(which):
        orders = []
        for order in range(chips):
            mask = sum(bit(f, which) for f in range(phases) if order >> f & 1)
            orders.append(mask)
        return orders

    masks = jnp.where(core == 0, jnp.array(table(0)), jnp.array(table(1)))
    masks_other = jnp.where(core == 0, jnp.array(table(1)), jnp.array(table(0)))
    where = jnp.concatenate(
        [jnp.stack([own, core]), chip ^ masks, chip ^ masks_other]
    ).astype(jnp.int32)

    def gather(value, *gates):
        for phase in range(phases - 1):
            value = jnp.concatenate([value, swap(value, phase)], axis=0)
        rest = swap(value, phases - 1)
        return value, rest, sibling(after(value, gates)), sibling(rest)

    w_one = jnp.concatenate([w_qkv, w_out], axis=1)
    part = w_one.shape[1] // reps
    rows = w_one.shape[0]
    piece_one = lax.dynamic_slice_in_dim(w_one, rank * part, part, axis=1)
    part_in = ff_width // reps
    piece_in = lax.dynamic_slice_in_dim(w_in, rank * part_in, part_in, axis=1)
    part_down = ff_rows // reps
    piece_down = lax.dynamic_slice_in_dim(w_down, rank * part_down, part_down, axis=0)

    class Gather:

        def __init__(self, value):
            self.value = value
            self.first = swap(value, 0)

        def step(self, *gates):
            other = self.first
            for phase in range(phases - 1):
                self.value = after(jnp.concatenate([self.value, other], axis=0), gates)
                other = swap(self.value, phase + 1)
            self.rest = other
            self.side = sibling(self.value)

        def finish(self, *gates):
            self.parts = (self.value, self.rest, self.side, sibling(after(self.rest, gates)))

    got_one = [from_shard(piece_one, s) for s in range(1, group)]

    vectors = (b_qv, b_out, gain_one, shift_one, b_in, b_down, gain_two, shift_two)
    sizes = [v.shape[0] for v in vectors]
    packed = jnp.concatenate(after(vectors, piece_one))
    first_parts = Gather(jnp.stack(got_one)[None])
    first_parts.step()
    packed = after(packed, first_parts.first)
    got_packed = [from_shard(packed, s) for s in range(1, group)]
    first_parts.finish()
    parts_one = first_parts.parts
    piece_in = after(piece_in, parts_one[3])
    got_in = [from_shard(piece_in, s) for s in range(1, group)]
    piece_down = after(piece_down, parts_one[3])

    relative = jnp.stack([packed] + got_packed)
    ordered = jnp.concatenate([relative, relative], axis=0)
    ordered = lax.dynamic_slice_in_dim(ordered, (group - own) % group, group, axis=0)
    full, start = [], 0
    for size in sizes:
        full.append(ordered[:, start : start + size].reshape(1, -1).astype(F32))
        start += size
    bias_qv, bias_out, norm_gone, norm_sone, bias_in, bias_down, norm_gtwo, norm_stwo = full
    none = jnp.zeros((1, model_width), F32)
    bias_qkv = jnp.concatenate(
        [bias_qv[:, :model_width], none, bias_qv[:, model_width:], none], axis=1
    )
    kind = segments[0] * 2 + (jnp.arange(seq_len) < lengths[0]).astype(jnp.int32)
    column, row = kind[:, None], kind[None, :]

    flat_in = tokens[0]
    projected, rest_out = qkv(where, flat_in, w_qkv, parts_one, bias_qkv, group)
    parts_in = Gather(after(jnp.stack(got_in)[None], projected))
    got_down = [from_shard(piece_down, s) for s in range(1, group)]
    count = model_width // (4 * HEAD_DIM)
    context, turned, logs_a = attention(where, projected, flat_in, column, row, 0, count)
    parts_in.step(logs_a)
    parts_down = Gather(after(jnp.stack(got_down)[None], logs_a))
    context, turned, logs_b = attention(
        where,
        projected,
        flat_in,
        column,
        row,
        count,
        count,
        (context, turned),
    )
    first_left = ([turned], [sibling(turned)])
    parts_down.step(logs_b)
    hidden, normed, normed_turned = out_norm(
        where,
        context,
        flat_in,
        w_out,
        rest_out,
        bias_out,
        norm_gone,
        norm_sone,
        group,
    )
    parts_in.finish(hidden)
    parts_in = parts_in.parts
    in_left = ([normed_turned[None]], [sibling(normed_turned)[None]])
    where_down = where
    act, *act_turned, slope = inner(where, normed, w_in, parts_in, bias_in, group)
    parts_down.finish(act)
    parts_down = parts_down.parts
    if part_down % 128:
        merged = jnp.zeros((group - 1, ff_rows, model_width), BF16)
        for unit in range(reps):
            piece = parts_down[2 * unit // chips][unit % (chips // 2)]
            at = block_of(where, unit, chips) * part_down
            merged = lax.dynamic_update_slice_in_dim(merged, piece, at, axis=1)
        fourth = ff_rows // 4
        parts_down = [merged[:, b * fourth : (b + 1) * fourth][None] for b in (0, 2, 1, 3)]
        where_down = jnp.stack([own, 0, 0, 1, 0, 1]).astype(jnp.int32)
    down_left = ([v[None] for v in act_turned], [sibling(v)[None] for v in act_turned])
    output_rows, grad_second, grad_branch, branch_other, sums_two = outer(
        where_down,
        act,
        w_down,
        parts_down,
        hidden,
        cotangent[0],
        (norm_gone, norm_sone, bias_down, norm_gtwo, norm_stwo),
        group,
    )

    class Scatter:

        def __init__(self, left, right, maps, shape):
            self.fixed = (where, left, right, maps, shape)
            self.received = []

        def send(self, *gates):
            phase = len(self.received)
            units = list(range(1 << phase, chips, 2 << phase))
            received = after(self.received, gates) if phase else []
            sent = grads(*self.fixed, units, received, group)[0]
            self.received.append(swap(sent, phase))
            return sent

        def send_rest(self, *gates):
            while len(self.received) < phases:
                sent = self.send(*gates)
            return sent

        def finish(self, *gates, extra=None):
            received = after(self.received, gates)
            parts = grads(*self.fixed, [0], received, group, extra)
            self.own = parts[0]
            self.given = [to_shard(parts[s], s) for s in range(1, group)]
            return parts[0]

        def total(self):
            total = self.own.astype(F32)
            for value in self.given:
                total = total + value.astype(F32)
            return total

    half = model_width // 2
    part_rows = ff_rows // chips
    down_maps = (
        lambda o, s, w: (0, natural(w, s, group) * chips + w[2 + o], 0),
        lambda o, s, w: (0, 0, w[1]),
        lambda o, s, w: (0, 0, 0),
    )
    down_right = (grad_branch[None], sibling(branch_other)[None])
    down = Scatter(down_left, down_right, down_maps, (part_rows, half))
    sent = down.send()
    grad_inner, inner_other, sums_in = slope_back(
        where_down, after(grad_branch, sent), w_down, parts_down, slope, part_in, group
    )
    grad_first, grad_attn, grad_context, sums_one = inner_back(
        where,
        after(grad_inner, in_left),
        w_in,
        parts_in,
        grad_second,
        hidden,
        norm_gone,
        w_out,
        rest_out,
        group,
    )
    in_other = sibling(inner_other)
    sent = down.send_rest(grad_first, first_left)
    in_maps = (
        lambda o, s, w: (0, natural(w, s, group), 0),
        lambda o, s, w: (0, 0, 2 * w[2 + o] + w[1]),
        lambda o, s, w: (0, 0, w[2 + o]),
    )
    in_right = after((grad_inner[None], in_other[None]), sent)
    inward = Scatter(in_left, in_right, in_maps, (rows, part_in))
    sent = inward.send()
    logs = (logs_a, logs_b)
    others, sums_others = attention_back(
        where, projected, after(grad_context, sent), logs, grad_attn, column, row, False, part
    )
    done = down.finish(others)
    other_proj = sibling(after(others, done))
    mine, sums_mine = attention_back(
        where, projected, after(grad_context, done), logs, grad_attn, column, row, True, part
    )
    sent = inward.send_rest(mine)
    each = model_width // part

    def plane(order, w):
        return 2 * w[2 + order] + w[1]

    def compact(o, s, w):
        return (plane(o, w) // each, 0, lax.rem(plane(o, w), each) // 2)

    first_maps = (
        lambda o, s, w: (plane(o, w) // (3 * each), natural(w, s, group), 0),
        compact,
        compact,
    )
    first_right = after((mine, other_proj), sent, down.given)
    first = Scatter(first_left, first_right, first_maps, (rows, part))
    sent = first.send()
    gather_down = Gather(down.total().astype(BF16)[None, None])
    def blocks(core_parity):
        value = jnp.where(core == core_parity, sums_mine, sums_others)
        return value.reshape(3, -1, 1, part)

    sums_proj = jnp.concatenate([blocks(0), blocks(1)], axis=2).reshape(3, model_width)
    small = (
        jnp.concatenate([sums_proj[0], sums_proj[2]]),
        sums_one[2],
        sums_one[0],
        sums_one[1],
        sums_in[0],
        sums_two[2],
        sums_two[0],
        sums_two[1],
    )
    small = jnp.concatenate([v.reshape(group, -1) for v in small], axis=1)
    grad_input = input_back(
        where, after(mine, sent), others, grad_first, w_qkv, parts_one, group
    )
    done = inward.finish(grad_input)
    sent = first.send_rest(done)
    small = jnp.concatenate([small, small], axis=0)
    small = lax.dynamic_slice_in_dim(small, own, group, axis=0)
    extra = -(-small.shape[1] // (16 * part)) * 16
    padded = jnp.pad(small, ((0, 0), (0, extra * part - small.shape[1])))
    padded = padded.reshape(group, extra, part).astype(BF16)
    done = first.finish(sent, extra=padded)
    gather_down = Gather(after(down.total().astype(BF16)[None], done))
    gather_down.step()
    gather_down.finish()
    grad_wdown = widen_rows(where, gather_down.parts, phases, (ff_rows, model_width))
    shares = jnp.concatenate([inward.total(), first.total()], axis=0).astype(BF16)
    final = Gather(shares[None])
    final.step(grad_wdown)
    final.finish()
    grad_win, grad_wqkv, grad_wout, total = widen(
        where,
        final.parts,
        phases,
        [[(rows, ff_width)], [(rows, qkv_width), (rows, model_width)]],
    )
    total = total.reshape(-1)

    vecs, start = [], 0
    for size in sizes:
        vecs.append(total[start : start + size])
        start += size

    return (
        output_rows.reshape(tokens.shape),
        grad_input.reshape(tokens.shape),
        grad_wqkv,
        vecs[0],
        grad_wout,
        vecs[1],
        vecs[2],
        vecs[3],
        grad_win,
        vecs[4],
        grad_wdown,
        vecs[5],
        vecs[6],
        vecs[7],
    )


def solution(mesh):
    reps, group = mesh.devices.shape
    fine = Mesh(mesh.devices.reshape(reps // 2, 2, group), ALL)
    rows = P(ALL, None, None)
    matrix = P("shard", None)
    vector = P("shard")
    in_specs = (
        rows,
        P(ALL, None),
        P(ALL),
        rows,
        matrix,
        vector,
        matrix,
        vector,
        vector,
        vector,
        matrix,
        vector,
        matrix,
        vector,
        vector,
        vector,
    )
    out_specs = (
        rows,
        rows,
        matrix,
        vector,
        matrix,
        vector,
        vector,
        vector,
        matrix,
        vector,
        matrix,
        vector,
        vector,
        vector,
    )
    return jax.shard_map(
        partial(local, reps // 2, group),
        mesh=fine,
        in_specs=in_specs,
        out_specs=out_specs,
        check_vma=False,
    )
```

```python
from functools import partial

import jax
import jax.numpy as jnp
from jax import lax
from jax.experimental import pallas as pl
from jax.experimental.pallas import tpu as pltpu
from jax.sharding import Mesh
from jax.sharding import PartitionSpec as P

HEAD_DIM = 64
REP = ("chip", "core")
ALL = ("chip", "core", "shard")
F32 = jnp.float32
BF16 = jnp.bfloat16
MIB = 1024 * 1024
HINT = 3690000


def dot(left, right):
    return jnp.dot(left, right, preferred_element_type=F32)


def dot_t(left, right):
    return lax.dot_general(left, right, (((1,), (1,)), ((), ())), preferred_element_type=F32)


def t_dot(left, right):
    return lax.dot_general(left, right, (((0,), (0,)), ((), ())), preferred_element_type=F32)


def call(body, grid, ins, outs, out_shape, scratch=(), micros=1, limit=63, aliases=None):
    return pl.pallas_call(
        body,
        grid_spec=pltpu.PrefetchScalarGridSpec(
            num_scalar_prefetch=1,
            grid=grid,
            in_specs=ins,
            out_specs=outs,
            scratch_shapes=list(scratch),
        ),
        out_shape=out_shape,
        compiler_params=pltpu.CompilerParams(
            dimension_semantics=("arbitrary",) * len(grid), vmem_limit_bytes=limit * MIB
        ),
        input_output_aliases=aliases or {},
        cost_estimate=pl.CostEstimate(
            flops=0, bytes_accessed=int(micros * HINT), transcendentals=0
        ),
    )


def spec(shape, index):
    return pl.BlockSpec(shape, index)


def fixed(shape):
    zeros = (0,) * len(shape)
    return pl.BlockSpec(shape, lambda *_: zeros)


def struct(shape, dtype):
    return jax.ShapeDtypeStruct(shape, dtype)


def natural(where, step, group):
    return lax.rem(where[0] + step, group)


def block_of(where, unit, chips):
    return 2 * where[2 + unit] + jnp.where(unit < chips, where[1], 1 - where[1])


ANYWHERE = pl.BlockSpec(memory_space=pl.ANY)


def stream(unit, parts, buffer, sems):
    half = parts[0].shape[0]

    def start(number, slot):
        for index, part in enumerate(parts):

            @pl.when(number // half == index)
            def _(part=part):
                source = part.at[lax.rem(number, half)]
                pltpu.make_async_copy(source, buffer.at[slot], sems.at[slot]).start()

    slot = lax.rem(unit, 2)

    @pl.when(unit == 0)
    def _():
        start(unit, slot)

    @pl.when(unit + 1 < half * len(parts))
    def _():
        start(unit + 1, 1 - slot)

    pltpu.make_async_copy(parts[0].at[0], buffer.at[slot], sems.at[slot]).wait()
    return buffer[slot].reshape(-1, buffer.shape[3])


def stream_scratch(parts):
    return [pltpu.VMEM((2, *parts[0].shape[1:]), BF16), pltpu.SemaphoreType.DMA((2,))]


def stream_whole(step, parts, buffer, sems):
    for index, part in enumerate(parts):

        @pl.when(step == index)
        def _(index=index, part=part):
            slot = index % 2
            pltpu.make_async_copy(part, buffer.at[slot], sems.at[slot]).start()

        @pl.when(step == index + 1)
        def _(index=index, part=part):
            slot = index % 2
            pltpu.make_async_copy(part, buffer.at[slot], sems.at[slot]).wait()


def whole_scratch(parts):
    return [pltpu.VMEM((2, *parts[0].shape), BF16), pltpu.SemaphoreType.DMA((2,))]


def normalise(hidden):
    average = jnp.mean(hidden, axis=-1, keepdims=True)
    centred = hidden - average
    variance = jnp.mean(centred * centred, axis=-1, keepdims=True)
    inverse = lax.rsqrt(variance + 1e-06)
    return centred * inverse, inverse


def normalise_back(grad, unit, inverse, gain):
    scaled = grad * gain
    first = jnp.mean(scaled, axis=-1, keepdims=True)
    second = jnp.mean(scaled * unit, axis=-1, keepdims=True)
    return inverse * (scaled - first - unit * second)


def rows_sum(value):
    return jnp.sum(value, axis=0, keepdims=True)


def roll_into(rolled, x, where, rows, group):
    for s in range(group):
        start = pl.multiple_of(natural(where, s, group) * rows, 128)
        rolled[:, s * rows : (s + 1) * rows] = x[:, pl.ds(start, rows)]


def qkv_kernel(dims, where, x, own, a, b, c, d, bias, out, rest_out, rolled, *scratch):
    group, half, qkv_width = dims
    unit = pl.program_id(0)
    rows, columns = own.shape

    @pl.when(unit == 0)
    def _():
        roll_into(rolled, x, where, rows, group)

    rest = stream(unit, (a, b, c, d), *scratch)
    start = block_of(where, unit, 2 * half) * columns

    @pl.when(start < qkv_width)
    def _():
        total = dot(rolled[:, :rows], own[...]) + dot(rolled[:, rows:], rest)
        out[...] = (total + bias[...]).astype(BF16)

    @pl.when(start >= qkv_width)
    def _():
        place = pl.ds(pl.multiple_of(start - qkv_width, 128), columns)
        rest_out[:, place] = rest


def qkv(where, x, w_qkv, parts, bias, group):
    seq, width = x.shape
    rows, qkv_width = w_qkv.shape
    half, _, _, block = parts[0].shape
    chips = 2 * half
    total = 2 * chips * block
    top = qkv_width // block - 1
    return call(
        partial(qkv_kernel, (group, half, qkv_width)),
        (2 * chips,),
        [
            fixed((seq, width)),
            spec((rows, block), lambda u, w: (0, jnp.minimum(block_of(w, u, chips), top))),
        ]
        + [ANYWHERE] * 4
        + [spec((1, block), lambda u, w: (0, block_of(w, u, chips)))],
        [
            spec((seq, block), lambda u, w: (0, block_of(w, u, chips))),
            fixed((width - rows, total - qkv_width)),
        ],
        [struct((seq, total), BF16), struct((width - rows, total - qkv_width), BF16)],
        [pltpu.VMEM((seq, width), BF16)] + stream_scratch(parts),
        micros=12,
    )(where, x, w_qkv, *parts, bias)


def attend_kernel(first, where, q, k, v, x, column, row, *refs):
    out, turned, log_totals, bias = refs[-4:]
    step = pl.program_id(0)
    turned[0] = x[...].T

    @pl.when(step == 0)
    def _():
        bias[...] = jnp.where(column[...] == row[...], 0.0, -1e30)
        log_totals[...] = jnp.zeros_like(log_totals)

    lanes = lax.broadcasted_iota(jnp.int32, (1, 128), 1)
    heads = q.shape[1] // HEAD_DIM
    for h in range(heads):
        part = slice(h * HEAD_DIM, (h + 1) * HEAD_DIM)
        scores = dot_t(q[:, part] * BF16(HEAD_DIM**-0.5), k[:, part]) + bias[...]
        maxima = jnp.max(scores, axis=1, keepdims=True)
        expo = jnp.exp(scores - maxima)
        totals = jnp.sum(expo, axis=1, keepdims=True)
        probs = (expo * (1.0 / totals)).astype(BF16)
        out[:, part] = dot(probs, v[:, part]).astype(BF16)
        log_totals[...] = jnp.where(
            lanes == (first + step) * heads + h, maxima + jnp.log(totals), log_totals[...]
        )
    turned[1] = out[...].T


def attention(where, projected, x, column, row, first, count, before=()):
    seq, width = x.shape
    block = 2 * HEAD_DIM
    each = width // block
    anywhere = pl.BlockSpec(memory_space=pl.ANY)
    return call(
        partial(attend_kernel, first),
        (count,),
        [
            spec((seq, block), lambda h, w: (0, first + h)),
            spec((seq, block), lambda h, w: (0, each + first + h)),
            spec((seq, block), lambda h, w: (0, 2 * each + first + h)),
            spec((seq, block), lambda h, w: (0, first + h)),
            fixed((seq, 1)),
            fixed((1, seq)),
        ]
        + [anywhere] * len(before),
        [
            spec((seq, block), lambda h, w: (0, first + h)),
            spec((2, block, seq), lambda h, w: (0, first + h, 0)),
            fixed((seq, 128)),
        ],
        [
            struct((seq, width), BF16),
            struct((2, width, seq), BF16),
            struct((seq, 128), F32),
        ],
        [pltpu.VMEM((seq, seq), F32)],
        micros=11,
        aliases={7: 0, 8: 1} if before else None,
    )(where, projected, projected, projected, x, column, row, *before)


def attend_back_kernel(dims, where, q, k, v, grad, logs_a, logs_b, attn, column, row, *refs):
    out, sums, bias = refs
    mine, per = dims
    step = pl.program_id(0)
    pair = pair_of(where, step, mine, per)
    out[3] = attn[...]

    @pl.when(step == 0)
    def _():
        bias[...] = jnp.where(column[...] == row[...], 0.0, -1e30)

    lanes = lax.broadcasted_iota(jnp.int32, (1, 128), 1)
    heads = q.shape[1] // HEAD_DIM
    for h in range(heads):
        part = slice(h * HEAD_DIM, (h + 1) * HEAD_DIM)
        picked = jnp.where(lanes == pair * heads + h, logs_a[...] + logs_b[...], 0.0)
        logs = jnp.sum(picked, axis=1, keepdims=True)
        query = q[:, part] * BF16(HEAD_DIM**-0.5)
        scores = dot_t(query, k[:, part]) + bias[...]
        probs = jnp.exp(scores - logs)
        grad_probs = dot_t(grad[:, part], v[:, part])
        weighted = probs * grad_probs
        low = (weighted - probs * jnp.sum(weighted, axis=1, keepdims=True)).astype(BF16)
        grad_q = (dot(low, k[:, part]) * (HEAD_DIM**-0.5)).astype(BF16)
        grad_k = t_dot(low, query).astype(BF16)
        grad_v = t_dot(probs.astype(BF16), grad[:, part]).astype(BF16)
        for m, value in enumerate((grad_q, grad_k, grad_v)):
            out[m, :, part] = value
            sums[m, :, part] = rows_sum(value.astype(F32))


def pair_of(where, step, mine, per):
    parity = where[1] if mine else 1 - where[1]
    return (2 * (step // per) + parity) * per + lax.rem(step, per)


def attention_back(where, projected, grad, logs, attn, column, row, mine, part):
    seq, width = grad.shape
    block = 2 * HEAD_DIM
    each = width // block
    per = part // block

    def pairs(first):
        return spec((seq, block), lambda h, w: (0, first + pair_of(w, h, mine, per)))

    return call(
        partial(attend_back_kernel, (mine, per)),
        (each // 2,),
        [
            pairs(0),
            pairs(each),
            pairs(2 * each),
            pairs(0),
            fixed((seq, 128)),
            fixed((seq, 128)),
            pairs(0),
            fixed((seq, 1)),
            fixed((1, seq)),
        ],
        [
            spec((4, seq, block), lambda h, w: (0, 0, h)),
            spec((3, 1, block), lambda h, w: (0, 0, h)),
        ],
        [struct((4, seq, width // 2), BF16), struct((3, 1, width // 2), F32)],
        [pltpu.VMEM((seq, seq), F32)],
        micros=13,
    )(where, projected, projected, projected, grad, *logs, attn, column, row)


def out_kernel(group, where, context, x, own, rest, bias, gain, shift, hidden, low, turned):
    rows = own.shape[0]
    total = bias[...] + x[...].astype(F32)
    for s in range(group):
        start = pl.multiple_of(natural(where, s, group) * rows, 128)
        weight = own[...] if s == 0 else rest[(s - 1) * rows : s * rows, :]
        total = total + dot(context[:, pl.ds(start, rows)], weight)
    hidden[...] = total
    unit, _ = normalise(total)
    value = (unit * gain[...] + shift[...]).astype(BF16)
    low[...] = value
    turned[...] = value.T


def out_norm(where, context, x, w_out, rest_out, bias, gain, shift, group):
    seq, width = x.shape
    rows = w_out.shape[0]
    block = seq // 2
    vector = fixed((1, width))
    return call(
        partial(out_kernel, group),
        (seq // block,),
        [
            spec((block, width), lambda i, w: (i, 0)),
            spec((block, width), lambda i, w: (i, 0)),
            fixed((rows, width)),
            fixed((width - rows, width)),
            vector,
            vector,
            vector,
        ],
        [spec((block, width), lambda i, w: (i, 0))] * 2
        + [spec((width, block), lambda i, w: (0, i))],
        [
            struct((seq, width), F32),
            struct((seq, width), BF16),
            struct((width, seq), BF16),
        ],
        micros=6,
    )(where, context, x, w_out, rest_out, bias, gain, shift)


def inner_kernel(dims, where, x, own, a, b, c, d, bias, act, early, late, slope, rolled, *scratch):
    group, half = dims
    unit = pl.program_id(0)

    @pl.when(unit == 0)
    def _():
        roll_into(rolled, x, where, own.shape[0], group)

    rest = stream(unit, (a, b, c, d), *scratch)
    rows = own.shape[0]
    total = dot(rolled[:, :rows], own[...]) + dot(rolled[:, rows:], rest) + bias[...]
    below = 0.5 + 0.5 * lax.erf(total * (0.5**0.5))
    value = (total * below).astype(BF16)
    act[...] = value
    half_seq = early.shape[1]
    early[...] = value[:half_seq].T
    late[...] = value[half_seq:].T
    density = jnp.exp(-0.5 * total * total) * ((2.0 * jnp.pi) ** -0.5)
    slope[...] = (below + total * density).astype(BF16)


def inner(where, x, w_in, parts, bias, group):
    seq, width = x.shape
    rows, columns = w_in.shape
    half, _, _, block = parts[0].shape
    chips = 2 * half

    def columns_at(height):
        return spec((height, block), lambda u, w: (0, block_of(w, u, chips)))

    return call(
        partial(inner_kernel, (group, half)),
        (2 * chips,),
        [fixed((seq, width)), columns_at(rows)] + [ANYWHERE] * 4 + [columns_at(1)],
        [
            columns_at(seq),
            spec((block, seq // 2), lambda u, w: (block_of(w, u, chips), 0)),
            spec((block, seq // 2), lambda u, w: (block_of(w, u, chips), 0)),
            columns_at(seq),
        ],
        [
            struct((seq, columns), BF16),
            struct((columns, seq // 2), BF16),
            struct((columns, seq // 2), BF16),
            struct((seq, columns), BF16),
        ],
        [pltpu.VMEM((seq, width), BF16)] + stream_scratch(parts),
        micros=16,
    )(where, x, w_in, *parts, bias)


def outer_kernel(
    dims,
    where,
    act,
    own,
    a,
    b,
    c,
    d,
    hidden,
    cotangent,
    gain_one,
    shift_one,
    bias,
    gain_two,
    shift_two,
    out,
    grad,
    low,
    low_other,
    sums,
    total,
    picked,
    kept,
    given_rows,
    kept_sems,
    *scratch,
):
    group, half = dims
    step = pl.program_id(0)
    ff_rows = own.shape[0]
    rows = a.shape[2]
    late = [
        pltpu.make_async_copy(hidden, kept, kept_sems.at[0]),
        pltpu.make_async_copy(cotangent, given_rows, kept_sems.at[1]),
    ]
    stream_whole(step, (a, b, c, d), *scratch)

    @pl.when(step == 1)
    def _():
        for copy in late:
            copy.start()

    @pl.when(step == 0)
    def _():
        start = pl.multiple_of(where[0] * ff_rows, 128)
        total[...] = dot(act[:, pl.ds(start, ff_rows)], own[...])

    @pl.when(step > 0)
    def _():
        at = 0
        for i in range(half):
            block = block_of(where, (step - 1) * half + i, 2 * half)
            for s in range(1, group):
                start = natural(where, s, group) * ff_rows + block * rows
                picked[:, at : at + rows] = act[:, pl.ds(pl.multiple_of(start, rows), rows)]
                at += rows
        rest = scratch[0][lax.rem(step - 1, 2)].reshape(-1, a.shape[3])
        total[...] += dot(picked[...], rest)

    @pl.when(step == 4)
    def _():
        for copy in late:
            copy.wait()
        unit_one, _ = normalise(kept[...])
        second = unit_one * gain_one[...] + shift_one[...] + total[...] + bias[...]
        unit, inverse = normalise(second)
        out[...] = (unit * gain_two[...] + shift_two[...]).astype(BF16)
        given = given_rows[...].astype(F32)
        back = normalise_back(given, unit, inverse, gain_two[...])
        grad[...] = back
        rounded = back.astype(BF16)
        low[...] = rounded
        size = low_other.shape[1]
        start = pl.multiple_of((1 - where[1]) * size, 128)
        low_other[...] = low[:, pl.ds(start, size)]
        sums[0:1, :] = rows_sum(given * unit)
        sums[1:2, :] = rows_sum(given)
        sums[2:3, :] = rows_sum(rounded.astype(F32))


def outer(where, act, w_down, parts, hidden, cotangent, vectors, group):
    seq, width = hidden.shape
    rows = w_down.shape[0]
    half, steps, size, _ = parts[0].shape
    full = fixed((seq, width))
    vector = fixed((1, width))
    return call(
        partial(outer_kernel, (group, half)),
        (5,),
        [fixed(act.shape), fixed((rows, width))]
        + [ANYWHERE] * 6
        + [vector] * 5,
        [full, full, full, fixed((seq, width // 2)), fixed((8, width))],
        [
            struct((seq, width), BF16),
            struct((seq, width), F32),
            struct((seq, width), BF16),
            struct((seq, width // 2), BF16),
            struct((8, width), F32),
        ],
        [
            pltpu.VMEM((seq, width), F32),
            pltpu.VMEM((seq, half * steps * size), BF16),
            pltpu.VMEM((seq, width), F32),
            pltpu.VMEM((seq, width), BF16),
            pltpu.SemaphoreType.DMA((2,)),
        ]
        + whole_scratch(parts),
        micros=60,
    )(where, act, w_down, *parts, hidden, cotangent, *vectors)


def slope_kernel(
    dims, where, low, own, a, b, c, d, given, grad, grad_other, sums, slope, slope_sem, *scratch
):
    group, half, width = dims
    step = pl.program_id(0)
    ff_rows = own.shape[0]
    rows = a.shape[2]

    def finish(back, start, size):
        place = pl.ds(pl.multiple_of(start, size), size)
        value = (back * slope[:, place].astype(F32)).astype(BF16)
        grad[:, place] = value
        sums[:, place] = rows_sum(value.astype(F32))
        piece = min(size, width)
        for at in range(0, size, piece):
            block = (start + at) // width
            inside = start + at - block * width

            @pl.when(lax.rem(block, 2) != where[1])
            def _(at=at, block=block, inside=inside):
                there = pl.multiple_of((block // 2) * width + inside, piece)
                grad_other[:, pl.ds(there, piece)] = value[:, at : at + piece]

    slopes = pltpu.make_async_copy(given, slope, slope_sem)
    stream_whole(step, (a, b, c, d), *scratch)

    @pl.when(step == 0)
    def _():
        slopes.start()
        back = dot_t(low[...], own[...])
        slopes.wait()
        finish(back, where[0] * ff_rows, ff_rows)

    @pl.when(step > 0)
    def _():
        rest = scratch[0][lax.rem(step - 1, 2)].reshape(-1, a.shape[3])
        back = dot_t(low[...], rest)
        at = 0
        for i in range(half):
            block = block_of(where, (step - 1) * half + i, 2 * half)
            for s in range(1, group):
                start = natural(where, s, group) * ff_rows + block * rows
                finish(back[:, at : at + rows], start, rows)
                at += rows


def slope_back(where, low, w_down, parts, slope, part, group):
    seq, width = low.shape
    rows = w_down.shape[0]
    half = parts[0].shape[0]
    columns = slope.shape[1]
    return call(
        partial(slope_kernel, (group, half, part)),
        (5,),
        [fixed((seq, width)), fixed((rows, width))]
        + [ANYWHERE] * 5,
        [fixed((seq, columns)), fixed((seq, columns // 2)), fixed((1, columns))],
        [
            struct((seq, columns), BF16),
            struct((seq, columns // 2), BF16),
            struct((1, columns), F32),
        ],
        [pltpu.VMEM((seq, columns), BF16), pltpu.SemaphoreType.DMA(())] + whole_scratch(parts),
        micros=14,
    )(where, low, w_down, *parts, slope)


def inner_back_kernel(
    dims,
    where,
    grad_inner,
    own,
    a,
    b,
    c,
    d,
    grad_two,
    hidden,
    gain,
    own_out,
    rest_out,
    grad_one,
    low_one,
    grad_context,
    sums,
    total,
    *scratch,
):
    group, half = dims
    unit = pl.program_id(0)
    rows = own.shape[0]

    def place(s):
        return pl.ds(pl.multiple_of(natural(where, s, group) * rows, 128), rows)

    @pl.when(unit == 0)
    def _():
        total[...] = jnp.zeros_like(total)

    rest = stream(unit, (a, b, c, d), *scratch)
    total[:, :rows] += dot_t(grad_inner[...], own[...])
    total[:, rows:] += dot_t(grad_inner[...], rest)

    @pl.when(unit == 4 * half - 1)
    def _():
        unit_one, inverse = normalise(hidden[...])
        for s in range(group):
            grad_one[:, place(s)] = total[:, s * rows : (s + 1) * rows]
        given = grad_one[...] + grad_two[...]
        back = normalise_back(given, unit_one, inverse, gain[...])
        grad_one[...] = back
        rounded = back.astype(BF16)
        low_one[...] = rounded
        sums[0:1, :] = rows_sum(given * unit_one)
        sums[1:2, :] = rows_sum(given)
        sums[2:3, :] = rows_sum(rounded.astype(F32))
        grad_context[:, place(0)] = dot_t(rounded, own_out[...]).astype(BF16)
        for s in range(1, group):
            piece = rest_out[(s - 1) * rows : s * rows, :]
            grad_context[:, place(s)] = dot_t(rounded, piece).astype(BF16)


def inner_back(where, grad_inner, w_in, parts, grad_two, hidden, gain, w_out, rest_out, group):
    seq, width = hidden.shape
    rows, columns = w_in.shape
    half, _, _, block = parts[0].shape
    chips = 2 * half
    full = fixed((seq, width))

    def columns_at(height):
        return spec((height, block), lambda u, w: (0, block_of(w, u, chips)))

    return call(
        partial(inner_back_kernel, (group, half)),
        (2 * chips,),
        [columns_at(seq), columns_at(rows)]
        + [ANYWHERE] * 4
        + [full, full, fixed((1, width)), fixed((rows, width)), fixed((width - rows, width))],
        [full, full, full, fixed((8, width))],
        [
            struct((seq, width), F32),
            struct((seq, width), BF16),
            struct((seq, width), BF16),
            struct((8, width), F32),
        ],
        [pltpu.VMEM((seq, width), F32)] + stream_scratch(parts),
        micros=19,
    )(where, grad_inner, w_in, *parts, grad_two, hidden, gain, w_out, rest_out)


def input_back_kernel(dims, where, mine, others, own, a, b, c, d, first, out, total, *scratch):
    group, half, qkv_width = dims
    unit = pl.program_id(0)
    rows, columns = own.shape

    @pl.when(unit == 0)
    def _():
        total[...] = jnp.zeros_like(total)

    rest = stream(unit, (a, b, c, d), *scratch)
    block = block_of(where, unit, 2 * half)
    inside = block * columns < qkv_width
    same = lax.rem(block, 2) == where[1]

    @pl.when(inside)
    def _():
        grad = jnp.where(same, mine[0], others[0])
        total[:, :rows] += dot_t(grad, own[...])
        total[:, rows:] += dot_t(grad, rest)

    @pl.when(unit == 4 * half - 1)
    def _():
        for s in range(group):
            place = pl.ds(pl.multiple_of(natural(where, s, group) * rows, 128), rows)
            out[:, place] = first[:, place] + total[:, s * rows : (s + 1) * rows]


def input_back(where, mine, others, first, w_qkv, parts, group):
    seq, width = first.shape
    rows, qkv_width = w_qkv.shape
    half, _, _, block = parts[0].shape
    chips = 2 * half
    each = width // block
    top = qkv_width // block - 1

    def plane(u, w):
        n = jnp.minimum(block_of(w, u, chips), top)
        return (n // each, 0, lax.rem(n, each) // 2)

    return call(
        partial(input_back_kernel, (group, half, qkv_width)),
        (2 * chips,),
        [
            spec((1, seq, block), plane),
            spec((1, seq, block), plane),
            spec((rows, block), lambda u, w: (0, jnp.minimum(block_of(w, u, chips), top))),
        ]
        + [ANYWHERE] * 4
        + [fixed((seq, width))],
        fixed((seq, width)),
        struct((seq, width), F32),
        [pltpu.VMEM((seq, width), F32)] + stream_scratch(parts),
        micros=12,
    )(where, mine, others, w_qkv, *parts, first)


def widen_kernel(dims, where, *refs):
    parts, outs = refs[:4], refs[4:]
    phases, kinds, more = dims
    chips = 1 << phases
    half = chips // 2
    if more:
        outs, extra = outs[:-1], outs[-1]
        extra[...] = jnp.zeros_like(extra)
    for side in range(2):
        core = where[1] if side == 0 else 1 - where[1]
        for order in range(chips):
            chip = where[2 + side * chips + order]
            given = parts[2 * side + order // half].at[order % half]
            at, row = 0, 0
            for by_rows, rows, count in kinds:
                targets, at = outs[at : at + count], at + count
                columns = given.shape[1]
                step = min(rows, 128)

                @pl.loop(0, rows // step)
                def _(index, row=row, rows=rows, step=step, targets=targets, by_rows=by_rows):
                    inside = pl.multiple_of(index * step, step)
                    value = given[pl.ds(row + inside, step), :].astype(F32)
                    if by_rows:
                        down = pl.ds(pl.multiple_of(chip * rows + inside, step), step)
                        across = pl.ds(pl.multiple_of(core * columns, 128), columns)
                        targets[0][down, across] = value
                        return
                    base = 0
                    for out in targets:
                        first = (2 * chip + core) * columns - base

                        @pl.when((first >= 0) & (first < out.shape[1]))
                        def _(out=out, first=first):
                            across = pl.ds(pl.multiple_of(first, 128), columns)
                            out[pl.ds(inside, step), across] = value

                        base += out.shape[1]

                row += rows
            if more:
                extra[...] += given[row:, :].astype(F32)


def widen(where, parts, phases, kinds, more=0):
    shapes = [shape for *_, given in kinds for shape in given]
    if more:
        shapes.append((more, parts[0].shape[2]))
    short = [(by_rows, rows, len(given)) for by_rows, rows, given in kinds]
    return call(
        partial(widen_kernel, (phases, short, more)),
        (1,),
        [fixed(part.shape) for part in parts],
        [fixed(shape) for shape in shapes],
        [struct(shape, F32) for shape in shapes],
        micros=4,
    )(where, *parts)


def grads_kernel(dims, where, *refs):
    orders, adds, last, group, cuts, extra = dims
    units = len(orders)
    step = pl.program_id(0)
    at = 0
    outs = refs[units * (2 + 2 * cuts + adds) + extra :]
    for u in range(units):
        right, right_other = refs[at : at + 2]
        at += 2
        value = 0.0
        for given in (right, right_other):
            size = given.shape[1] // cuts
            for i in range(cuts):
                value = value + dot(refs[at][0], given[0, i * size : (i + 1) * size, :])
                at += 1
        for add in refs[at : at + adds]:
            value = value + add[0].astype(F32)
        at += adds
        value = value.astype(BF16)
        if not last:
            outs[0][u] = value
            continue
        for s in range(group):

            @pl.when(step == s)
            def _(s=s, value=value):
                outs[s][: value.shape[0], :] = value
                if extra:
                    outs[s][value.shape[0] :, :] = refs[-group - 1][s]


def grads(where, left, right, maps, shape, units, received, group, extra=None):
    rows, columns = shape
    cuts = len(left[0])
    seq = left[0][0].shape[2]
    left_map, right_map, other_map = maps
    last = units == [0]
    ins, args = [], []
    for order in units:
        lefts = spec((1, rows, seq), partial(left_map, order))
        ins.append(spec((1, seq * cuts, columns), partial(right_map, order)))
        ins.append(spec((1, seq * cuts, columns), partial(other_map, order)))
        ins += [lefts] * (2 * cuts)
        args += [right[0], right[1], *left[0], *left[1]]
        for phase, value in enumerate(received):
            index = order >> (phase + 1)
            ins.append(spec((1, rows, columns), lambda s, w, index=index: (index, s, 0)))
            args.append(value)
    count = len(units)
    more = 0 if extra is None else extra.shape[1]
    if more:
        ins.append(fixed(extra.shape))
        args.append(extra)
    if last:
        outs = [fixed((rows + more, columns))] * group
        out_shape = [struct((rows + more, columns), BF16)] * group
    else:
        outs = [spec((count, rows, columns), lambda s, w: (0, s, 0))]
        out_shape = [struct((count, group * rows, columns), BF16)]
    return call(
        partial(grads_kernel, (units, len(received), last, group, cuts, int(more > 0))),
        (group,),
        ins,
        outs,
        out_shape,
        micros=6,
    )(where, *args)


def after(value, *others):
    return lax.optimization_barrier((value, others))[0]


def local(
    chips,
    group,
    tokens,
    segments,
    lengths,
    cotangent,
    w_qkv,
    b_qv,
    w_out,
    b_out,
    gain_one,
    shift_one,
    w_in,
    b_in,
    w_down,
    b_down,
    gain_two,
    shift_two,
):
    reps = 2 * chips
    phases = chips.bit_length() - 1
    core = lax.axis_index("core")
    chip = lax.axis_index("chip")
    rank = chip * 2 + core
    own = lax.axis_index("shard")
    _, seq_len, model_width = tokens.shape
    ff_rows = w_down.shape[0]
    ff_width = w_in.shape[1]
    qkv_width = w_qkv.shape[1]

    def from_shard(value, step):
        return lax.ppermute(value, "shard", [(i, (i - step) % group) for i in range(group)])

    def to_shard(value, step):
        return lax.ppermute(value, "shard", [(i, (i + step) % group) for i in range(group)])

    def sibling(value):
        return lax.ppermute(value, "core", [(0, 1), (1, 0)])

    def bit(phase, which):
        return 1 << ((phase + which) % phases)

    def swap(value, phase):
        pairs = [
            (q * 2 + c, (q ^ bit(phase, c)) * 2 + c) for q in range(chips) for c in range(2)
        ]
        return lax.ppermute(value, REP, pairs)

    def table(which):
        orders = []
        for order in range(chips):
            mask = sum(bit(f, which) for f in range(phases) if order >> f & 1)
            orders.append(mask)
        return orders

    masks = jnp.where(core == 0, jnp.array(table(0)), jnp.array(table(1)))
    masks_other = jnp.where(core == 0, jnp.array(table(1)), jnp.array(table(0)))
    where = jnp.concatenate(
        [jnp.stack([own, core]), chip ^ masks, chip ^ masks_other]
    ).astype(jnp.int32)

    def gather(value, *gates):
        for phase in range(phases - 1):
            value = jnp.concatenate([value, swap(value, phase)], axis=0)
        rest = swap(value, phases - 1)
        return value, rest, sibling(after(value, gates)), sibling(rest)

    w_one = jnp.concatenate([w_qkv, w_out], axis=1)
    part = w_one.shape[1] // reps
    rows = w_one.shape[0]
    piece_one = lax.dynamic_slice_in_dim(w_one, rank * part, part, axis=1)
    part_in = ff_width // reps
    piece_in = lax.dynamic_slice_in_dim(w_in, rank * part_in, part_in, axis=1)
    part_down = ff_rows // reps
    piece_down = lax.dynamic_slice_in_dim(w_down, rank * part_down, part_down, axis=0)

    class Gather:

        def __init__(self, value):
            self.value = value
            self.first = swap(value, 0)

        def step(self, *gates):
            other = self.first
            for phase in range(phases - 1):
                self.value = after(jnp.concatenate([self.value, other], axis=0), gates)
                other = swap(self.value, phase + 1)
            self.rest = other
            self.side = sibling(self.value)

        def finish(self, *gates):
            self.parts = (self.value, self.rest, self.side, sibling(after(self.rest, gates)))

    got_one = [from_shard(piece_one, s) for s in range(1, group)]

    vectors = (b_qv, b_out, gain_one, shift_one, b_in, b_down, gain_two, shift_two)
    sizes = [v.shape[0] for v in vectors]
    packed = jnp.concatenate(after(vectors, piece_one))
    first_parts = Gather(jnp.stack(got_one)[None])
    first_parts.step()
    packed = after(packed, first_parts.first)
    got_packed = [from_shard(packed, s) for s in range(1, group)]
    first_parts.finish()
    parts_one = first_parts.parts
    piece_in = after(piece_in, parts_one[3])
    got_in = [from_shard(piece_in, s) for s in range(1, group)]
    piece_down = after(piece_down, parts_one[3])

    relative = jnp.stack([packed] + got_packed)
    ordered = jnp.concatenate([relative, relative], axis=0)
    ordered = lax.dynamic_slice_in_dim(ordered, (group - own) % group, group, axis=0)
    full, start = [], 0
    for size in sizes:
        full.append(ordered[:, start : start + size].reshape(1, -1).astype(F32))
        start += size
    bias_qv, bias_out, norm_gone, norm_sone, bias_in, bias_down, norm_gtwo, norm_stwo = full
    none = jnp.zeros((1, model_width), F32)
    bias_qkv = jnp.concatenate(
        [bias_qv[:, :model_width], none, bias_qv[:, model_width:], none], axis=1
    )
    kind = segments[0] * 2 + (jnp.arange(seq_len) < lengths[0]).astype(jnp.int32)
    column, row = kind[:, None], kind[None, :]

    flat_in = tokens[0]
    projected, rest_out = qkv(where, flat_in, w_qkv, parts_one, bias_qkv, group)
    parts_in = Gather(after(jnp.stack(got_in)[None], projected))
    got_down = [from_shard(piece_down, s) for s in range(1, group)]
    count = model_width // (4 * HEAD_DIM)
    context, turned, logs_a = attention(where, projected, flat_in, column, row, 0, count)
    parts_in.step(logs_a)
    parts_down = Gather(after(jnp.stack(got_down)[None], logs_a))
    context, turned, logs_b = attention(
        where,
        projected,
        flat_in,
        column,
        row,
        count,
        count,
        (context, turned),
    )
    first_left = ([turned], [sibling(turned)])
    parts_down.step(logs_b)
    hidden, normed, normed_turned = out_norm(
        where,
        context,
        flat_in,
        w_out,
        rest_out,
        bias_out,
        norm_gone,
        norm_sone,
        group,
    )
    parts_in.finish(hidden)
    parts_in = parts_in.parts
    in_left = ([normed_turned[None]], [sibling(normed_turned)[None]])
    where_down = where
    act, *act_turned, slope = inner(where, normed, w_in, parts_in, bias_in, group)
    parts_down.finish(act)
    parts_down = parts_down.parts
    if part_down % 128:
        merged = jnp.zeros((group - 1, ff_rows, model_width), BF16)
        for unit in range(reps):
            piece = parts_down[2 * unit // chips][unit % (chips // 2)]
            at = block_of(where, unit, chips) * part_down
            merged = lax.dynamic_update_slice_in_dim(merged, piece, at, axis=1)
        fourth = ff_rows // 4
        parts_down = [merged[:, b * fourth : (b + 1) * fourth][None] for b in (0, 2, 1, 3)]
        where_down = jnp.stack([own, 0, 0, 1, 0, 1]).astype(jnp.int32)
    down_left = ([v[None] for v in act_turned], [sibling(v)[None] for v in act_turned])
    output_rows, grad_second, grad_branch, branch_other, sums_two = outer(
        where_down,
        act,
        w_down,
        parts_down,
        hidden,
        cotangent[0],
        (norm_gone, norm_sone, bias_down, norm_gtwo, norm_stwo),
        group,
    )

    class Scatter:

        def __init__(self, left, right, maps, shape):
            self.fixed = (where, left, right, maps, shape)
            self.received = []

        def send(self, *gates):
            phase = len(self.received)
            units = list(range(1 << phase, chips, 2 << phase))
            received = after(self.received, gates) if phase else []
            sent = grads(*self.fixed, units, received, group)[0]
            self.received.append(swap(sent, phase))
            return sent

        def send_rest(self, *gates):
            while len(self.received) < phases:
                sent = self.send(*gates)
            return sent

        def finish(self, *gates, extra=None):
            received = after(self.received, gates)
            parts = grads(*self.fixed, [0], received, group, extra)
            self.own = parts[0]
            self.given = [to_shard(parts[s], s) for s in range(1, group)]
            return parts[0]

        def total(self):
            total = self.own.astype(F32)
            for value in self.given:
                total = total + value.astype(F32)
            return total

    half = model_width // 2
    part_rows = ff_rows // chips
    down_maps = (
        lambda o, s, w: (0, natural(w, s, group) * chips + w[2 + o], 0),
        lambda o, s, w: (0, 0, w[1]),
        lambda o, s, w: (0, 0, 0),
    )
    down_right = (grad_branch[None], sibling(branch_other)[None])
    down = Scatter(down_left, down_right, down_maps, (part_rows, half))
    sent = down.send()
    grad_inner, inner_other, sums_in = slope_back(
        where_down, after(grad_branch, sent), w_down, parts_down, slope, part_in, group
    )
    grad_first, grad_attn, grad_context, sums_one = inner_back(
        where,
        after(grad_inner, in_left),
        w_in,
        parts_in,
        grad_second,
        hidden,
        norm_gone,
        w_out,
        rest_out,
        group,
    )
    in_other = sibling(inner_other)
    sent = down.send_rest(grad_first, first_left)
    in_maps = (
        lambda o, s, w: (0, natural(w, s, group), 0),
        lambda o, s, w: (0, 0, 2 * w[2 + o] + w[1]),
        lambda o, s, w: (0, 0, w[2 + o]),
    )
    in_right = after((grad_inner[None], in_other[None]), sent)
    inward = Scatter(in_left, in_right, in_maps, (rows, part_in))
    sent = inward.send()
    logs = (logs_a, logs_b)
    others, sums_others = attention_back(
        where, projected, after(grad_context, sent), logs, grad_attn, column, row, False, part
    )
    done = down.finish(others)
    other_proj = sibling(after(others, done))
    mine, sums_mine = attention_back(
        where, projected, after(grad_context, done), logs, grad_attn, column, row, True, part
    )
    sent = inward.send_rest(mine)
    each = model_width // part

    def plane(order, w):
        return 2 * w[2 + order] + w[1]

    def compact(o, s, w):
        return (plane(o, w) // each, 0, lax.rem(plane(o, w), each) // 2)

    first_maps = (
        lambda o, s, w: (plane(o, w) // (3 * each), natural(w, s, group), 0),
        compact,
        compact,
    )
    first_right = after((mine, other_proj), sent, down.given)
    first = Scatter(first_left, first_right, first_maps, (rows, part))
    sent = first.send()
    def blocks(core_parity):
        value = jnp.where(core == core_parity, sums_mine, sums_others)
        return value.reshape(3, -1, 1, part)

    sums_proj = jnp.concatenate([blocks(0), blocks(1)], axis=2).reshape(3, model_width)
    small = (
        jnp.concatenate([sums_proj[0], sums_proj[2]]),
        sums_one[2],
        sums_one[0],
        sums_one[1],
        sums_in[0],
        sums_two[2],
        sums_two[0],
        sums_two[1],
    )
    small = jnp.concatenate([v.reshape(group, -1) for v in small], axis=1)
    grad_input = input_back(
        where, after(mine, sent), others, grad_first, w_qkv, parts_one, group
    )
    done = inward.finish(grad_input)
    sent = first.send_rest(done)
    small = jnp.concatenate([small, small], axis=0)
    small = lax.dynamic_slice_in_dim(small, own, group, axis=0)
    extra = -(-small.shape[1] // (16 * part)) * 16
    padded = jnp.pad(small, ((0, 0), (0, extra * part - small.shape[1])))
    padded = padded.reshape(group, extra, part).astype(BF16)
    done = first.finish(sent, extra=padded)
    gather_down = Gather(after(down.total().astype(BF16)[None], done))
    gather_down.step()
    gather_down.finish()
    (grad_wdown,) = widen(
        where, gather_down.parts, phases, [(True, part_rows, [(ff_rows, model_width)])]
    )
    shares = jnp.concatenate([inward.total(), first.total()], axis=0).astype(BF16)
    final = Gather(shares[None])
    final.step(grad_wdown)
    final.finish()
    grad_win, grad_wqkv, grad_wout, total = widen(
        where,
        final.parts,
        phases,
        [
            (False, rows, [(rows, ff_width)]),
            (False, rows, [(rows, qkv_width), (rows, model_width)]),
        ],
        extra,
    )
    total = total.reshape(-1)

    vecs, start = [], 0
    for size in sizes:
        vecs.append(total[start : start + size])
        start += size

    return (
        output_rows.reshape(tokens.shape),
        grad_input.reshape(tokens.shape),
        grad_wqkv,
        vecs[0],
        grad_wout,
        vecs[1],
        vecs[2],
        vecs[3],
        grad_win,
        vecs[4],
        grad_wdown,
        vecs[5],
        vecs[6],
        vecs[7],
    )


def solution(mesh):
    reps, group = mesh.devices.shape
    fine = Mesh(mesh.devices.reshape(reps // 2, 2, group), ALL)
    rows = P(ALL, None, None)
    matrix = P("shard", None)
    vector = P("shard")
    in_specs = (
        rows,
        P(ALL, None),
        P(ALL),
        rows,
        matrix,
        vector,
        matrix,
        vector,
        vector,
        vector,
        matrix,
        vector,
        matrix,
        vector,
        vector,
        vector,
    )
    out_specs = (
        rows,
        rows,
        matrix,
        vector,
        matrix,
        vector,
        vector,
        vector,
        matrix,
        vector,
        matrix,
        vector,
        vector,
        vector,
    )
    return jax.shard_map(
        partial(local, reps // 2, group),
        mesh=fine,
        in_specs=in_specs,
        out_specs=out_specs,
        check_vma=False,
    )
```

```python
from functools import partial

import jax
import jax.numpy as jnp
from jax import lax
from jax.experimental import pallas as pl
from jax.experimental.pallas import tpu as pltpu
from jax.sharding import Mesh
from jax.sharding import PartitionSpec as P

HEAD_DIM = 64
REP = ("chip", "core")
ALL = ("chip", "core", "shard")
F32 = jnp.float32
BF16 = jnp.bfloat16
MIB = 1024 * 1024
HINT = 3690000


def dot(left, right):
    return jnp.dot(left, right, preferred_element_type=F32)


def dot_t(left, right):
    return lax.dot_general(left, right, (((1,), (1,)), ((), ())), preferred_element_type=F32)


def t_dot(left, right):
    return lax.dot_general(left, right, (((0,), (0,)), ((), ())), preferred_element_type=F32)


def call(body, grid, ins, outs, out_shape, scratch=(), micros=1, limit=63, aliases=None):
    return pl.pallas_call(
        body,
        grid_spec=pltpu.PrefetchScalarGridSpec(
            num_scalar_prefetch=1,
            grid=grid,
            in_specs=ins,
            out_specs=outs,
            scratch_shapes=list(scratch),
        ),
        out_shape=out_shape,
        compiler_params=pltpu.CompilerParams(
            dimension_semantics=("arbitrary",) * len(grid), vmem_limit_bytes=limit * MIB
        ),
        input_output_aliases=aliases or {},
        cost_estimate=pl.CostEstimate(
            flops=0, bytes_accessed=int(micros * HINT), transcendentals=0
        ),
    )


def spec(shape, index):
    return pl.BlockSpec(shape, index)


def fixed(shape):
    zeros = (0,) * len(shape)
    return pl.BlockSpec(shape, lambda *_: zeros)


def struct(shape, dtype):
    return jax.ShapeDtypeStruct(shape, dtype)


def natural(where, step, group):
    return lax.rem(where[0] + step, group)


def block_of(where, unit, chips):
    return 2 * where[2 + unit] + jnp.where(unit < chips, where[1], 1 - where[1])


ANYWHERE = pl.BlockSpec(memory_space=pl.ANY)


def stream(unit, parts, buffer, sems):
    half = parts[0].shape[0]

    def start(number, slot):
        for index, part in enumerate(parts):

            @pl.when(number // half == index)
            def _(part=part):
                source = part.at[lax.rem(number, half)]
                pltpu.make_async_copy(source, buffer.at[slot], sems.at[slot]).start()

    slot = lax.rem(unit, 2)

    @pl.when(unit == 0)
    def _():
        start(unit, slot)

    @pl.when(unit + 1 < half * len(parts))
    def _():
        start(unit + 1, 1 - slot)

    pltpu.make_async_copy(parts[0].at[0], buffer.at[slot], sems.at[slot]).wait()
    return buffer[slot].reshape(-1, buffer.shape[3])


def stream_scratch(parts):
    return [pltpu.VMEM((2, *parts[0].shape[1:]), BF16), pltpu.SemaphoreType.DMA((2,))]


def stream_whole(step, parts, buffer, sems):
    for index, part in enumerate(parts):

        @pl.when(step == index)
        def _(index=index, part=part):
            slot = index % 2
            pltpu.make_async_copy(part, buffer.at[slot], sems.at[slot]).start()

        @pl.when(step == index + 1)
        def _(index=index, part=part):
            slot = index % 2
            pltpu.make_async_copy(part, buffer.at[slot], sems.at[slot]).wait()


def whole_scratch(parts):
    return [pltpu.VMEM((2, *parts[0].shape), BF16), pltpu.SemaphoreType.DMA((2,))]


def normalise(hidden):
    average = jnp.mean(hidden, axis=-1, keepdims=True)
    centred = hidden - average
    variance = jnp.mean(centred * centred, axis=-1, keepdims=True)
    inverse = lax.rsqrt(variance + 1e-06)
    return centred * inverse, inverse


def normalise_back(grad, unit, inverse, gain):
    scaled = grad * gain
    first = jnp.mean(scaled, axis=-1, keepdims=True)
    second = jnp.mean(scaled * unit, axis=-1, keepdims=True)
    return inverse * (scaled - first - unit * second)


def rows_sum(value):
    return jnp.sum(value, axis=0, keepdims=True)


def roll_into(rolled, x, where, rows, group):
    for s in range(group):
        start = pl.multiple_of(natural(where, s, group) * rows, 128)
        rolled[:, s * rows : (s + 1) * rows] = x[:, pl.ds(start, rows)]


def qkv_kernel(dims, where, x, own, a, b, c, d, bias, out, rest_out, rolled, *scratch):
    group, half, qkv_width = dims
    unit = pl.program_id(0)
    rows, columns = own.shape

    @pl.when(unit == 0)
    def _():
        roll_into(rolled, x, where, rows, group)

    rest = stream(unit, (a, b, c, d), *scratch)
    start = block_of(where, unit, 2 * half) * columns

    @pl.when(start < qkv_width)
    def _():
        total = dot(rolled[:, :rows], own[...]) + dot(rolled[:, rows:], rest)
        out[...] = (total + bias[...]).astype(BF16)

    @pl.when(start >= qkv_width)
    def _():
        place = pl.ds(pl.multiple_of(start - qkv_width, 128), columns)
        rest_out[:, place] = rest


def qkv(where, x, w_qkv, parts, bias, group):
    seq, width = x.shape
    rows, qkv_width = w_qkv.shape
    half, _, _, block = parts[0].shape
    chips = 2 * half
    total = 2 * chips * block
    top = qkv_width // block - 1
    return call(
        partial(qkv_kernel, (group, half, qkv_width)),
        (2 * chips,),
        [
            fixed((seq, width)),
            spec((rows, block), lambda u, w: (0, jnp.minimum(block_of(w, u, chips), top))),
        ]
        + [ANYWHERE] * 4
        + [spec((1, block), lambda u, w: (0, block_of(w, u, chips)))],
        [
            spec((seq, block), lambda u, w: (0, block_of(w, u, chips))),
            fixed((width - rows, total - qkv_width)),
        ],
        [struct((seq, total), BF16), struct((width - rows, total - qkv_width), BF16)],
        [pltpu.VMEM((seq, width), BF16)] + stream_scratch(parts),
        micros=12,
    )(where, x, w_qkv, *parts, bias)


def attend_kernel(first, where, q, k, v, x, column, row, *refs):
    out, turned, log_totals, bias = refs[-4:]
    step = pl.program_id(0)
    turned[0] = x[...].T

    @pl.when(step == 0)
    def _():
        bias[...] = jnp.where(column[...] == row[...], 0.0, -1e30)
        log_totals[...] = jnp.zeros_like(log_totals)

    lanes = lax.broadcasted_iota(jnp.int32, (1, 128), 1)
    heads = q.shape[1] // HEAD_DIM
    for h in range(heads):
        part = slice(h * HEAD_DIM, (h + 1) * HEAD_DIM)
        scores = dot_t(q[:, part] * BF16(HEAD_DIM**-0.5), k[:, part]) + bias[...]
        maxima = jnp.max(scores, axis=1, keepdims=True)
        expo = jnp.exp(scores - maxima)
        totals = jnp.sum(expo, axis=1, keepdims=True)
        probs = (expo * (1.0 / totals)).astype(BF16)
        out[:, part] = dot(probs, v[:, part]).astype(BF16)
        log_totals[...] = jnp.where(
            lanes == (first + step) * heads + h, maxima + jnp.log(totals), log_totals[...]
        )
    turned[1] = out[...].T


def attention(where, projected, x, column, row, first, count, before=()):
    seq, width = x.shape
    block = 2 * HEAD_DIM
    each = width // block
    anywhere = pl.BlockSpec(memory_space=pl.ANY)
    return call(
        partial(attend_kernel, first),
        (count,),
        [
            spec((seq, block), lambda h, w: (0, first + h)),
            spec((seq, block), lambda h, w: (0, each + first + h)),
            spec((seq, block), lambda h, w: (0, 2 * each + first + h)),
            spec((seq, block), lambda h, w: (0, first + h)),
            fixed((seq, 1)),
            fixed((1, seq)),
        ]
        + [anywhere] * len(before),
        [
            spec((seq, block), lambda h, w: (0, first + h)),
            spec((2, block, seq), lambda h, w: (0, first + h, 0)),
            fixed((seq, 128)),
        ],
        [
            struct((seq, width), BF16),
            struct((2, width, seq), BF16),
            struct((seq, 128), F32),
        ],
        [pltpu.VMEM((seq, seq), F32)],
        micros=11,
        aliases={7: 0, 8: 1} if before else None,
    )(where, projected, projected, projected, x, column, row, *before)


def attend_back_kernel(dims, where, q, k, v, grad, logs_a, logs_b, attn, column, row, *refs):
    out, sums, bias = refs
    mine, per = dims
    step = pl.program_id(0)
    pair = pair_of(where, step, mine, per)
    out[3] = attn[...]

    @pl.when(step == 0)
    def _():
        bias[...] = jnp.where(column[...] == row[...], 0.0, -1e30)

    lanes = lax.broadcasted_iota(jnp.int32, (1, 128), 1)
    heads = q.shape[1] // HEAD_DIM
    for h in range(heads):
        part = slice(h * HEAD_DIM, (h + 1) * HEAD_DIM)
        picked = jnp.where(lanes == pair * heads + h, logs_a[...] + logs_b[...], 0.0)
        logs = jnp.sum(picked, axis=1, keepdims=True)
        query = q[:, part] * BF16(HEAD_DIM**-0.5)
        scores = dot_t(query, k[:, part]) + bias[...]
        probs = jnp.exp(scores - logs)
        grad_probs = dot_t(grad[:, part], v[:, part])
        weighted = probs * grad_probs
        low = (weighted - probs * jnp.sum(weighted, axis=1, keepdims=True)).astype(BF16)
        grad_q = (dot(low, k[:, part]) * (HEAD_DIM**-0.5)).astype(BF16)
        grad_k = t_dot(low, query).astype(BF16)
        grad_v = t_dot(probs.astype(BF16), grad[:, part]).astype(BF16)
        for m, value in enumerate((grad_q, grad_k, grad_v)):
            out[m, :, part] = value
            sums[m, :, part] = rows_sum(value.astype(F32))


def pair_of(where, step, mine, per):
    parity = where[1] if mine else 1 - where[1]
    return (2 * (step // per) + parity) * per + lax.rem(step, per)


def attention_back(where, projected, grad, logs, attn, column, row, mine, part):
    seq, width = grad.shape
    block = 2 * HEAD_DIM
    each = width // block
    per = part // block

    def pairs(first):
        return spec((seq, block), lambda h, w: (0, first + pair_of(w, h, mine, per)))

    return call(
        partial(attend_back_kernel, (mine, per)),
        (each // 2,),
        [
            pairs(0),
            pairs(each),
            pairs(2 * each),
            pairs(0),
            fixed((seq, 128)),
            fixed((seq, 128)),
            pairs(0),
            fixed((seq, 1)),
            fixed((1, seq)),
        ],
        [
            spec((4, seq, block), lambda h, w: (0, 0, h)),
            spec((3, 1, block), lambda h, w: (0, 0, h)),
        ],
        [struct((4, seq, width // 2), BF16), struct((3, 1, width // 2), F32)],
        [pltpu.VMEM((seq, seq), F32)],
        micros=13,
    )(where, projected, projected, projected, grad, *logs, attn, column, row)


def out_kernel(group, where, context, x, own, rest, bias, gain, shift, hidden, low, turned):
    rows = own.shape[0]
    total = bias[...] + x[...].astype(F32)
    for s in range(group):
        start = pl.multiple_of(natural(where, s, group) * rows, 128)
        weight = own[...] if s == 0 else rest[(s - 1) * rows : s * rows, :]
        total = total + dot(context[:, pl.ds(start, rows)], weight)
    hidden[...] = total
    unit, _ = normalise(total)
    value = (unit * gain[...] + shift[...]).astype(BF16)
    low[...] = value
    turned[...] = value.T


def out_norm(where, context, x, w_out, rest_out, bias, gain, shift, group):
    seq, width = x.shape
    rows = w_out.shape[0]
    block = seq // 2
    vector = fixed((1, width))
    return call(
        partial(out_kernel, group),
        (seq // block,),
        [
            spec((block, width), lambda i, w: (i, 0)),
            spec((block, width), lambda i, w: (i, 0)),
            fixed((rows, width)),
            fixed((width - rows, width)),
            vector,
            vector,
            vector,
        ],
        [spec((block, width), lambda i, w: (i, 0))] * 2
        + [spec((width, block), lambda i, w: (0, i))],
        [
            struct((seq, width), F32),
            struct((seq, width), BF16),
            struct((width, seq), BF16),
        ],
        micros=6,
    )(where, context, x, w_out, rest_out, bias, gain, shift)


def inner_kernel(dims, where, x, own, a, b, c, d, bias, act, early, late, slope, rolled, *scratch):
    group, half = dims
    unit = pl.program_id(0)

    @pl.when(unit == 0)
    def _():
        roll_into(rolled, x, where, own.shape[0], group)

    rest = stream(unit, (a, b, c, d), *scratch)
    rows = own.shape[0]
    total = dot(rolled[:, :rows], own[...]) + dot(rolled[:, rows:], rest) + bias[...]
    below = 0.5 + 0.5 * lax.erf(total * (0.5**0.5))
    value = (total * below).astype(BF16)
    act[...] = value
    half_seq = early.shape[1]
    early[...] = value[:half_seq].T
    late[...] = value[half_seq:].T
    density = jnp.exp(-0.5 * total * total) * ((2.0 * jnp.pi) ** -0.5)
    slope[...] = (below + total * density).astype(BF16)


def inner(where, x, w_in, parts, bias, group):
    seq, width = x.shape
    rows, columns = w_in.shape
    half, _, _, block = parts[0].shape
    chips = 2 * half

    def columns_at(height):
        return spec((height, block), lambda u, w: (0, block_of(w, u, chips)))

    return call(
        partial(inner_kernel, (group, half)),
        (2 * chips,),
        [fixed((seq, width)), columns_at(rows)] + [ANYWHERE] * 4 + [columns_at(1)],
        [
            columns_at(seq),
            spec((block, seq // 2), lambda u, w: (block_of(w, u, chips), 0)),
            spec((block, seq // 2), lambda u, w: (block_of(w, u, chips), 0)),
            columns_at(seq),
        ],
        [
            struct((seq, columns), BF16),
            struct((columns, seq // 2), BF16),
            struct((columns, seq // 2), BF16),
            struct((seq, columns), BF16),
        ],
        [pltpu.VMEM((seq, width), BF16)] + stream_scratch(parts),
        micros=16,
    )(where, x, w_in, *parts, bias)


def outer_kernel(
    dims,
    where,
    act,
    own,
    a,
    b,
    c,
    d,
    hidden,
    cotangent,
    gain_one,
    shift_one,
    bias,
    gain_two,
    shift_two,
    out,
    grad,
    low,
    low_other,
    sums,
    total,
    picked,
    kept,
    given_rows,
    kept_sems,
    *scratch,
):
    group, half = dims
    step = pl.program_id(0)
    ff_rows = own.shape[0]
    rows = a.shape[2]
    late = [
        pltpu.make_async_copy(hidden, kept, kept_sems.at[0]),
        pltpu.make_async_copy(cotangent, given_rows, kept_sems.at[1]),
    ]
    stream_whole(step, (a, b, c, d), *scratch)

    @pl.when(step == 1)
    def _():
        for copy in late:
            copy.start()

    @pl.when(step == 0)
    def _():
        start = pl.multiple_of(where[0] * ff_rows, 128)
        total[...] = dot(act[:, pl.ds(start, ff_rows)], own[...])

    @pl.when(step > 0)
    def _():
        at = 0
        for i in range(half):
            block = block_of(where, (step - 1) * half + i, 2 * half)
            for s in range(1, group):
                start = natural(where, s, group) * ff_rows + block * rows
                picked[:, at : at + rows] = act[:, pl.ds(pl.multiple_of(start, rows), rows)]
                at += rows
        rest = scratch[0][lax.rem(step - 1, 2)].reshape(-1, a.shape[3])
        total[...] += dot(picked[...], rest)

    @pl.when(step == 4)
    def _():
        for copy in late:
            copy.wait()
        unit_one, _ = normalise(kept[...])
        second = unit_one * gain_one[...] + shift_one[...] + total[...] + bias[...]
        unit, inverse = normalise(second)
        out[...] = (unit * gain_two[...] + shift_two[...]).astype(BF16)
        given = given_rows[...].astype(F32)
        back = normalise_back(given, unit, inverse, gain_two[...])
        grad[...] = back
        rounded = back.astype(BF16)
        low[...] = rounded
        size = low_other.shape[1]
        start = pl.multiple_of((1 - where[1]) * size, 128)
        low_other[...] = low[:, pl.ds(start, size)]
        sums[0:1, :] = rows_sum(given * unit)
        sums[1:2, :] = rows_sum(given)
        sums[2:3, :] = rows_sum(rounded.astype(F32))


def outer(where, act, w_down, parts, hidden, cotangent, vectors, group):
    seq, width = hidden.shape
    rows = w_down.shape[0]
    half, steps, size, _ = parts[0].shape
    full = fixed((seq, width))
    vector = fixed((1, width))
    return call(
        partial(outer_kernel, (group, half)),
        (5,),
        [fixed(act.shape), fixed((rows, width))]
        + [ANYWHERE] * 6
        + [vector] * 5,
        [full, full, full, fixed((seq, width // 2)), fixed((8, width))],
        [
            struct((seq, width), BF16),
            struct((seq, width), F32),
            struct((seq, width), BF16),
            struct((seq, width // 2), BF16),
            struct((8, width), F32),
        ],
        [
            pltpu.VMEM((seq, width), F32),
            pltpu.VMEM((seq, half * steps * size), BF16),
            pltpu.VMEM((seq, width), F32),
            pltpu.VMEM((seq, width), BF16),
            pltpu.SemaphoreType.DMA((2,)),
        ]
        + whole_scratch(parts),
        micros=60,
    )(where, act, w_down, *parts, hidden, cotangent, *vectors)


def slope_kernel(
    dims, where, low, own, a, b, c, d, given, grad, grad_other, sums, slope, slope_sem, *scratch
):
    group, half, width = dims
    step = pl.program_id(0)
    ff_rows = own.shape[0]
    rows = a.shape[2]

    def finish(back, start, size):
        place = pl.ds(pl.multiple_of(start, size), size)
        value = (back * slope[:, place].astype(F32)).astype(BF16)
        grad[:, place] = value
        sums[:, place] = rows_sum(value.astype(F32))
        piece = min(size, width)
        for at in range(0, size, piece):
            block = (start + at) // width
            inside = start + at - block * width

            @pl.when(lax.rem(block, 2) != where[1])
            def _(at=at, block=block, inside=inside):
                there = pl.multiple_of((block // 2) * width + inside, piece)
                grad_other[:, pl.ds(there, piece)] = value[:, at : at + piece]

    slopes = pltpu.make_async_copy(given, slope, slope_sem)
    stream_whole(step, (a, b, c, d), *scratch)

    @pl.when(step == 0)
    def _():
        slopes.start()
        back = dot_t(low[...], own[...])
        slopes.wait()
        finish(back, where[0] * ff_rows, ff_rows)

    @pl.when(step > 0)
    def _():
        rest = scratch[0][lax.rem(step - 1, 2)].reshape(-1, a.shape[3])
        back = dot_t(low[...], rest)
        at = 0
        for i in range(half):
            block = block_of(where, (step - 1) * half + i, 2 * half)
            for s in range(1, group):
                start = natural(where, s, group) * ff_rows + block * rows
                finish(back[:, at : at + rows], start, rows)
                at += rows


def slope_back(where, low, w_down, parts, slope, part, group):
    seq, width = low.shape
    rows = w_down.shape[0]
    half = parts[0].shape[0]
    columns = slope.shape[1]
    return call(
        partial(slope_kernel, (group, half, part)),
        (5,),
        [fixed((seq, width)), fixed((rows, width))]
        + [ANYWHERE] * 5,
        [fixed((seq, columns)), fixed((seq, columns // 2)), fixed((1, columns))],
        [
            struct((seq, columns), BF16),
            struct((seq, columns // 2), BF16),
            struct((1, columns), F32),
        ],
        [pltpu.VMEM((seq, columns), BF16), pltpu.SemaphoreType.DMA(())] + whole_scratch(parts),
        micros=14,
    )(where, low, w_down, *parts, slope)


def inner_back_kernel(
    dims,
    where,
    grad_inner,
    own,
    a,
    b,
    c,
    d,
    grad_two,
    hidden,
    gain,
    own_out,
    rest_out,
    grad_one,
    low_one,
    grad_context,
    sums,
    total,
    *scratch,
):
    group, half = dims
    unit = pl.program_id(0)
    rows = own.shape[0]

    def place(s):
        return pl.ds(pl.multiple_of(natural(where, s, group) * rows, 128), rows)

    @pl.when(unit == 0)
    def _():
        total[...] = jnp.zeros_like(total)

    rest = stream(unit, (a, b, c, d), *scratch)
    total[:, :rows] += dot_t(grad_inner[...], own[...])
    total[:, rows:] += dot_t(grad_inner[...], rest)

    @pl.when(unit == 4 * half - 1)
    def _():
        unit_one, inverse = normalise(hidden[...])
        for s in range(group):
            grad_one[:, place(s)] = total[:, s * rows : (s + 1) * rows]
        given = grad_one[...] + grad_two[...]
        back = normalise_back(given, unit_one, inverse, gain[...])
        grad_one[...] = back
        rounded = back.astype(BF16)
        low_one[...] = rounded
        sums[0:1, :] = rows_sum(given * unit_one)
        sums[1:2, :] = rows_sum(given)
        sums[2:3, :] = rows_sum(rounded.astype(F32))
        grad_context[:, place(0)] = dot_t(rounded, own_out[...]).astype(BF16)
        for s in range(1, group):
            piece = rest_out[(s - 1) * rows : s * rows, :]
            grad_context[:, place(s)] = dot_t(rounded, piece).astype(BF16)


def inner_back(where, grad_inner, w_in, parts, grad_two, hidden, gain, w_out, rest_out, group):
    seq, width = hidden.shape
    rows, columns = w_in.shape
    half, _, _, block = parts[0].shape
    chips = 2 * half
    full = fixed((seq, width))

    def columns_at(height):
        return spec((height, block), lambda u, w: (0, block_of(w, u, chips)))

    return call(
        partial(inner_back_kernel, (group, half)),
        (2 * chips,),
        [columns_at(seq), columns_at(rows)]
        + [ANYWHERE] * 4
        + [full, full, fixed((1, width)), fixed((rows, width)), fixed((width - rows, width))],
        [full, full, full, fixed((8, width))],
        [
            struct((seq, width), F32),
            struct((seq, width), BF16),
            struct((seq, width), BF16),
            struct((8, width), F32),
        ],
        [pltpu.VMEM((seq, width), F32)] + stream_scratch(parts),
        micros=19,
    )(where, grad_inner, w_in, *parts, grad_two, hidden, gain, w_out, rest_out)


def input_back_kernel(dims, where, mine, others, own, a, b, c, d, first, out, total, *scratch):
    group, half, qkv_width = dims
    unit = pl.program_id(0)
    rows, columns = own.shape

    @pl.when(unit == 0)
    def _():
        total[...] = jnp.zeros_like(total)

    rest = stream(unit, (a, b, c, d), *scratch)
    block = block_of(where, unit, 2 * half)
    inside = block * columns < qkv_width
    same = lax.rem(block, 2) == where[1]

    @pl.when(inside)
    def _():
        grad = jnp.where(same, mine[0], others[0])
        total[:, :rows] += dot_t(grad, own[...])
        total[:, rows:] += dot_t(grad, rest)

    @pl.when(unit == 4 * half - 1)
    def _():
        for s in range(group):
            place = pl.ds(pl.multiple_of(natural(where, s, group) * rows, 128), rows)
            out[:, place] = first[:, place] + total[:, s * rows : (s + 1) * rows]


def input_back(where, mine, others, first, w_qkv, parts, group):
    seq, width = first.shape
    rows, qkv_width = w_qkv.shape
    half, _, _, block = parts[0].shape
    chips = 2 * half
    each = width // block
    top = qkv_width // block - 1

    def plane(u, w):
        n = jnp.minimum(block_of(w, u, chips), top)
        return (n // each, 0, lax.rem(n, each) // 2)

    return call(
        partial(input_back_kernel, (group, half, qkv_width)),
        (2 * chips,),
        [
            spec((1, seq, block), plane),
            spec((1, seq, block), plane),
            spec((rows, block), lambda u, w: (0, jnp.minimum(block_of(w, u, chips), top))),
        ]
        + [ANYWHERE] * 4
        + [fixed((seq, width))],
        fixed((seq, width)),
        struct((seq, width), F32),
        [pltpu.VMEM((seq, width), F32)] + stream_scratch(parts),
        micros=12,
    )(where, mine, others, w_qkv, *parts, first)


def widen_kernel(dims, where, *refs):
    parts, outs = refs[:4], refs[4:]
    phases, kinds, more = dims
    chips = 1 << phases
    half = chips // 2
    if more:
        outs, extra = outs[:-1], outs[-1]
        extra[...] = jnp.zeros_like(extra)
    for side in range(2):
        core = where[1] if side == 0 else 1 - where[1]
        for order in range(chips):
            chip = where[2 + side * chips + order]
            given = parts[2 * side + order // half].at[order % half]
            at, row = 0, 0
            for by_rows, rows, count in kinds:
                targets, at = outs[at : at + count], at + count
                columns = given.shape[1]
                step = min(rows, 128)

                @pl.loop(0, rows // step)
                def _(index, row=row, rows=rows, step=step, targets=targets, by_rows=by_rows):
                    inside = pl.multiple_of(index * step, step)
                    value = given[pl.ds(row + inside, step), :].astype(F32)
                    if by_rows:
                        down = pl.ds(pl.multiple_of(chip * rows + inside, step), step)
                        across = pl.ds(pl.multiple_of(core * columns, 128), columns)
                        targets[0][down, across] = value
                        return
                    base = 0
                    for out in targets:
                        first = (2 * chip + core) * columns - base

                        @pl.when((first >= 0) & (first < out.shape[1]))
                        def _(out=out, first=first):
                            across = pl.ds(pl.multiple_of(first, 128), columns)
                            out[pl.ds(inside, step), across] = value

                        base += out.shape[1]

                row += rows
            if more:
                extra[...] += given[row:, :].astype(F32)


def widen(where, parts, phases, kinds, more=0):
    shapes = [shape for *_, given in kinds for shape in given]
    if more:
        shapes.append((more, parts[0].shape[2]))
    short = [(by_rows, rows, len(given)) for by_rows, rows, given in kinds]
    return call(
        partial(widen_kernel, (phases, short, more)),
        (1,),
        [fixed(part.shape) for part in parts],
        [fixed(shape) for shape in shapes],
        [struct(shape, F32) for shape in shapes],
        micros=4,
    )(where, *parts)


def grads_kernel(dims, where, *refs):
    orders, adds, last, group, cuts, extra = dims
    units = len(orders)
    step = pl.program_id(0)
    at = 0
    outs = refs[units * (2 + 2 * cuts + adds) + extra :]
    for u in range(units):
        right, right_other = refs[at : at + 2]
        at += 2
        value = 0.0
        for given in (right, right_other):
            size = given.shape[1] // cuts
            for i in range(cuts):
                value = value + dot(refs[at][0], given[0, i * size : (i + 1) * size, :])
                at += 1
        for add in refs[at : at + adds]:
            value = value + add[0].astype(F32)
        at += adds
        value = value.astype(BF16)
        if not last:
            outs[0][u] = value
            continue
        for s in range(group):

            @pl.when(step == s)
            def _(s=s, value=value):
                outs[s][: value.shape[0], :] = value
                if extra:
                    outs[s][value.shape[0] :, :] = refs[-group - 1][s]


def grads(where, left, right, maps, shape, units, received, group, extra=None):
    rows, columns = shape
    cuts = len(left[0])
    seq = left[0][0].shape[2]
    left_map, right_map, other_map = maps
    last = units == [0]
    ins, args = [], []
    for order in units:
        lefts = spec((1, rows, seq), partial(left_map, order))
        ins.append(spec((1, seq * cuts, columns), partial(right_map, order)))
        ins.append(spec((1, seq * cuts, columns), partial(other_map, order)))
        ins += [lefts] * (2 * cuts)
        args += [right[0], right[1], *left[0], *left[1]]
        for phase, value in enumerate(received):
            index = order >> (phase + 1)
            ins.append(spec((1, rows, columns), lambda s, w, index=index: (index, s, 0)))
            args.append(value)
    count = len(units)
    more = 0 if extra is None else extra.shape[1]
    if more:
        ins.append(fixed(extra.shape))
        args.append(extra)
    if last:
        outs = [fixed((rows + more, columns))] * group
        out_shape = [struct((rows + more, columns), BF16)] * group
    else:
        outs = [spec((count, rows, columns), lambda s, w: (0, s, 0))]
        out_shape = [struct((count, group * rows, columns), BF16)]
    return call(
        partial(grads_kernel, (units, len(received), last, group, cuts, int(more > 0))),
        (group,),
        ins,
        outs,
        out_shape,
        micros=6,
    )(where, *args)


def after(value, *others):
    return lax.optimization_barrier((value, others))[0]


def local(
    chips,
    group,
    tokens,
    segments,
    lengths,
    cotangent,
    w_qkv,
    b_qv,
    w_out,
    b_out,
    gain_one,
    shift_one,
    w_in,
    b_in,
    w_down,
    b_down,
    gain_two,
    shift_two,
):
    reps = 2 * chips
    phases = chips.bit_length() - 1
    core = lax.axis_index("core")
    chip = lax.axis_index("chip")
    rank = chip * 2 + core
    own = lax.axis_index("shard")
    _, seq_len, model_width = tokens.shape
    ff_rows = w_down.shape[0]
    ff_width = w_in.shape[1]
    qkv_width = w_qkv.shape[1]

    def from_shard(value, step):
        return lax.ppermute(value, "shard", [(i, (i - step) % group) for i in range(group)])

    def to_shard(value, step):
        return lax.ppermute(value, "shard", [(i, (i + step) % group) for i in range(group)])

    def sibling(value):
        return lax.ppermute(value, "core", [(0, 1), (1, 0)])

    def bit(phase, which):
        return 1 << ((phase + which) % phases)

    def swap(value, phase):
        pairs = [
            (q * 2 + c, (q ^ bit(phase, c)) * 2 + c) for q in range(chips) for c in range(2)
        ]
        return lax.ppermute(value, REP, pairs)

    def table(which):
        orders = []
        for order in range(chips):
            mask = sum(bit(f, which) for f in range(phases) if order >> f & 1)
            orders.append(mask)
        return orders

    masks = jnp.where(core == 0, jnp.array(table(0)), jnp.array(table(1)))
    masks_other = jnp.where(core == 0, jnp.array(table(1)), jnp.array(table(0)))
    where = jnp.concatenate(
        [jnp.stack([own, core]), chip ^ masks, chip ^ masks_other]
    ).astype(jnp.int32)

    def gather(value, *gates):
        for phase in range(phases - 1):
            value = jnp.concatenate([value, swap(value, phase)], axis=0)
        rest = swap(value, phases - 1)
        return value, rest, sibling(after(value, gates)), sibling(rest)

    w_one = jnp.concatenate([w_qkv, w_out], axis=1)
    part = w_one.shape[1] // reps
    rows = w_one.shape[0]
    piece_one = lax.dynamic_slice_in_dim(w_one, rank * part, part, axis=1)
    part_in = ff_width // reps
    piece_in = lax.dynamic_slice_in_dim(w_in, rank * part_in, part_in, axis=1)
    part_down = ff_rows // reps
    piece_down = lax.dynamic_slice_in_dim(w_down, rank * part_down, part_down, axis=0)

    class Gather:

        def __init__(self, value):
            self.value = value
            self.first = swap(value, 0)

        def step(self, *gates):
            other = self.first
            for phase in range(phases - 1):
                self.value = after(jnp.concatenate([self.value, other], axis=0), gates)
                other = swap(self.value, phase + 1)
            self.rest = other
            self.side = sibling(self.value)

        def finish(self, *gates):
            self.parts = (self.value, self.rest, self.side, sibling(after(self.rest, gates)))

    got_one = [from_shard(piece_one, s) for s in range(1, group)]

    vectors = (b_qv, b_out, gain_one, shift_one, b_in, b_down, gain_two, shift_two)
    sizes = [v.shape[0] for v in vectors]
    packed = jnp.concatenate(after(vectors, piece_one))
    first_parts = Gather(jnp.stack(got_one)[None])
    first_parts.step()
    packed = after(packed, got_one)
    got_packed = [from_shard(packed, s) for s in range(1, group)]
    first_parts.finish(got_packed)
    parts_one = first_parts.parts
    piece_in = after(piece_in, parts_one[3])
    got_in = [from_shard(piece_in, s) for s in range(1, group)]
    piece_down = after(piece_down, parts_one[3])

    relative = jnp.stack([packed] + got_packed)
    ordered = jnp.concatenate([relative, relative], axis=0)
    ordered = lax.dynamic_slice_in_dim(ordered, (group - own) % group, group, axis=0)
    full, start = [], 0
    for size in sizes:
        full.append(ordered[:, start : start + size].reshape(1, -1).astype(F32))
        start += size
    bias_qv, bias_out, norm_gone, norm_sone, bias_in, bias_down, norm_gtwo, norm_stwo = full
    none = jnp.zeros((1, model_width), F32)
    bias_qkv = jnp.concatenate(
        [bias_qv[:, :model_width], none, bias_qv[:, model_width:], none], axis=1
    )
    kind = segments[0] * 2 + (jnp.arange(seq_len) < lengths[0]).astype(jnp.int32)
    column, row = kind[:, None], kind[None, :]

    flat_in = tokens[0]
    projected, rest_out = qkv(where, flat_in, w_qkv, parts_one, bias_qkv, group)
    parts_in = Gather(after(jnp.stack(got_in)[None], projected))
    got_down = [from_shard(piece_down, s) for s in range(1, group)]
    count = model_width // (4 * HEAD_DIM)
    context, turned, logs_a = attention(where, projected, flat_in, column, row, 0, count)
    parts_in.step(logs_a)
    parts_down = Gather(after(jnp.stack(got_down)[None], logs_a))
    context, turned, logs_b = attention(
        where,
        projected,
        flat_in,
        column,
        row,
        count,
        count,
        (context, turned),
    )
    first_left = ([turned], [sibling(turned)])
    parts_down.step(logs_b)
    hidden, normed, normed_turned = out_norm(
        where,
        context,
        flat_in,
        w_out,
        rest_out,
        bias_out,
        norm_gone,
        norm_sone,
        group,
    )
    parts_in.finish(hidden)
    parts_in = parts_in.parts
    in_left = ([normed_turned[None]], [sibling(normed_turned)[None]])
    where_down = where
    act, *act_turned, slope = inner(where, normed, w_in, parts_in, bias_in, group)
    parts_down.finish(act)
    parts_down = parts_down.parts
    if part_down % 128:
        merged = jnp.zeros((group - 1, ff_rows, model_width), BF16)
        for unit in range(reps):
            piece = parts_down[2 * unit // chips][unit % (chips // 2)]
            at = block_of(where, unit, chips) * part_down
            merged = lax.dynamic_update_slice_in_dim(merged, piece, at, axis=1)
        fourth = ff_rows // 4
        parts_down = [merged[:, b * fourth : (b + 1) * fourth][None] for b in (0, 2, 1, 3)]
        where_down = jnp.stack([own, 0, 0, 1, 0, 1]).astype(jnp.int32)
    down_left = ([v[None] for v in act_turned], [sibling(v)[None] for v in act_turned])
    output_rows, grad_second, grad_branch, branch_other, sums_two = outer(
        where_down,
        act,
        w_down,
        parts_down,
        hidden,
        cotangent[0],
        (norm_gone, norm_sone, bias_down, norm_gtwo, norm_stwo),
        group,
    )

    class Scatter:

        def __init__(self, left, right, maps, shape):
            self.fixed = (where, left, right, maps, shape)
            self.received = []

        def send(self, *gates):
            phase = len(self.received)
            units = list(range(1 << phase, chips, 2 << phase))
            received = after(self.received, gates) if phase else []
            sent = grads(*self.fixed, units, received, group)[0]
            self.received.append(swap(sent, phase))
            return sent

        def send_rest(self, *gates):
            while len(self.received) < phases:
                sent = self.send(*gates)
            return sent

        def finish(self, *gates, extra=None):
            received = after(self.received, gates)
            parts = grads(*self.fixed, [0], received, group, extra)
            self.own = parts[0]
            self.given = [to_shard(parts[s], s) for s in range(1, group)]
            return parts[0]

        def total(self):
            total = self.own.astype(F32)
            for value in self.given:
                total = total + value.astype(F32)
            return total

    half = model_width // 2
    part_rows = ff_rows // chips
    down_maps = (
        lambda o, s, w: (0, natural(w, s, group) * chips + w[2 + o], 0),
        lambda o, s, w: (0, 0, w[1]),
        lambda o, s, w: (0, 0, 0),
    )
    down_right = (grad_branch[None], sibling(branch_other)[None])
    down = Scatter(down_left, down_right, down_maps, (part_rows, half))
    sent = down.send()
    grad_inner, inner_other, sums_in = slope_back(
        where_down, after(grad_branch, sent), w_down, parts_down, slope, part_in, group
    )
    grad_first, grad_attn, grad_context, sums_one = inner_back(
        where,
        after(grad_inner, in_left),
        w_in,
        parts_in,
        grad_second,
        hidden,
        norm_gone,
        w_out,
        rest_out,
        group,
    )
    in_other = sibling(inner_other)
    sent = down.send_rest(grad_first, first_left)
    in_maps = (
        lambda o, s, w: (0, natural(w, s, group), 0),
        lambda o, s, w: (0, 0, 2 * w[2 + o] + w[1]),
        lambda o, s, w: (0, 0, w[2 + o]),
    )
    in_right = after((grad_inner[None], in_other[None]), sent)
    inward = Scatter(in_left, in_right, in_maps, (rows, part_in))
    sent = inward.send()
    logs = (logs_a, logs_b)
    others, sums_others = attention_back(
        where, projected, after(grad_context, sent), logs, grad_attn, column, row, False, part
    )
    done = down.finish(others)
    other_proj = sibling(after(others, done))
    mine, sums_mine = attention_back(
        where, projected, after(grad_context, done), logs, grad_attn, column, row, True, part
    )
    sent = inward.send_rest(mine)
    each = model_width // part

    def plane(order, w):
        return 2 * w[2 + order] + w[1]

    def compact(o, s, w):
        return (plane(o, w) // each, 0, lax.rem(plane(o, w), each) // 2)

    first_maps = (
        lambda o, s, w: (plane(o, w) // (3 * each), natural(w, s, group), 0),
        compact,
        compact,
    )
    first_right = after((mine, other_proj), sent, down.given)
    first = Scatter(first_left, first_right, first_maps, (rows, part))
    sent = first.send()
    def blocks(core_parity):
        value = jnp.where(core == core_parity, sums_mine, sums_others)
        return value.reshape(3, -1, 1, part)

    sums_proj = jnp.concatenate([blocks(0), blocks(1)], axis=2).reshape(3, model_width)
    small = (
        jnp.concatenate([sums_proj[0], sums_proj[2]]),
        sums_one[2],
        sums_one[0],
        sums_one[1],
        sums_in[0],
        sums_two[2],
        sums_two[0],
        sums_two[1],
    )
    small = jnp.concatenate([v.reshape(group, -1) for v in small], axis=1)
    grad_input = input_back(
        where, after(mine, sent), others, grad_first, w_qkv, parts_one, group
    )
    done = inward.finish(grad_input)
    sent = first.send_rest(done)
    small = jnp.concatenate([small, small], axis=0)
    small = lax.dynamic_slice_in_dim(small, own, group, axis=0)
    extra = -(-small.shape[1] // (16 * part)) * 16
    padded = jnp.pad(small, ((0, 0), (0, extra * part - small.shape[1])))
    padded = padded.reshape(group, extra, part).astype(BF16)
    done = first.finish(sent, extra=padded)
    gather_down = Gather(after(down.total().astype(BF16)[None], done))
    gather_down.step()
    gather_down.finish()
    (grad_wdown,) = widen(
        where, gather_down.parts, phases, [(True, part_rows, [(ff_rows, model_width)])]
    )
    shares = jnp.concatenate([inward.total(), first.total()], axis=0).astype(BF16)
    final = Gather(shares[None])
    final.step(grad_wdown)
    final.finish()
    grad_win, grad_wqkv, grad_wout, total = widen(
        where,
        final.parts,
        phases,
        [
            (False, rows, [(rows, ff_width)]),
            (False, rows, [(rows, qkv_width), (rows, model_width)]),
        ],
        extra,
    )
    total = total.reshape(-1)

    vecs, start = [], 0
    for size in sizes:
        vecs.append(total[start : start + size])
        start += size

    return (
        output_rows.reshape(tokens.shape),
        grad_input.reshape(tokens.shape),
        grad_wqkv,
        vecs[0],
        grad_wout,
        vecs[1],
        vecs[2],
        vecs[3],
        grad_win,
        vecs[4],
        grad_wdown,
        vecs[5],
        vecs[6],
        vecs[7],
    )


def solution(mesh):
    reps, group = mesh.devices.shape
    fine = Mesh(mesh.devices.reshape(reps // 2, 2, group), ALL)
    rows = P(ALL, None, None)
    matrix = P("shard", None)
    vector = P("shard")
    in_specs = (
        rows,
        P(ALL, None),
        P(ALL),
        rows,
        matrix,
        vector,
        matrix,
        vector,
        vector,
        vector,
        matrix,
        vector,
        matrix,
        vector,
        vector,
        vector,
    )
    out_specs = (
        rows,
        rows,
        matrix,
        vector,
        matrix,
        vector,
        vector,
        vector,
        matrix,
        vector,
        matrix,
        vector,
        vector,
        vector,
    )
    return jax.shard_map(
        partial(local, reps // 2, group),
        mesh=fine,
        in_specs=in_specs,
        out_specs=out_specs,
        check_vma=False,
    )
```

```python
from functools import partial

import jax
import jax.numpy as jnp
from jax import lax
from jax.experimental import pallas as pl
from jax.experimental.pallas import tpu as pltpu
from jax.sharding import Mesh
from jax.sharding import PartitionSpec as P

HEAD_DIM = 64
REP = ("chip", "core")
ALL = ("chip", "core", "shard")
F32 = jnp.float32
BF16 = jnp.bfloat16
MIB = 1024 * 1024
HINT = 3690000


def dot(left, right):
    return jnp.dot(left, right, preferred_element_type=F32)


def dot_t(left, right):
    return lax.dot_general(left, right, (((1,), (1,)), ((), ())), preferred_element_type=F32)


def t_dot(left, right):
    return lax.dot_general(left, right, (((0,), (0,)), ((), ())), preferred_element_type=F32)


def call(body, grid, ins, outs, out_shape, scratch=(), micros=1, limit=63, aliases=None):
    return pl.pallas_call(
        body,
        grid_spec=pltpu.PrefetchScalarGridSpec(
            num_scalar_prefetch=1,
            grid=grid,
            in_specs=ins,
            out_specs=outs,
            scratch_shapes=list(scratch),
        ),
        out_shape=out_shape,
        compiler_params=pltpu.CompilerParams(
            dimension_semantics=("arbitrary",) * len(grid), vmem_limit_bytes=limit * MIB
        ),
        input_output_aliases=aliases or {},
        cost_estimate=pl.CostEstimate(
            flops=0, bytes_accessed=int(micros * HINT), transcendentals=0
        ),
    )


def spec(shape, index):
    return pl.BlockSpec(shape, index)


def fixed(shape):
    zeros = (0,) * len(shape)
    return pl.BlockSpec(shape, lambda *_: zeros)


def struct(shape, dtype):
    return jax.ShapeDtypeStruct(shape, dtype)


def natural(where, step, group):
    return lax.rem(where[0] + step, group)


def block_of(where, unit, chips):
    return 2 * where[2 + unit] + jnp.where(unit < chips, where[1], 1 - where[1])


ANYWHERE = pl.BlockSpec(memory_space=pl.ANY)


def stream(unit, parts, buffer, sems):
    half = parts[0].shape[0]

    def start(number, slot):
        for index, part in enumerate(parts):

            @pl.when(number // half == index)
            def _(part=part):
                source = part.at[lax.rem(number, half)]
                pltpu.make_async_copy(source, buffer.at[slot], sems.at[slot]).start()

    slot = lax.rem(unit, 2)

    @pl.when(unit == 0)
    def _():
        start(unit, slot)

    @pl.when(unit + 1 < half * len(parts))
    def _():
        start(unit + 1, 1 - slot)

    pltpu.make_async_copy(parts[0].at[0], buffer.at[slot], sems.at[slot]).wait()
    return buffer[slot].reshape(-1, buffer.shape[3])


def stream_scratch(parts):
    return [pltpu.VMEM((2, *parts[0].shape[1:]), BF16), pltpu.SemaphoreType.DMA((2,))]


def stream_whole(step, parts, buffer, sems):
    for index, part in enumerate(parts):

        @pl.when(step == index)
        def _(index=index, part=part):
            slot = index % 2
            pltpu.make_async_copy(part, buffer.at[slot], sems.at[slot]).start()

        @pl.when(step == index + 1)
        def _(index=index, part=part):
            slot = index % 2
            pltpu.make_async_copy(part, buffer.at[slot], sems.at[slot]).wait()


def whole_scratch(parts):
    return [pltpu.VMEM((2, *parts[0].shape), BF16), pltpu.SemaphoreType.DMA((2,))]


def normalise(hidden):
    average = jnp.mean(hidden, axis=-1, keepdims=True)
    centred = hidden - average
    variance = jnp.mean(centred * centred, axis=-1, keepdims=True)
    inverse = lax.rsqrt(variance + 1e-06)
    return centred * inverse, inverse


def normalise_back(grad, unit, inverse, gain):
    scaled = grad * gain
    first = jnp.mean(scaled, axis=-1, keepdims=True)
    second = jnp.mean(scaled * unit, axis=-1, keepdims=True)
    return inverse * (scaled - first - unit * second)


def rows_sum(value):
    return jnp.sum(value, axis=0, keepdims=True)


def roll_into(rolled, x, where, rows, group):
    for s in range(group):
        start = pl.multiple_of(natural(where, s, group) * rows, 128)
        rolled[:, s * rows : (s + 1) * rows] = x[:, pl.ds(start, rows)]


def qkv_kernel(dims, where, x, own, a, b, c, d, bias, out, rest_out, rolled, *scratch):
    group, half, qkv_width = dims
    unit = pl.program_id(0)
    rows, columns = own.shape

    @pl.when(unit == 0)
    def _():
        roll_into(rolled, x, where, rows, group)

    rest = stream(unit, (a, b, c, d), *scratch)
    start = block_of(where, unit, 2 * half) * columns

    @pl.when(start < qkv_width)
    def _():
        total = dot(rolled[:, :rows], own[...]) + dot(rolled[:, rows:], rest)
        out[...] = (total + bias[...]).astype(BF16)

    @pl.when(start >= qkv_width)
    def _():
        place = pl.ds(pl.multiple_of(start - qkv_width, 128), columns)
        rest_out[:, place] = rest


def qkv(where, x, w_qkv, parts, bias, group):
    seq, width = x.shape
    rows, qkv_width = w_qkv.shape
    half, _, _, block = parts[0].shape
    chips = 2 * half
    total = 2 * chips * block
    top = qkv_width // block - 1
    return call(
        partial(qkv_kernel, (group, half, qkv_width)),
        (2 * chips,),
        [
            fixed((seq, width)),
            spec((rows, block), lambda u, w: (0, jnp.minimum(block_of(w, u, chips), top))),
        ]
        + [ANYWHERE] * 4
        + [spec((1, block), lambda u, w: (0, block_of(w, u, chips)))],
        [
            spec((seq, block), lambda u, w: (0, block_of(w, u, chips))),
            fixed((width - rows, total - qkv_width)),
        ],
        [struct((seq, total), BF16), struct((width - rows, total - qkv_width), BF16)],
        [pltpu.VMEM((seq, width), BF16)] + stream_scratch(parts),
        micros=12,
    )(where, x, w_qkv, *parts, bias)


def attend_kernel(first, where, q, k, v, x, column, row, *refs):
    out, turned, log_totals, bias = refs[-4:]
    step = pl.program_id(0)
    turned[0] = x[...].T

    @pl.when(step == 0)
    def _():
        bias[...] = jnp.where(column[...] == row[...], 0.0, -1e30)
        log_totals[...] = jnp.zeros_like(log_totals)

    lanes = lax.broadcasted_iota(jnp.int32, (1, 128), 1)
    heads = q.shape[1] // HEAD_DIM
    for h in range(heads):
        part = slice(h * HEAD_DIM, (h + 1) * HEAD_DIM)
        scores = dot_t(q[:, part] * BF16(HEAD_DIM**-0.5), k[:, part]) + bias[...]
        maxima = jnp.max(scores, axis=1, keepdims=True)
        expo = jnp.exp(scores - maxima)
        totals = jnp.sum(expo, axis=1, keepdims=True)
        probs = (expo * (1.0 / totals)).astype(BF16)
        out[:, part] = dot(probs, v[:, part]).astype(BF16)
        log_totals[...] = jnp.where(
            lanes == (first + step) * heads + h, maxima + jnp.log(totals), log_totals[...]
        )
    turned[1] = out[...].T


def attention(where, projected, x, column, row, first, count, before=()):
    seq, width = x.shape
    block = 2 * HEAD_DIM
    each = width // block
    anywhere = pl.BlockSpec(memory_space=pl.ANY)
    return call(
        partial(attend_kernel, first),
        (count,),
        [
            spec((seq, block), lambda h, w: (0, first + h)),
            spec((seq, block), lambda h, w: (0, each + first + h)),
            spec((seq, block), lambda h, w: (0, 2 * each + first + h)),
            spec((seq, block), lambda h, w: (0, first + h)),
            fixed((seq, 1)),
            fixed((1, seq)),
        ]
        + [anywhere] * len(before),
        [
            spec((seq, block), lambda h, w: (0, first + h)),
            spec((2, block, seq), lambda h, w: (0, first + h, 0)),
            fixed((seq, 128)),
        ],
        [
            struct((seq, width), BF16),
            struct((2, width, seq), BF16),
            struct((seq, 128), F32),
        ],
        [pltpu.VMEM((seq, seq), F32)],
        micros=11,
        aliases={7: 0, 8: 1} if before else None,
    )(where, projected, projected, projected, x, column, row, *before)


def attend_back_kernel(dims, where, q, k, v, grad, logs_a, logs_b, attn, column, row, *refs):
    out, sums, bias = refs
    mine, per = dims
    step = pl.program_id(0)
    pair = pair_of(where, step, mine, per)
    out[3] = attn[...]

    @pl.when(step == 0)
    def _():
        bias[...] = jnp.where(column[...] == row[...], 0.0, -1e30)

    lanes = lax.broadcasted_iota(jnp.int32, (1, 128), 1)
    heads = q.shape[1] // HEAD_DIM
    for h in range(heads):
        part = slice(h * HEAD_DIM, (h + 1) * HEAD_DIM)
        picked = jnp.where(lanes == pair * heads + h, logs_a[...] + logs_b[...], 0.0)
        logs = jnp.sum(picked, axis=1, keepdims=True)
        query = q[:, part] * BF16(HEAD_DIM**-0.5)
        scores = dot_t(query, k[:, part]) + bias[...]
        probs = jnp.exp(scores - logs)
        grad_probs = dot_t(grad[:, part], v[:, part])
        weighted = probs * grad_probs
        low = (weighted - probs * jnp.sum(weighted, axis=1, keepdims=True)).astype(BF16)
        grad_q = (dot(low, k[:, part]) * (HEAD_DIM**-0.5)).astype(BF16)
        grad_k = t_dot(low, query).astype(BF16)
        grad_v = t_dot(probs.astype(BF16), grad[:, part]).astype(BF16)
        for m, value in enumerate((grad_q, grad_k, grad_v)):
            out[m, :, part] = value
            sums[m, :, part] = rows_sum(value.astype(F32))


def pair_of(where, step, mine, per):
    parity = where[1] if mine else 1 - where[1]
    return (2 * (step // per) + parity) * per + lax.rem(step, per)


def attention_back(where, projected, grad, logs, attn, column, row, mine, part):
    seq, width = grad.shape
    block = 2 * HEAD_DIM
    each = width // block
    per = part // block

    def pairs(first):
        return spec((seq, block), lambda h, w: (0, first + pair_of(w, h, mine, per)))

    return call(
        partial(attend_back_kernel, (mine, per)),
        (each // 2,),
        [
            pairs(0),
            pairs(each),
            pairs(2 * each),
            pairs(0),
            fixed((seq, 128)),
            fixed((seq, 128)),
            pairs(0),
            fixed((seq, 1)),
            fixed((1, seq)),
        ],
        [
            spec((4, seq, block), lambda h, w: (0, 0, h)),
            spec((3, 1, block), lambda h, w: (0, 0, h)),
        ],
        [struct((4, seq, width // 2), BF16), struct((3, 1, width // 2), F32)],
        [pltpu.VMEM((seq, seq), F32)],
        micros=13,
    )(where, projected, projected, projected, grad, *logs, attn, column, row)


def out_kernel(group, where, context, x, own, rest, bias, gain, shift, hidden, low, turned):
    rows = own.shape[0]
    total = bias[...] + x[...].astype(F32)
    for s in range(group):
        start = pl.multiple_of(natural(where, s, group) * rows, 128)
        weight = own[...] if s == 0 else rest[(s - 1) * rows : s * rows, :]
        total = total + dot(context[:, pl.ds(start, rows)], weight)
    hidden[...] = total
    unit, _ = normalise(total)
    value = (unit * gain[...] + shift[...]).astype(BF16)
    low[...] = value
    turned[...] = value.T


def out_norm(where, context, x, w_out, rest_out, bias, gain, shift, group):
    seq, width = x.shape
    rows = w_out.shape[0]
    block = seq // 2
    vector = fixed((1, width))
    return call(
        partial(out_kernel, group),
        (seq // block,),
        [
            spec((block, width), lambda i, w: (i, 0)),
            spec((block, width), lambda i, w: (i, 0)),
            fixed((rows, width)),
            fixed((width - rows, width)),
            vector,
            vector,
            vector,
        ],
        [spec((block, width), lambda i, w: (i, 0))] * 2
        + [spec((width, block), lambda i, w: (0, i))],
        [
            struct((seq, width), F32),
            struct((seq, width), BF16),
            struct((width, seq), BF16),
        ],
        micros=6,
    )(where, context, x, w_out, rest_out, bias, gain, shift)


def inner_kernel(dims, where, x, own, a, b, c, d, bias, act, early, late, slope, rolled, *scratch):
    group, half = dims
    unit = pl.program_id(0)

    @pl.when(unit == 0)
    def _():
        roll_into(rolled, x, where, own.shape[0], group)

    rest = stream(unit, (a, b, c, d), *scratch)
    rows = own.shape[0]
    total = dot(rolled[:, :rows], own[...]) + dot(rolled[:, rows:], rest) + bias[...]
    below = 0.5 + 0.5 * lax.erf(total * (0.5**0.5))
    value = (total * below).astype(BF16)
    act[...] = value
    half_seq = early.shape[1]
    early[...] = value[:half_seq].T
    late[...] = value[half_seq:].T
    density = jnp.exp(-0.5 * total * total) * ((2.0 * jnp.pi) ** -0.5)
    slope[...] = (below + total * density).astype(BF16)


def inner(where, x, w_in, parts, bias, group):
    seq, width = x.shape
    rows, columns = w_in.shape
    half, _, _, block = parts[0].shape
    chips = 2 * half

    def columns_at(height):
        return spec((height, block), lambda u, w: (0, block_of(w, u, chips)))

    return call(
        partial(inner_kernel, (group, half)),
        (2 * chips,),
        [fixed((seq, width)), columns_at(rows)] + [ANYWHERE] * 4 + [columns_at(1)],
        [
            columns_at(seq),
            spec((block, seq // 2), lambda u, w: (block_of(w, u, chips), 0)),
            spec((block, seq // 2), lambda u, w: (block_of(w, u, chips), 0)),
            columns_at(seq),
        ],
        [
            struct((seq, columns), BF16),
            struct((columns, seq // 2), BF16),
            struct((columns, seq // 2), BF16),
            struct((seq, columns), BF16),
        ],
        [pltpu.VMEM((seq, width), BF16)] + stream_scratch(parts),
        micros=16,
    )(where, x, w_in, *parts, bias)


def outer_kernel(
    dims,
    where,
    act,
    own,
    a,
    b,
    c,
    d,
    hidden,
    cotangent,
    gain_one,
    shift_one,
    bias,
    gain_two,
    shift_two,
    out,
    grad,
    low,
    low_other,
    sums,
    total,
    picked,
    kept,
    given_rows,
    kept_sems,
    *scratch,
):
    group, half = dims
    step = pl.program_id(0)
    ff_rows = own.shape[0]
    rows = a.shape[2]
    late = [
        pltpu.make_async_copy(hidden, kept, kept_sems.at[0]),
        pltpu.make_async_copy(cotangent, given_rows, kept_sems.at[1]),
    ]
    stream_whole(step, (a, b, c, d), *scratch)

    @pl.when(step == 1)
    def _():
        for copy in late:
            copy.start()

    @pl.when(step == 0)
    def _():
        start = pl.multiple_of(where[0] * ff_rows, 128)
        total[...] = dot(act[:, pl.ds(start, ff_rows)], own[...])

    @pl.when(step > 0)
    def _():
        at = 0
        for i in range(half):
            block = block_of(where, (step - 1) * half + i, 2 * half)
            for s in range(1, group):
                start = natural(where, s, group) * ff_rows + block * rows
                picked[:, at : at + rows] = act[:, pl.ds(pl.multiple_of(start, rows), rows)]
                at += rows
        rest = scratch[0][lax.rem(step - 1, 2)].reshape(-1, a.shape[3])
        total[...] += dot(picked[...], rest)

    @pl.when(step == 4)
    def _():
        for copy in late:
            copy.wait()
        unit_one, _ = normalise(kept[...])
        second = unit_one * gain_one[...] + shift_one[...] + total[...] + bias[...]
        unit, inverse = normalise(second)
        out[...] = (unit * gain_two[...] + shift_two[...]).astype(BF16)
        given = given_rows[...].astype(F32)
        back = normalise_back(given, unit, inverse, gain_two[...])
        grad[...] = back
        rounded = back.astype(BF16)
        low[...] = rounded
        size = low_other.shape[1]
        start = pl.multiple_of((1 - where[1]) * size, 128)
        low_other[...] = low[:, pl.ds(start, size)]
        sums[0:1, :] = rows_sum(given * unit)
        sums[1:2, :] = rows_sum(given)
        sums[2:3, :] = rows_sum(rounded.astype(F32))


def outer(where, act, w_down, parts, hidden, cotangent, vectors, group):
    seq, width = hidden.shape
    rows = w_down.shape[0]
    half, steps, size, _ = parts[0].shape
    full = fixed((seq, width))
    vector = fixed((1, width))
    return call(
        partial(outer_kernel, (group, half)),
        (5,),
        [fixed(act.shape), fixed((rows, width))]
        + [ANYWHERE] * 6
        + [vector] * 5,
        [full, full, full, fixed((seq, width // 2)), fixed((8, width))],
        [
            struct((seq, width), BF16),
            struct((seq, width), F32),
            struct((seq, width), BF16),
            struct((seq, width // 2), BF16),
            struct((8, width), F32),
        ],
        [
            pltpu.VMEM((seq, width), F32),
            pltpu.VMEM((seq, half * steps * size), BF16),
            pltpu.VMEM((seq, width), F32),
            pltpu.VMEM((seq, width), BF16),
            pltpu.SemaphoreType.DMA((2,)),
        ]
        + whole_scratch(parts),
        micros=60,
    )(where, act, w_down, *parts, hidden, cotangent, *vectors)


def slope_kernel(
    dims, where, low, own, a, b, c, d, given, grad, grad_other, sums, slope, slope_sem, *scratch
):
    group, half, width = dims
    step = pl.program_id(0)
    ff_rows = own.shape[0]
    rows = a.shape[2]

    def finish(back, start, size):
        place = pl.ds(pl.multiple_of(start, size), size)
        value = (back * slope[:, place].astype(F32)).astype(BF16)
        grad[:, place] = value
        sums[:, place] = rows_sum(value.astype(F32))
        piece = min(size, width)
        for at in range(0, size, piece):
            block = (start + at) // width
            inside = start + at - block * width

            @pl.when(lax.rem(block, 2) != where[1])
            def _(at=at, block=block, inside=inside):
                there = pl.multiple_of((block // 2) * width + inside, piece)
                grad_other[:, pl.ds(there, piece)] = value[:, at : at + piece]

    slopes = pltpu.make_async_copy(given, slope, slope_sem)
    stream_whole(step, (a, b, c, d), *scratch)

    @pl.when(step == 0)
    def _():
        slopes.start()
        back = dot_t(low[...], own[...])
        slopes.wait()
        finish(back, where[0] * ff_rows, ff_rows)

    @pl.when(step > 0)
    def _():
        rest = scratch[0][lax.rem(step - 1, 2)].reshape(-1, a.shape[3])
        back = dot_t(low[...], rest)
        at = 0
        for i in range(half):
            block = block_of(where, (step - 1) * half + i, 2 * half)
            for s in range(1, group):
                start = natural(where, s, group) * ff_rows + block * rows
                finish(back[:, at : at + rows], start, rows)
                at += rows


def slope_back(where, low, w_down, parts, slope, part, group):
    seq, width = low.shape
    rows = w_down.shape[0]
    half = parts[0].shape[0]
    columns = slope.shape[1]
    return call(
        partial(slope_kernel, (group, half, part)),
        (5,),
        [fixed((seq, width)), fixed((rows, width))]
        + [ANYWHERE] * 5,
        [fixed((seq, columns)), fixed((seq, columns // 2)), fixed((1, columns))],
        [
            struct((seq, columns), BF16),
            struct((seq, columns // 2), BF16),
            struct((1, columns), F32),
        ],
        [pltpu.VMEM((seq, columns), BF16), pltpu.SemaphoreType.DMA(())] + whole_scratch(parts),
        micros=14,
    )(where, low, w_down, *parts, slope)


def inner_back_kernel(
    dims,
    where,
    grad_inner,
    own,
    a,
    b,
    c,
    d,
    grad_two,
    hidden,
    gain,
    own_out,
    rest_out,
    grad_one,
    low_one,
    grad_context,
    sums,
    total,
    *scratch,
):
    group, half = dims
    unit = pl.program_id(0)
    rows = own.shape[0]

    def place(s):
        return pl.ds(pl.multiple_of(natural(where, s, group) * rows, 128), rows)

    @pl.when(unit == 0)
    def _():
        total[...] = jnp.zeros_like(total)

    rest = stream(unit, (a, b, c, d), *scratch)
    total[:, :rows] += dot_t(grad_inner[...], own[...])
    total[:, rows:] += dot_t(grad_inner[...], rest)

    @pl.when(unit == 4 * half - 1)
    def _():
        unit_one, inverse = normalise(hidden[...])
        for s in range(group):
            grad_one[:, place(s)] = total[:, s * rows : (s + 1) * rows]
        given = grad_one[...] + grad_two[...]
        back = normalise_back(given, unit_one, inverse, gain[...])
        grad_one[...] = back
        rounded = back.astype(BF16)
        low_one[...] = rounded
        sums[0:1, :] = rows_sum(given * unit_one)
        sums[1:2, :] = rows_sum(given)
        sums[2:3, :] = rows_sum(rounded.astype(F32))
        grad_context[:, place(0)] = dot_t(rounded, own_out[...]).astype(BF16)
        for s in range(1, group):
            piece = rest_out[(s - 1) * rows : s * rows, :]
            grad_context[:, place(s)] = dot_t(rounded, piece).astype(BF16)


def inner_back(where, grad_inner, w_in, parts, grad_two, hidden, gain, w_out, rest_out, group):
    seq, width = hidden.shape
    rows, columns = w_in.shape
    half, _, _, block = parts[0].shape
    chips = 2 * half
    full = fixed((seq, width))

    def columns_at(height):
        return spec((height, block), lambda u, w: (0, block_of(w, u, chips)))

    return call(
        partial(inner_back_kernel, (group, half)),
        (2 * chips,),
        [columns_at(seq), columns_at(rows)]
        + [ANYWHERE] * 4
        + [full, full, fixed((1, width)), fixed((rows, width)), fixed((width - rows, width))],
        [full, full, full, fixed((8, width))],
        [
            struct((seq, width), F32),
            struct((seq, width), BF16),
            struct((seq, width), BF16),
            struct((8, width), F32),
        ],
        [pltpu.VMEM((seq, width), F32)] + stream_scratch(parts),
        micros=19,
    )(where, grad_inner, w_in, *parts, grad_two, hidden, gain, w_out, rest_out)


def input_back_kernel(dims, where, mine, others, own, a, b, c, d, first, out, total, *scratch):
    group, half, qkv_width = dims
    unit = pl.program_id(0)
    rows, columns = own.shape

    @pl.when(unit == 0)
    def _():
        total[...] = jnp.zeros_like(total)

    rest = stream(unit, (a, b, c, d), *scratch)
    block = block_of(where, unit, 2 * half)
    inside = block * columns < qkv_width
    same = lax.rem(block, 2) == where[1]

    @pl.when(inside)
    def _():
        grad = jnp.where(same, mine[0], others[0])
        total[:, :rows] += dot_t(grad, own[...])
        total[:, rows:] += dot_t(grad, rest)

    @pl.when(unit == 4 * half - 1)
    def _():
        for s in range(group):
            place = pl.ds(pl.multiple_of(natural(where, s, group) * rows, 128), rows)
            out[:, place] = first[:, place] + total[:, s * rows : (s + 1) * rows]


def input_back(where, mine, others, first, w_qkv, parts, group):
    seq, width = first.shape
    rows, qkv_width = w_qkv.shape
    half, _, _, block = parts[0].shape
    chips = 2 * half
    each = width // block
    top = qkv_width // block - 1

    def plane(u, w):
        n = jnp.minimum(block_of(w, u, chips), top)
        return (n // each, 0, lax.rem(n, each) // 2)

    return call(
        partial(input_back_kernel, (group, half, qkv_width)),
        (2 * chips,),
        [
            spec((1, seq, block), plane),
            spec((1, seq, block), plane),
            spec((rows, block), lambda u, w: (0, jnp.minimum(block_of(w, u, chips), top))),
        ]
        + [ANYWHERE] * 4
        + [fixed((seq, width))],
        fixed((seq, width)),
        struct((seq, width), F32),
        [pltpu.VMEM((seq, width), F32)] + stream_scratch(parts),
        micros=12,
    )(where, mine, others, w_qkv, *parts, first)


def widen_kernel(dims, where, *refs):
    parts, outs = refs[:4], refs[4:]
    phases, kinds, more = dims
    chips = 1 << phases
    half = chips // 2
    if more:
        outs, extra = outs[:-1], outs[-1]
        extra[...] = jnp.zeros_like(extra)
    for side in range(2):
        core = where[1] if side == 0 else 1 - where[1]
        for order in range(chips):
            chip = where[2 + side * chips + order]
            given = parts[2 * side + order // half].at[order % half]
            at, row = 0, 0
            for by_rows, rows, count in kinds:
                targets, at = outs[at : at + count], at + count
                columns = given.shape[1]
                step = min(rows, 128)

                @pl.loop(0, rows // step)
                def _(index, row=row, rows=rows, step=step, targets=targets, by_rows=by_rows):
                    inside = pl.multiple_of(index * step, step)
                    value = given[pl.ds(row + inside, step), :].astype(F32)
                    if by_rows:
                        down = pl.ds(pl.multiple_of(chip * rows + inside, step), step)
                        across = pl.ds(pl.multiple_of(core * columns, 128), columns)
                        targets[0][down, across] = value
                        return
                    base = 0
                    for out in targets:
                        first = (2 * chip + core) * columns - base

                        @pl.when((first >= 0) & (first < out.shape[1]))
                        def _(out=out, first=first):
                            across = pl.ds(pl.multiple_of(first, 128), columns)
                            out[pl.ds(inside, step), across] = value

                        base += out.shape[1]

                row += rows
            if more:
                extra[...] += given[row:, :].astype(F32)


def widen(where, parts, phases, kinds, more=0):
    shapes = [shape for *_, given in kinds for shape in given]
    if more:
        shapes.append((more, parts[0].shape[2]))
    short = [(by_rows, rows, len(given)) for by_rows, rows, given in kinds]
    return call(
        partial(widen_kernel, (phases, short, more)),
        (1,),
        [fixed(part.shape) for part in parts],
        [fixed(shape) for shape in shapes],
        [struct(shape, F32) for shape in shapes],
        micros=4,
    )(where, *parts)


def grads_kernel(dims, where, *refs):
    orders, adds, last, group, cuts, extra = dims
    units = len(orders)
    step = pl.program_id(0)
    at = 0
    outs = refs[units * (2 + 2 * cuts + adds) + extra :]
    for u in range(units):
        right, right_other = refs[at : at + 2]
        at += 2
        value = 0.0
        for given in (right, right_other):
            size = given.shape[1] // cuts
            for i in range(cuts):
                value = value + dot(refs[at][0], given[0, i * size : (i + 1) * size, :])
                at += 1
        for add in refs[at : at + adds]:
            value = value + add[0].astype(F32)
        at += adds
        value = value.astype(BF16)
        if not last:
            outs[0][u] = value
            continue
        for s in range(group):

            @pl.when(step == s)
            def _(s=s, value=value):
                outs[s][: value.shape[0], :] = value
                if extra:
                    outs[s][value.shape[0] :, :] = refs[-group - 1][s]


def grads(where, left, right, maps, shape, units, received, group, extra=None):
    rows, columns = shape
    cuts = len(left[0])
    seq = left[0][0].shape[2]
    left_map, right_map, other_map = maps
    last = units == [0]
    ins, args = [], []
    for order in units:
        lefts = spec((1, rows, seq), partial(left_map, order))
        ins.append(spec((1, seq * cuts, columns), partial(right_map, order)))
        ins.append(spec((1, seq * cuts, columns), partial(other_map, order)))
        ins += [lefts] * (2 * cuts)
        args += [right[0], right[1], *left[0], *left[1]]
        for phase, value in enumerate(received):
            index = order >> (phase + 1)
            ins.append(spec((1, rows, columns), lambda s, w, index=index: (index, s, 0)))
            args.append(value)
    count = len(units)
    more = 0 if extra is None else extra.shape[1]
    if more:
        ins.append(fixed(extra.shape))
        args.append(extra)
    if last:
        outs = [fixed((rows + more, columns))] * group
        out_shape = [struct((rows + more, columns), BF16)] * group
    else:
        outs = [spec((count, rows, columns), lambda s, w: (0, s, 0))]
        out_shape = [struct((count, group * rows, columns), BF16)]
    return call(
        partial(grads_kernel, (units, len(received), last, group, cuts, int(more > 0))),
        (group,),
        ins,
        outs,
        out_shape,
        micros=6,
    )(where, *args)


def after(value, *others):
    return lax.optimization_barrier((value, others))[0]


def local(
    chips,
    group,
    tokens,
    segments,
    lengths,
    cotangent,
    w_qkv,
    b_qv,
    w_out,
    b_out,
    gain_one,
    shift_one,
    w_in,
    b_in,
    w_down,
    b_down,
    gain_two,
    shift_two,
):
    reps = 2 * chips
    phases = chips.bit_length() - 1
    core = lax.axis_index("core")
    chip = lax.axis_index("chip")
    rank = chip * 2 + core
    own = lax.axis_index("shard")
    _, seq_len, model_width = tokens.shape
    ff_rows = w_down.shape[0]
    ff_width = w_in.shape[1]
    qkv_width = w_qkv.shape[1]

    def from_shard(value, step):
        return lax.ppermute(value, "shard", [(i, (i - step) % group) for i in range(group)])

    def to_shard(value, step):
        return lax.ppermute(value, "shard", [(i, (i + step) % group) for i in range(group)])

    def sibling(value):
        return lax.ppermute(value, "core", [(0, 1), (1, 0)])

    def bit(phase, which):
        return 1 << ((phase + which) % phases)

    def swap(value, phase):
        pairs = [
            (q * 2 + c, (q ^ bit(phase, c)) * 2 + c) for q in range(chips) for c in range(2)
        ]
        return lax.ppermute(value, REP, pairs)

    def table(which):
        orders = []
        for order in range(chips):
            mask = sum(bit(f, which) for f in range(phases) if order >> f & 1)
            orders.append(mask)
        return orders

    masks = jnp.where(core == 0, jnp.array(table(0)), jnp.array(table(1)))
    masks_other = jnp.where(core == 0, jnp.array(table(1)), jnp.array(table(0)))
    where = jnp.concatenate(
        [jnp.stack([own, core]), chip ^ masks, chip ^ masks_other]
    ).astype(jnp.int32)

    def gather(value, *gates):
        for phase in range(phases - 1):
            value = jnp.concatenate([value, swap(value, phase)], axis=0)
        rest = swap(value, phases - 1)
        return value, rest, sibling(after(value, gates)), sibling(rest)

    w_one = jnp.concatenate([w_qkv, w_out], axis=1)
    part = w_one.shape[1] // reps
    rows = w_one.shape[0]
    piece_one = lax.dynamic_slice_in_dim(w_one, rank * part, part, axis=1)
    part_in = ff_width // reps
    piece_in = lax.dynamic_slice_in_dim(w_in, rank * part_in, part_in, axis=1)
    part_down = ff_rows // reps
    piece_down = lax.dynamic_slice_in_dim(w_down, rank * part_down, part_down, axis=0)

    class Gather:

        def __init__(self, value):
            self.value = value
            self.first = swap(value, 0)

        def step(self, *gates):
            other = self.first
            for phase in range(phases - 1):
                self.value = after(jnp.concatenate([self.value, other], axis=0), gates)
                other = swap(self.value, phase + 1)
            self.rest = other
            self.side = sibling(self.value)

        def finish(self, *gates):
            self.parts = (self.value, self.rest, self.side, sibling(after(self.rest, gates)))

    got_one = [from_shard(piece_one, s) for s in range(1, group)]

    vectors = (b_qv, b_out, gain_one, shift_one, b_in, b_down, gain_two, shift_two)
    sizes = [v.shape[0] for v in vectors]
    packed = jnp.concatenate(after(vectors, piece_one))
    first_parts = Gather(jnp.stack(got_one)[None])
    first_parts.step()
    packed = after(packed, got_one)
    got_packed = [from_shard(packed, s) for s in range(1, group)]
    first_parts.finish(got_packed)
    parts_one = first_parts.parts
    piece_in = after(piece_in, parts_one[3])
    got_in = [from_shard(piece_in, s) for s in range(1, group)]
    piece_down = after(piece_down, parts_one[3])

    relative = jnp.stack([packed] + got_packed)
    ordered = jnp.concatenate([relative, relative], axis=0)
    ordered = lax.dynamic_slice_in_dim(ordered, (group - own) % group, group, axis=0)
    full, start = [], 0
    for size in sizes:
        full.append(ordered[:, start : start + size].reshape(1, -1).astype(F32))
        start += size
    bias_qv, bias_out, norm_gone, norm_sone, bias_in, bias_down, norm_gtwo, norm_stwo = full
    none = jnp.zeros((1, model_width), F32)
    bias_qkv = jnp.concatenate(
        [bias_qv[:, :model_width], none, bias_qv[:, model_width:], none], axis=1
    )
    kind = segments[0] * 2 + (jnp.arange(seq_len) < lengths[0]).astype(jnp.int32)
    column, row = kind[:, None], kind[None, :]

    flat_in = tokens[0]
    projected, rest_out = qkv(where, flat_in, w_qkv, parts_one, bias_qkv, group)
    parts_in = Gather(after(jnp.stack(got_in)[None], projected))
    got_down = [from_shard(piece_down, s) for s in range(1, group)]
    count = model_width // (4 * HEAD_DIM)
    context, turned, logs_a = attention(where, projected, flat_in, column, row, 0, count)
    parts_in.step(logs_a)
    context, turned, logs_b = attention(
        where,
        projected,
        flat_in,
        column,
        row,
        count,
        count,
        (context, turned),
    )
    first_left = ([turned], [sibling(turned)])
    parts_down = Gather(after(jnp.stack(got_down)[None], logs_b))
    parts_down.step(logs_b)
    hidden, normed, normed_turned = out_norm(
        where,
        context,
        flat_in,
        w_out,
        rest_out,
        bias_out,
        norm_gone,
        norm_sone,
        group,
    )
    parts_in.finish(hidden)
    parts_in = parts_in.parts
    in_left = ([normed_turned[None]], [sibling(normed_turned)[None]])
    where_down = where
    normed = after(normed, parts_down.first)
    act, *act_turned, slope = inner(where, normed, w_in, parts_in, bias_in, group)
    parts_down.finish(act)
    parts_down = parts_down.parts
    if part_down % 128:
        merged = jnp.zeros((group - 1, ff_rows, model_width), BF16)
        for unit in range(reps):
            piece = parts_down[2 * unit // chips][unit % (chips // 2)]
            at = block_of(where, unit, chips) * part_down
            merged = lax.dynamic_update_slice_in_dim(merged, piece, at, axis=1)
        fourth = ff_rows // 4
        parts_down = [merged[:, b * fourth : (b + 1) * fourth][None] for b in (0, 2, 1, 3)]
        where_down = jnp.stack([own, 0, 0, 1, 0, 1]).astype(jnp.int32)
    down_left = ([v[None] for v in act_turned], [sibling(v)[None] for v in act_turned])
    output_rows, grad_second, grad_branch, branch_other, sums_two = outer(
        where_down,
        act,
        w_down,
        parts_down,
        hidden,
        cotangent[0],
        (norm_gone, norm_sone, bias_down, norm_gtwo, norm_stwo),
        group,
    )

    class Scatter:

        def __init__(self, left, right, maps, shape):
            self.fixed = (where, left, right, maps, shape)
            self.received = []

        def send(self, *gates):
            phase = len(self.received)
            units = list(range(1 << phase, chips, 2 << phase))
            received = after(self.received, gates) if phase else []
            sent = grads(*self.fixed, units, received, group)[0]
            self.received.append(swap(sent, phase))
            return sent

        def send_rest(self, *gates):
            while len(self.received) < phases:
                sent = self.send(*gates)
            return sent

        def finish(self, *gates, extra=None):
            received = after(self.received, gates)
            parts = grads(*self.fixed, [0], received, group, extra)
            self.own = parts[0]
            self.given = [to_shard(parts[s], s) for s in range(1, group)]
            return parts[0]

        def total(self):
            total = self.own.astype(F32)
            for value in self.given:
                total = total + value.astype(F32)
            return total

    half = model_width // 2
    part_rows = ff_rows // chips
    down_maps = (
        lambda o, s, w: (0, natural(w, s, group) * chips + w[2 + o], 0),
        lambda o, s, w: (0, 0, w[1]),
        lambda o, s, w: (0, 0, 0),
    )
    down_right = (grad_branch[None], sibling(branch_other)[None])
    down = Scatter(down_left, down_right, down_maps, (part_rows, half))
    sent = down.send()
    grad_inner, inner_other, sums_in = slope_back(
        where_down, after(grad_branch, sent), w_down, parts_down, slope, part_in, group
    )
    grad_first, grad_attn, grad_context, sums_one = inner_back(
        where,
        after(grad_inner, in_left),
        w_in,
        parts_in,
        grad_second,
        hidden,
        norm_gone,
        w_out,
        rest_out,
        group,
    )
    in_other = sibling(inner_other)
    sent = down.send_rest(grad_first, first_left)
    in_maps = (
        lambda o, s, w: (0, natural(w, s, group), 0),
        lambda o, s, w: (0, 0, 2 * w[2 + o] + w[1]),
        lambda o, s, w: (0, 0, w[2 + o]),
    )
    in_right = after((grad_inner[None], in_other[None]), sent)
    inward = Scatter(in_left, in_right, in_maps, (rows, part_in))
    sent = inward.send()
    logs = (logs_a, logs_b)
    others, sums_others = attention_back(
        where, projected, after(grad_context, sent), logs, grad_attn, column, row, False, part
    )
    done = down.finish(others)
    other_proj = sibling(after(others, done))
    mine, sums_mine = attention_back(
        where, projected, after(grad_context, done), logs, grad_attn, column, row, True, part
    )
    sent = inward.send_rest(mine)
    each = model_width // part

    def plane(order, w):
        return 2 * w[2 + order] + w[1]

    def compact(o, s, w):
        return (plane(o, w) // each, 0, lax.rem(plane(o, w), each) // 2)

    first_maps = (
        lambda o, s, w: (plane(o, w) // (3 * each), natural(w, s, group), 0),
        compact,
        compact,
    )
    first_right = after((mine, other_proj), sent, down.given)
    first = Scatter(first_left, first_right, first_maps, (rows, part))
    sent = first.send()
    def blocks(core_parity):
        value = jnp.where(core == core_parity, sums_mine, sums_others)
        return value.reshape(3, -1, 1, part)

    sums_proj = jnp.concatenate([blocks(0), blocks(1)], axis=2).reshape(3, model_width)
    small = (
        jnp.concatenate([sums_proj[0], sums_proj[2]]),
        sums_one[2],
        sums_one[0],
        sums_one[1],
        sums_in[0],
        sums_two[2],
        sums_two[0],
        sums_two[1],
    )
    small = jnp.concatenate([v.reshape(group, -1) for v in small], axis=1)
    grad_input = input_back(
        where, after(mine, sent), others, grad_first, w_qkv, parts_one, group
    )
    done = inward.finish(grad_input)
    sent = first.send_rest(done)
    small = jnp.concatenate([small, small], axis=0)
    small = lax.dynamic_slice_in_dim(small, own, group, axis=0)
    extra = -(-small.shape[1] // (16 * part)) * 16
    padded = jnp.pad(small, ((0, 0), (0, extra * part - small.shape[1])))
    padded = padded.reshape(group, extra, part).astype(BF16)
    done = first.finish(sent, extra=padded)
    gather_down = Gather(after(down.total().astype(BF16)[None], done))
    gather_down.step()
    gather_down.finish()
    (grad_wdown,) = widen(
        where, gather_down.parts, phases, [(True, part_rows, [(ff_rows, model_width)])]
    )
    shares = jnp.concatenate([inward.total(), first.total()], axis=0).astype(BF16)
    final = Gather(shares[None])
    final.step(grad_wdown)
    final.finish()
    grad_win, grad_wqkv, grad_wout, total = widen(
        where,
        final.parts,
        phases,
        [
            (False, rows, [(rows, ff_width)]),
            (False, rows, [(rows, qkv_width), (rows, model_width)]),
        ],
        extra,
    )
    total = total.reshape(-1)

    vecs, start = [], 0
    for size in sizes:
        vecs.append(total[start : start + size])
        start += size

    return (
        output_rows.reshape(tokens.shape),
        grad_input.reshape(tokens.shape),
        grad_wqkv,
        vecs[0],
        grad_wout,
        vecs[1],
        vecs[2],
        vecs[3],
        grad_win,
        vecs[4],
        grad_wdown,
        vecs[5],
        vecs[6],
        vecs[7],
    )


def solution(mesh):
    reps, group = mesh.devices.shape
    fine = Mesh(mesh.devices.reshape(reps // 2, 2, group), ALL)
    rows = P(ALL, None, None)
    matrix = P("shard", None)
    vector = P("shard")
    in_specs = (
        rows,
        P(ALL, None),
        P(ALL),
        rows,
        matrix,
        vector,
        matrix,
        vector,
        vector,
        vector,
        matrix,
        vector,
        matrix,
        vector,
        vector,
        vector,
    )
    out_specs = (
        rows,
        rows,
        matrix,
        vector,
        matrix,
        vector,
        vector,
        vector,
        matrix,
        vector,
        matrix,
        vector,
        vector,
        vector,
    )
    return jax.shard_map(
        partial(local, reps // 2, group),
        mesh=fine,
        in_specs=in_specs,
        out_specs=out_specs,
        check_vma=False,
    )
```

```python
from functools import partial

import jax
import jax.numpy as jnp
from jax import lax
from jax.experimental import pallas as pl
from jax.experimental.pallas import tpu as pltpu
from jax.sharding import Mesh
from jax.sharding import PartitionSpec as P

HEAD_DIM = 64
REP = ("chip", "core")
ALL = ("chip", "core", "shard")
F32 = jnp.float32
BF16 = jnp.bfloat16
MIB = 1024 * 1024
HINT = 3690000


def dot(left, right):
    return jnp.dot(left, right, preferred_element_type=F32)


def dot_t(left, right):
    return lax.dot_general(left, right, (((1,), (1,)), ((), ())), preferred_element_type=F32)


def t_dot(left, right):
    return lax.dot_general(left, right, (((0,), (0,)), ((), ())), preferred_element_type=F32)


def call(body, grid, ins, outs, out_shape, scratch=(), micros=1, limit=63, aliases=None):
    return pl.pallas_call(
        body,
        grid_spec=pltpu.PrefetchScalarGridSpec(
            num_scalar_prefetch=1,
            grid=grid,
            in_specs=ins,
            out_specs=outs,
            scratch_shapes=list(scratch),
        ),
        out_shape=out_shape,
        compiler_params=pltpu.CompilerParams(
            dimension_semantics=("arbitrary",) * len(grid), vmem_limit_bytes=limit * MIB
        ),
        input_output_aliases=aliases or {},
        cost_estimate=pl.CostEstimate(
            flops=0, bytes_accessed=int(micros * HINT), transcendentals=0
        ),
    )


def spec(shape, index):
    return pl.BlockSpec(shape, index)


def fixed(shape):
    zeros = (0,) * len(shape)
    return pl.BlockSpec(shape, lambda *_: zeros)


def struct(shape, dtype):
    return jax.ShapeDtypeStruct(shape, dtype)


def natural(where, step, group):
    return lax.rem(where[0] + step, group)


def block_of(where, unit, chips):
    return 2 * where[2 + unit] + jnp.where(unit < chips, where[1], 1 - where[1])


ANYWHERE = pl.BlockSpec(memory_space=pl.ANY)


def stream(unit, parts, buffer, sems):
    half = parts[0].shape[0]

    def start(number, slot):
        for index, part in enumerate(parts):

            @pl.when(number // half == index)
            def _(part=part):
                source = part.at[lax.rem(number, half)]
                pltpu.make_async_copy(source, buffer.at[slot], sems.at[slot]).start()

    slot = lax.rem(unit, 2)

    @pl.when(unit == 0)
    def _():
        start(unit, slot)

    @pl.when(unit + 1 < half * len(parts))
    def _():
        start(unit + 1, 1 - slot)

    pltpu.make_async_copy(parts[0].at[0], buffer.at[slot], sems.at[slot]).wait()
    return buffer[slot].reshape(-1, buffer.shape[3])


def stream_scratch(parts):
    return [pltpu.VMEM((2, *parts[0].shape[1:]), BF16), pltpu.SemaphoreType.DMA((2,))]


def stream_whole(step, parts, buffer, sems):
    for index, part in enumerate(parts):

        @pl.when(step == index)
        def _(index=index, part=part):
            slot = index % 2
            pltpu.make_async_copy(part, buffer.at[slot], sems.at[slot]).start()

        @pl.when(step == index + 1)
        def _(index=index, part=part):
            slot = index % 2
            pltpu.make_async_copy(part, buffer.at[slot], sems.at[slot]).wait()


def whole_scratch(parts):
    return [pltpu.VMEM((2, *parts[0].shape), BF16), pltpu.SemaphoreType.DMA((2,))]


def normalise(hidden):
    average = jnp.mean(hidden, axis=-1, keepdims=True)
    centred = hidden - average
    variance = jnp.mean(centred * centred, axis=-1, keepdims=True)
    inverse = lax.rsqrt(variance + 1e-06)
    return centred * inverse, inverse


def normalise_back(grad, unit, inverse, gain):
    scaled = grad * gain
    first = jnp.mean(scaled, axis=-1, keepdims=True)
    second = jnp.mean(scaled * unit, axis=-1, keepdims=True)
    return inverse * (scaled - first - unit * second)


def rows_sum(value):
    return jnp.sum(value, axis=0, keepdims=True)


def roll_into(rolled, x, where, rows, group):
    for s in range(group):
        start = pl.multiple_of(natural(where, s, group) * rows, 128)
        rolled[:, s * rows : (s + 1) * rows] = x[:, pl.ds(start, rows)]


def qkv_kernel(dims, where, x, own, a, b, c, d, bias, out, rest_out, rolled, *scratch):
    group, half, qkv_width = dims
    unit = pl.program_id(0)
    rows, columns = own.shape

    @pl.when(unit == 0)
    def _():
        roll_into(rolled, x, where, rows, group)

    rest = stream(unit, (a, b, c, d), *scratch)
    start = block_of(where, unit, 2 * half) * columns

    @pl.when(start < qkv_width)
    def _():
        total = dot(rolled[:, :rows], own[...]) + dot(rolled[:, rows:], rest)
        out[...] = (total + bias[...]).astype(BF16)

    @pl.when(start >= qkv_width)
    def _():
        place = pl.ds(pl.multiple_of(start - qkv_width, 128), columns)
        rest_out[:, place] = rest


def qkv(where, x, w_qkv, parts, bias, group):
    seq, width = x.shape
    rows, qkv_width = w_qkv.shape
    half, _, _, block = parts[0].shape
    chips = 2 * half
    total = 2 * chips * block
    top = qkv_width // block - 1
    return call(
        partial(qkv_kernel, (group, half, qkv_width)),
        (2 * chips,),
        [
            fixed((seq, width)),
            spec((rows, block), lambda u, w: (0, jnp.minimum(block_of(w, u, chips), top))),
        ]
        + [ANYWHERE] * 4
        + [spec((1, block), lambda u, w: (0, block_of(w, u, chips)))],
        [
            spec((seq, block), lambda u, w: (0, block_of(w, u, chips))),
            fixed((width - rows, total - qkv_width)),
        ],
        [struct((seq, total), BF16), struct((width - rows, total - qkv_width), BF16)],
        [pltpu.VMEM((seq, width), BF16)] + stream_scratch(parts),
        micros=12,
    )(where, x, w_qkv, *parts, bias)


def attend_kernel(first, where, q, k, v, x, column, row, *refs):
    out, turned, log_totals, bias = refs[-4:]
    step = pl.program_id(0)
    turned[0] = x[...].T

    @pl.when(step == 0)
    def _():
        bias[...] = jnp.where(column[...] == row[...], 0.0, -1e30)
        log_totals[...] = jnp.zeros_like(log_totals)

    lanes = lax.broadcasted_iota(jnp.int32, (1, 128), 1)
    heads = q.shape[1] // HEAD_DIM
    for h in range(heads):
        part = slice(h * HEAD_DIM, (h + 1) * HEAD_DIM)
        scores = dot_t(q[:, part] * BF16(HEAD_DIM**-0.5), k[:, part]) + bias[...]
        maxima = jnp.max(scores, axis=1, keepdims=True)
        expo = jnp.exp(scores - maxima)
        totals = jnp.sum(expo, axis=1, keepdims=True)
        probs = (expo * (1.0 / totals)).astype(BF16)
        out[:, part] = dot(probs, v[:, part]).astype(BF16)
        log_totals[...] = jnp.where(
            lanes == (first + step) * heads + h, maxima + jnp.log(totals), log_totals[...]
        )
    turned[1] = out[...].T


def attention(where, projected, x, column, row, first, count, before=()):
    seq, width = x.shape
    block = 2 * HEAD_DIM
    each = width // block
    anywhere = pl.BlockSpec(memory_space=pl.ANY)
    return call(
        partial(attend_kernel, first),
        (count,),
        [
            spec((seq, block), lambda h, w: (0, first + h)),
            spec((seq, block), lambda h, w: (0, each + first + h)),
            spec((seq, block), lambda h, w: (0, 2 * each + first + h)),
            spec((seq, block), lambda h, w: (0, first + h)),
            fixed((seq, 1)),
            fixed((1, seq)),
        ]
        + [anywhere] * len(before),
        [
            spec((seq, block), lambda h, w: (0, first + h)),
            spec((2, block, seq), lambda h, w: (0, first + h, 0)),
            fixed((seq, 128)),
        ],
        [
            struct((seq, width), BF16),
            struct((2, width, seq), BF16),
            struct((seq, 128), F32),
        ],
        [pltpu.VMEM((seq, seq), F32)],
        micros=11,
        aliases={7: 0, 8: 1} if before else None,
    )(where, projected, projected, projected, x, column, row, *before)


def attend_back_kernel(dims, where, q, k, v, grad, logs_a, logs_b, attn, column, row, *refs):
    out, sums, bias = refs
    mine, per = dims
    step = pl.program_id(0)
    pair = pair_of(where, step, mine, per)
    out[3] = attn[...]

    @pl.when(step == 0)
    def _():
        bias[...] = jnp.where(column[...] == row[...], 0.0, -1e30)

    lanes = lax.broadcasted_iota(jnp.int32, (1, 128), 1)
    heads = q.shape[1] // HEAD_DIM
    for h in range(heads):
        part = slice(h * HEAD_DIM, (h + 1) * HEAD_DIM)
        picked = jnp.where(lanes == pair * heads + h, logs_a[...] + logs_b[...], 0.0)
        logs = jnp.sum(picked, axis=1, keepdims=True)
        query = q[:, part] * BF16(HEAD_DIM**-0.5)
        scores = dot_t(query, k[:, part]) + bias[...]
        probs = jnp.exp(scores - logs)
        grad_probs = dot_t(grad[:, part], v[:, part])
        weighted = probs * grad_probs
        low = (weighted - probs * jnp.sum(weighted, axis=1, keepdims=True)).astype(BF16)
        grad_q = (dot(low, k[:, part]) * (HEAD_DIM**-0.5)).astype(BF16)
        grad_k = t_dot(low, query).astype(BF16)
        grad_v = t_dot(probs.astype(BF16), grad[:, part]).astype(BF16)
        for m, value in enumerate((grad_q, grad_k, grad_v)):
            out[m, :, part] = value
            sums[m, :, part] = rows_sum(value.astype(F32))


def pair_of(where, step, mine, per):
    parity = where[1] if mine else 1 - where[1]
    return (2 * (step // per) + parity) * per + lax.rem(step, per)


def attention_back(where, projected, grad, logs, attn, column, row, mine, part):
    seq, width = grad.shape
    block = 2 * HEAD_DIM
    each = width // block
    per = part // block

    def pairs(first):
        return spec((seq, block), lambda h, w: (0, first + pair_of(w, h, mine, per)))

    return call(
        partial(attend_back_kernel, (mine, per)),
        (each // 2,),
        [
            pairs(0),
            pairs(each),
            pairs(2 * each),
            pairs(0),
            fixed((seq, 128)),
            fixed((seq, 128)),
            pairs(0),
            fixed((seq, 1)),
            fixed((1, seq)),
        ],
        [
            spec((4, seq, block), lambda h, w: (0, 0, h)),
            spec((3, 1, block), lambda h, w: (0, 0, h)),
        ],
        [struct((4, seq, width // 2), BF16), struct((3, 1, width // 2), F32)],
        [pltpu.VMEM((seq, seq), F32)],
        micros=13,
    )(where, projected, projected, projected, grad, *logs, attn, column, row)


def out_kernel(group, where, context, x, own, rest, bias, gain, shift, hidden, low, turned):
    rows = own.shape[0]
    total = bias[...] + x[...].astype(F32)
    for s in range(group):
        start = pl.multiple_of(natural(where, s, group) * rows, 128)
        weight = own[...] if s == 0 else rest[(s - 1) * rows : s * rows, :]
        total = total + dot(context[:, pl.ds(start, rows)], weight)
    hidden[...] = total
    unit, _ = normalise(total)
    value = (unit * gain[...] + shift[...]).astype(BF16)
    low[...] = value
    turned[...] = value.T


def out_norm(where, context, x, w_out, rest_out, bias, gain, shift, group):
    seq, width = x.shape
    rows = w_out.shape[0]
    block = seq // 2
    vector = fixed((1, width))
    return call(
        partial(out_kernel, group),
        (seq // block,),
        [
            spec((block, width), lambda i, w: (i, 0)),
            spec((block, width), lambda i, w: (i, 0)),
            fixed((rows, width)),
            fixed((width - rows, width)),
            vector,
            vector,
            vector,
        ],
        [spec((block, width), lambda i, w: (i, 0))] * 2
        + [spec((width, block), lambda i, w: (0, i))],
        [
            struct((seq, width), F32),
            struct((seq, width), BF16),
            struct((width, seq), BF16),
        ],
        micros=6,
    )(where, context, x, w_out, rest_out, bias, gain, shift)


def inner_kernel(dims, where, x, own, a, b, c, d, bias, act, early, late, slope, rolled, *scratch):
    group, half = dims
    unit = pl.program_id(0)

    @pl.when(unit == 0)
    def _():
        roll_into(rolled, x, where, own.shape[0], group)

    rest = stream(unit, (a, b, c, d), *scratch)
    rows = own.shape[0]
    total = dot(rolled[:, :rows], own[...]) + dot(rolled[:, rows:], rest) + bias[...]
    below = 0.5 + 0.5 * lax.erf(total * (0.5**0.5))
    value = (total * below).astype(BF16)
    act[...] = value
    half_seq = early.shape[1]
    early[...] = value[:half_seq].T
    late[...] = value[half_seq:].T
    density = jnp.exp(-0.5 * total * total) * ((2.0 * jnp.pi) ** -0.5)
    slope[...] = (below + total * density).astype(BF16)


def inner(where, x, w_in, parts, bias, group):
    seq, width = x.shape
    rows, columns = w_in.shape
    half, _, _, block = parts[0].shape
    chips = 2 * half

    def columns_at(height):
        return spec((height, block), lambda u, w: (0, block_of(w, u, chips)))

    return call(
        partial(inner_kernel, (group, half)),
        (2 * chips,),
        [fixed((seq, width)), columns_at(rows)] + [ANYWHERE] * 4 + [columns_at(1)],
        [
            columns_at(seq),
            spec((block, seq // 2), lambda u, w: (block_of(w, u, chips), 0)),
            spec((block, seq // 2), lambda u, w: (block_of(w, u, chips), 0)),
            columns_at(seq),
        ],
        [
            struct((seq, columns), BF16),
            struct((columns, seq // 2), BF16),
            struct((columns, seq // 2), BF16),
            struct((seq, columns), BF16),
        ],
        [pltpu.VMEM((seq, width), BF16)] + stream_scratch(parts),
        micros=16,
    )(where, x, w_in, *parts, bias)


def outer_kernel(
    dims,
    where,
    act,
    own,
    a,
    b,
    c,
    d,
    hidden,
    cotangent,
    gain_one,
    shift_one,
    bias,
    gain_two,
    shift_two,
    out,
    grad,
    low,
    low_other,
    sums,
    total,
    picked,
    kept,
    given_rows,
    kept_sems,
    *scratch,
):
    group, half = dims
    step = pl.program_id(0)
    ff_rows = own.shape[0]
    rows = a.shape[2]
    late = [
        pltpu.make_async_copy(hidden, kept, kept_sems.at[0]),
        pltpu.make_async_copy(cotangent, given_rows, kept_sems.at[1]),
    ]
    stream_whole(step, (a, b, c, d), *scratch)

    @pl.when(step == 1)
    def _():
        for copy in late:
            copy.start()

    @pl.when(step == 0)
    def _():
        start = pl.multiple_of(where[0] * ff_rows, 128)
        total[...] = dot(act[:, pl.ds(start, ff_rows)], own[...])

    @pl.when(step > 0)
    def _():
        at = 0
        for i in range(half):
            block = block_of(where, (step - 1) * half + i, 2 * half)
            for s in range(1, group):
                start = natural(where, s, group) * ff_rows + block * rows
                picked[:, at : at + rows] = act[:, pl.ds(pl.multiple_of(start, rows), rows)]
                at += rows
        rest = scratch[0][lax.rem(step - 1, 2)].reshape(-1, a.shape[3])
        total[...] += dot(picked[...], rest)

    @pl.when(step == 4)
    def _():
        for copy in late:
            copy.wait()
        unit_one, _ = normalise(kept[...])
        second = unit_one * gain_one[...] + shift_one[...] + total[...] + bias[...]
        unit, inverse = normalise(second)
        out[...] = (unit * gain_two[...] + shift_two[...]).astype(BF16)
        given = given_rows[...].astype(F32)
        back = normalise_back(given, unit, inverse, gain_two[...])
        grad[...] = back
        rounded = back.astype(BF16)
        low[...] = rounded
        size = low_other.shape[1]
        start = pl.multiple_of((1 - where[1]) * size, 128)
        low_other[...] = low[:, pl.ds(start, size)]
        sums[0:1, :] = rows_sum(given * unit)
        sums[1:2, :] = rows_sum(given)
        sums[2:3, :] = rows_sum(rounded.astype(F32))


def outer(where, act, w_down, parts, hidden, cotangent, vectors, group):
    seq, width = hidden.shape
    rows = w_down.shape[0]
    half, steps, size, _ = parts[0].shape
    full = fixed((seq, width))
    vector = fixed((1, width))
    return call(
        partial(outer_kernel, (group, half)),
        (5,),
        [fixed(act.shape), fixed((rows, width))]
        + [ANYWHERE] * 6
        + [vector] * 5,
        [full, full, full, fixed((seq, width // 2)), fixed((8, width))],
        [
            struct((seq, width), BF16),
            struct((seq, width), F32),
            struct((seq, width), BF16),
            struct((seq, width // 2), BF16),
            struct((8, width), F32),
        ],
        [
            pltpu.VMEM((seq, width), F32),
            pltpu.VMEM((seq, half * steps * size), BF16),
            pltpu.VMEM((seq, width), F32),
            pltpu.VMEM((seq, width), BF16),
            pltpu.SemaphoreType.DMA((2,)),
        ]
        + whole_scratch(parts),
        micros=60,
    )(where, act, w_down, *parts, hidden, cotangent, *vectors)


def slope_kernel(
    dims, where, low, own, a, b, c, d, given, grad, grad_other, sums, slope, slope_sem, *scratch
):
    group, half, width = dims
    step = pl.program_id(0)
    ff_rows = own.shape[0]
    rows = a.shape[2]

    def finish(back, start, size):
        place = pl.ds(pl.multiple_of(start, size), size)
        value = (back * slope[:, place].astype(F32)).astype(BF16)
        grad[:, place] = value
        sums[:, place] = rows_sum(value.astype(F32))
        piece = min(size, width)
        for at in range(0, size, piece):
            block = (start + at) // width
            inside = start + at - block * width

            @pl.when(lax.rem(block, 2) != where[1])
            def _(at=at, block=block, inside=inside):
                there = pl.multiple_of((block // 2) * width + inside, piece)
                grad_other[:, pl.ds(there, piece)] = value[:, at : at + piece]

    slopes = pltpu.make_async_copy(given, slope, slope_sem)
    stream_whole(step, (a, b, c, d), *scratch)

    @pl.when(step == 0)
    def _():
        slopes.start()
        back = dot_t(low[...], own[...])
        slopes.wait()
        finish(back, where[0] * ff_rows, ff_rows)

    @pl.when(step > 0)
    def _():
        rest = scratch[0][lax.rem(step - 1, 2)].reshape(-1, a.shape[3])
        back = dot_t(low[...], rest)
        at = 0
        for i in range(half):
            block = block_of(where, (step - 1) * half + i, 2 * half)
            for s in range(1, group):
                start = natural(where, s, group) * ff_rows + block * rows
                finish(back[:, at : at + rows], start, rows)
                at += rows


def slope_back(where, low, w_down, parts, slope, part, group):
    seq, width = low.shape
    rows = w_down.shape[0]
    half = parts[0].shape[0]
    columns = slope.shape[1]
    return call(
        partial(slope_kernel, (group, half, part)),
        (5,),
        [fixed((seq, width)), fixed((rows, width))]
        + [ANYWHERE] * 5,
        [fixed((seq, columns)), fixed((seq, columns // 2)), fixed((1, columns))],
        [
            struct((seq, columns), BF16),
            struct((seq, columns // 2), BF16),
            struct((1, columns), F32),
        ],
        [pltpu.VMEM((seq, columns), BF16), pltpu.SemaphoreType.DMA(())] + whole_scratch(parts),
        micros=14,
    )(where, low, w_down, *parts, slope)


def inner_back_kernel(
    dims,
    where,
    grad_inner,
    own,
    a,
    b,
    c,
    d,
    grad_two,
    hidden,
    gain,
    own_out,
    rest_out,
    grad_one,
    low_one,
    grad_context,
    sums,
    total,
    *scratch,
):
    group, half = dims
    unit = pl.program_id(0)
    rows = own.shape[0]

    def place(s):
        return pl.ds(pl.multiple_of(natural(where, s, group) * rows, 128), rows)

    @pl.when(unit == 0)
    def _():
        total[...] = jnp.zeros_like(total)

    rest = stream(unit, (a, b, c, d), *scratch)
    total[:, :rows] += dot_t(grad_inner[...], own[...])
    total[:, rows:] += dot_t(grad_inner[...], rest)

    @pl.when(unit == 4 * half - 1)
    def _():
        unit_one, inverse = normalise(hidden[...])
        for s in range(group):
            grad_one[:, place(s)] = total[:, s * rows : (s + 1) * rows]
        given = grad_one[...] + grad_two[...]
        back = normalise_back(given, unit_one, inverse, gain[...])
        grad_one[...] = back
        rounded = back.astype(BF16)
        low_one[...] = rounded
        sums[0:1, :] = rows_sum(given * unit_one)
        sums[1:2, :] = rows_sum(given)
        sums[2:3, :] = rows_sum(rounded.astype(F32))
        grad_context[:, place(0)] = dot_t(rounded, own_out[...]).astype(BF16)
        for s in range(1, group):
            piece = rest_out[(s - 1) * rows : s * rows, :]
            grad_context[:, place(s)] = dot_t(rounded, piece).astype(BF16)


def inner_back(where, grad_inner, w_in, parts, grad_two, hidden, gain, w_out, rest_out, group):
    seq, width = hidden.shape
    rows, columns = w_in.shape
    half, _, _, block = parts[0].shape
    chips = 2 * half
    full = fixed((seq, width))

    def columns_at(height):
        return spec((height, block), lambda u, w: (0, block_of(w, u, chips)))

    return call(
        partial(inner_back_kernel, (group, half)),
        (2 * chips,),
        [columns_at(seq), columns_at(rows)]
        + [ANYWHERE] * 4
        + [full, full, fixed((1, width)), fixed((rows, width)), fixed((width - rows, width))],
        [full, full, full, fixed((8, width))],
        [
            struct((seq, width), F32),
            struct((seq, width), BF16),
            struct((seq, width), BF16),
            struct((8, width), F32),
        ],
        [pltpu.VMEM((seq, width), F32)] + stream_scratch(parts),
        micros=19,
    )(where, grad_inner, w_in, *parts, grad_two, hidden, gain, w_out, rest_out)


def input_back_kernel(dims, where, mine, others, own, a, b, c, d, first, out, total, *scratch):
    group, half, qkv_width = dims
    unit = pl.program_id(0)
    rows, columns = own.shape

    @pl.when(unit == 0)
    def _():
        total[...] = jnp.zeros_like(total)

    rest = stream(unit, (a, b, c, d), *scratch)
    block = block_of(where, unit, 2 * half)
    inside = block * columns < qkv_width
    same = lax.rem(block, 2) == where[1]

    @pl.when(inside)
    def _():
        grad = jnp.where(same, mine[0], others[0])
        total[:, :rows] += dot_t(grad, own[...])
        total[:, rows:] += dot_t(grad, rest)

    @pl.when(unit == 4 * half - 1)
    def _():
        for s in range(group):
            place = pl.ds(pl.multiple_of(natural(where, s, group) * rows, 128), rows)
            out[:, place] = first[:, place] + total[:, s * rows : (s + 1) * rows]


def input_back(where, mine, others, first, w_qkv, parts, group):
    seq, width = first.shape
    rows, qkv_width = w_qkv.shape
    half, _, _, block = parts[0].shape
    chips = 2 * half
    each = width // block
    top = qkv_width // block - 1

    def plane(u, w):
        n = jnp.minimum(block_of(w, u, chips), top)
        return (n // each, 0, lax.rem(n, each) // 2)

    return call(
        partial(input_back_kernel, (group, half, qkv_width)),
        (2 * chips,),
        [
            spec((1, seq, block), plane),
            spec((1, seq, block), plane),
            spec((rows, block), lambda u, w: (0, jnp.minimum(block_of(w, u, chips), top))),
        ]
        + [ANYWHERE] * 4
        + [fixed((seq, width))],
        fixed((seq, width)),
        struct((seq, width), F32),
        [pltpu.VMEM((seq, width), F32)] + stream_scratch(parts),
        micros=12,
    )(where, mine, others, w_qkv, *parts, first)


def widen_kernel(dims, where, *refs):
    parts, outs = refs[:4], refs[4:]
    phases, kinds, more = dims
    chips = 1 << phases
    half = chips // 2
    if more:
        outs, extra = outs[:-1], outs[-1]
        extra[...] = jnp.zeros_like(extra)
    for side in range(2):
        core = where[1] if side == 0 else 1 - where[1]
        for order in range(chips):
            chip = where[2 + side * chips + order]
            given = parts[2 * side + order // half].at[order % half]
            at, row = 0, 0
            for by_rows, rows, count in kinds:
                targets, at = outs[at : at + count], at + count
                columns = given.shape[1]
                step = min(rows, 128)

                @pl.loop(0, rows // step)
                def _(index, row=row, rows=rows, step=step, targets=targets, by_rows=by_rows):
                    inside = pl.multiple_of(index * step, step)
                    value = given[pl.ds(row + inside, step), :].astype(F32)
                    if by_rows:
                        down = pl.ds(pl.multiple_of(chip * rows + inside, step), step)
                        across = pl.ds(pl.multiple_of(core * columns, 128), columns)
                        targets[0][down, across] = value
                        return
                    base = 0
                    for out in targets:
                        first = (2 * chip + core) * columns - base

                        @pl.when((first >= 0) & (first < out.shape[1]))
                        def _(out=out, first=first):
                            across = pl.ds(pl.multiple_of(first, 128), columns)
                            out[pl.ds(inside, step), across] = value

                        base += out.shape[1]

                row += rows
            if more:
                extra[...] += given[row:, :].astype(F32)


def widen(where, parts, phases, kinds, more=0):
    shapes = [shape for *_, given in kinds for shape in given]
    if more:
        shapes.append((more, parts[0].shape[2]))
    short = [(by_rows, rows, len(given)) for by_rows, rows, given in kinds]
    return call(
        partial(widen_kernel, (phases, short, more)),
        (1,),
        [fixed(part.shape) for part in parts],
        [fixed(shape) for shape in shapes],
        [struct(shape, F32) for shape in shapes],
        micros=4,
    )(where, *parts)


def grads_kernel(dims, where, *refs):
    orders, adds, last, group, cuts, extra = dims
    units = len(orders)
    step = pl.program_id(0)
    at = 0
    outs = refs[units * (2 + 2 * cuts + adds) + extra :]
    for u in range(units):
        right, right_other = refs[at : at + 2]
        at += 2
        value = 0.0
        for given in (right, right_other):
            size = given.shape[1] // cuts
            for i in range(cuts):
                value = value + dot(refs[at][0], given[0, i * size : (i + 1) * size, :])
                at += 1
        for add in refs[at : at + adds]:
            value = value + add[0].astype(F32)
        at += adds
        value = value.astype(BF16)
        if not last:
            outs[0][u] = value
            continue
        for s in range(group):

            @pl.when(step == s)
            def _(s=s, value=value):
                outs[s][: value.shape[0], :] = value
                if extra:
                    outs[s][value.shape[0] :, :] = refs[-group - 1][s]


def grads(where, left, right, maps, shape, units, received, group, extra=None):
    rows, columns = shape
    cuts = len(left[0])
    seq = left[0][0].shape[2]
    left_map, right_map, other_map = maps
    last = units == [0]
    ins, args = [], []
    for order in units:
        lefts = spec((1, rows, seq), partial(left_map, order))
        ins.append(spec((1, seq * cuts, columns), partial(right_map, order)))
        ins.append(spec((1, seq * cuts, columns), partial(other_map, order)))
        ins += [lefts] * (2 * cuts)
        args += [right[0], right[1], *left[0], *left[1]]
        for phase, value in enumerate(received):
            index = order >> (phase + 1)
            ins.append(spec((1, rows, columns), lambda s, w, index=index: (index, s, 0)))
            args.append(value)
    count = len(units)
    more = 0 if extra is None else extra.shape[1]
    if more:
        ins.append(fixed(extra.shape))
        args.append(extra)
    if last:
        outs = [fixed((rows + more, columns))] * group
        out_shape = [struct((rows + more, columns), BF16)] * group
    else:
        outs = [spec((count, rows, columns), lambda s, w: (0, s, 0))]
        out_shape = [struct((count, group * rows, columns), BF16)]
    return call(
        partial(grads_kernel, (units, len(received), last, group, cuts, int(more > 0))),
        (group,),
        ins,
        outs,
        out_shape,
        micros=6,
    )(where, *args)


def after(value, *others):
    return lax.optimization_barrier((value, others))[0]


def local(
    chips,
    group,
    tokens,
    segments,
    lengths,
    cotangent,
    w_qkv,
    b_qv,
    w_out,
    b_out,
    gain_one,
    shift_one,
    w_in,
    b_in,
    w_down,
    b_down,
    gain_two,
    shift_two,
):
    reps = 2 * chips
    phases = chips.bit_length() - 1
    core = lax.axis_index("core")
    chip = lax.axis_index("chip")
    rank = chip * 2 + core
    own = lax.axis_index("shard")
    _, seq_len, model_width = tokens.shape
    ff_rows = w_down.shape[0]
    ff_width = w_in.shape[1]
    qkv_width = w_qkv.shape[1]

    def from_shard(value, step):
        return lax.ppermute(value, "shard", [(i, (i - step) % group) for i in range(group)])

    def to_shard(value, step):
        return lax.ppermute(value, "shard", [(i, (i + step) % group) for i in range(group)])

    def sibling(value):
        return lax.ppermute(value, "core", [(0, 1), (1, 0)])

    def bit(phase, which):
        return 1 << ((phase + which) % phases)

    def swap(value, phase):
        pairs = [
            (q * 2 + c, (q ^ bit(phase, c)) * 2 + c) for q in range(chips) for c in range(2)
        ]
        return lax.ppermute(value, REP, pairs)

    def table(which):
        orders = []
        for order in range(chips):
            mask = sum(bit(f, which) for f in range(phases) if order >> f & 1)
            orders.append(mask)
        return orders

    masks = jnp.where(core == 0, jnp.array(table(0)), jnp.array(table(1)))
    masks_other = jnp.where(core == 0, jnp.array(table(1)), jnp.array(table(0)))
    where = jnp.concatenate(
        [jnp.stack([own, core]), chip ^ masks, chip ^ masks_other]
    ).astype(jnp.int32)

    def gather(value, *gates):
        for phase in range(phases - 1):
            value = jnp.concatenate([value, swap(value, phase)], axis=0)
        rest = swap(value, phases - 1)
        return value, rest, sibling(after(value, gates)), sibling(rest)

    w_one = jnp.concatenate([w_qkv, w_out], axis=1)
    part = w_one.shape[1] // reps
    rows = w_one.shape[0]
    piece_one = lax.dynamic_slice_in_dim(w_one, rank * part, part, axis=1)
    part_in = ff_width // reps
    piece_in = lax.dynamic_slice_in_dim(w_in, rank * part_in, part_in, axis=1)
    part_down = ff_rows // reps
    piece_down = lax.dynamic_slice_in_dim(w_down, rank * part_down, part_down, axis=0)

    class Gather:

        def __init__(self, value):
            self.value = value
            self.first = swap(value, 0)

        def step(self, *gates):
            other = self.first
            for phase in range(phases - 1):
                self.value = after(jnp.concatenate([self.value, other], axis=0), gates)
                other = swap(self.value, phase + 1)
            self.rest = other
            self.side = sibling(self.value)

        def finish(self, *gates):
            self.parts = (self.value, self.rest, self.side, sibling(after(self.rest, gates)))

    got_one = [from_shard(piece_one, s) for s in range(1, group)]

    vectors = (b_qv, b_out, gain_one, shift_one, b_in, b_down, gain_two, shift_two)
    sizes = [v.shape[0] for v in vectors]
    packed = jnp.concatenate(after(vectors, piece_one))
    first_parts = Gather(jnp.stack(got_one)[None])
    first_parts.step()
    packed = after(packed, got_one)
    got_packed = [from_shard(packed, s) for s in range(1, group)]
    first_parts.finish(got_packed)
    parts_one = first_parts.parts
    piece_in = after(piece_in, parts_one[3])
    got_in = [from_shard(piece_in, s) for s in range(1, group)]
    piece_down = after(piece_down, parts_one[3])

    relative = jnp.stack([packed] + got_packed)
    ordered = jnp.concatenate([relative, relative], axis=0)
    ordered = lax.dynamic_slice_in_dim(ordered, (group - own) % group, group, axis=0)
    full, start = [], 0
    for size in sizes:
        full.append(ordered[:, start : start + size].reshape(1, -1).astype(F32))
        start += size
    bias_qv, bias_out, norm_gone, norm_sone, bias_in, bias_down, norm_gtwo, norm_stwo = full
    none = jnp.zeros((1, model_width), F32)
    bias_qkv = jnp.concatenate(
        [bias_qv[:, :model_width], none, bias_qv[:, model_width:], none], axis=1
    )
    kind = segments[0] * 2 + (jnp.arange(seq_len) < lengths[0]).astype(jnp.int32)
    column, row = kind[:, None], kind[None, :]

    flat_in = tokens[0]
    projected, rest_out = qkv(where, flat_in, w_qkv, parts_one, bias_qkv, group)
    parts_in = Gather(after(jnp.stack(got_in)[None], projected))
    got_down = [from_shard(piece_down, s) for s in range(1, group)]
    count = model_width // (4 * HEAD_DIM)
    context, turned, logs_a = attention(where, projected, flat_in, column, row, 0, count)
    parts_in.step(logs_a)
    context, turned, logs_b = attention(
        where,
        projected,
        flat_in,
        column,
        row,
        count,
        count,
        (context, turned),
    )
    first_left = ([turned], [sibling(turned)])
    parts_down = Gather(after(jnp.stack(got_down)[None], logs_b))
    parts_down.step(logs_b)
    hidden, normed, normed_turned = out_norm(
        where,
        context,
        flat_in,
        w_out,
        rest_out,
        bias_out,
        norm_gone,
        norm_sone,
        group,
    )
    parts_in.finish(hidden)
    parts_in = parts_in.parts
    in_left = ([normed_turned[None]], [sibling(normed_turned)[None]])
    where_down = where
    normed = after(normed, parts_down.first)
    act, *act_turned, slope = inner(where, normed, w_in, parts_in, bias_in, group)
    parts_down.finish(act)
    parts_down = parts_down.parts
    if part_down % 128:
        merged = jnp.zeros((group - 1, ff_rows, model_width), BF16)
        for unit in range(reps):
            piece = parts_down[2 * unit // chips][unit % (chips // 2)]
            at = block_of(where, unit, chips) * part_down
            merged = lax.dynamic_update_slice_in_dim(merged, piece, at, axis=1)
        fourth = ff_rows // 4
        parts_down = [merged[:, b * fourth : (b + 1) * fourth][None] for b in (0, 2, 1, 3)]
        where_down = jnp.stack([own, 0, 0, 1, 0, 1]).astype(jnp.int32)
    down_left = ([v[None] for v in act_turned], [sibling(v)[None] for v in act_turned])
    output_rows, grad_second, grad_branch, branch_other, sums_two = outer(
        where_down,
        act,
        w_down,
        parts_down,
        hidden,
        cotangent[0],
        (norm_gone, norm_sone, bias_down, norm_gtwo, norm_stwo),
        group,
    )

    class Scatter:

        def __init__(self, left, right, maps, shape):
            self.fixed = (where, left, right, maps, shape)
            self.received = []

        def send(self, *gates):
            phase = len(self.received)
            units = list(range(1 << phase, chips, 2 << phase))
            received = after(self.received, gates) if phase else []
            sent = grads(*self.fixed, units, received, group)[0]
            self.received.append(swap(sent, phase))
            return sent

        def send_rest(self, *gates):
            while len(self.received) < phases:
                sent = self.send(*gates)
            return sent

        def finish(self, *gates, extra=None):
            received = after(self.received, gates)
            parts = grads(*self.fixed, [0], received, group, extra)
            self.own = parts[0]
            self.given = [to_shard(parts[s], s) for s in range(1, group)]
            return parts[0]

        def total(self):
            total = self.own.astype(F32)
            for value in self.given:
                total = total + value.astype(F32)
            return total

    half = model_width // 2
    part_rows = ff_rows // chips
    down_maps = (
        lambda o, s, w: (0, natural(w, s, group) * chips + w[2 + o], 0),
        lambda o, s, w: (0, 0, w[1]),
        lambda o, s, w: (0, 0, 0),
    )
    down_right = (grad_branch[None], sibling(branch_other)[None])
    down = Scatter(down_left, down_right, down_maps, (part_rows, half))
    sent = down.send()
    grad_inner, inner_other, sums_in = slope_back(
        where_down, after(grad_branch, sent), w_down, parts_down, slope, part_in, group
    )
    grad_first, grad_attn, grad_context, sums_one = inner_back(
        where,
        after(grad_inner, in_left),
        w_in,
        parts_in,
        grad_second,
        hidden,
        norm_gone,
        w_out,
        rest_out,
        group,
    )
    in_other = sibling(inner_other)
    sent = down.send_rest(grad_first, first_left)
    in_maps = (
        lambda o, s, w: (0, natural(w, s, group), 0),
        lambda o, s, w: (0, 0, 2 * w[2 + o] + w[1]),
        lambda o, s, w: (0, 0, w[2 + o]),
    )
    in_right = after((grad_inner[None], in_other[None]), sent)
    inward = Scatter(in_left, in_right, in_maps, (rows, part_in))
    sent = inward.send()
    logs = (logs_a, logs_b)
    others, sums_others = attention_back(
        where, projected, after(grad_context, sent), logs, grad_attn, column, row, False, part
    )
    done = down.finish(others)
    other_proj = sibling(after(others, done))
    mine, sums_mine = attention_back(
        where, projected, after(grad_context, done), logs, grad_attn, column, row, True, part
    )
    sent = inward.send_rest(mine)
    each = model_width // part

    def plane(order, w):
        return 2 * w[2 + order] + w[1]

    def compact(o, s, w):
        return (plane(o, w) // each, 0, lax.rem(plane(o, w), each) // 2)

    first_maps = (
        lambda o, s, w: (plane(o, w) // (3 * each), natural(w, s, group), 0),
        compact,
        compact,
    )
    first_right = after((mine, other_proj), sent, down.given)
    first = Scatter(first_left, first_right, first_maps, (rows, part))
    sent = first.send()
    def blocks(core_parity):
        value = jnp.where(core == core_parity, sums_mine, sums_others)
        return value.reshape(3, -1, 1, part)

    sums_proj = jnp.concatenate([blocks(0), blocks(1)], axis=2).reshape(3, model_width)
    small = (
        jnp.concatenate([sums_proj[0], sums_proj[2]]),
        sums_one[2],
        sums_one[0],
        sums_one[1],
        sums_in[0],
        sums_two[2],
        sums_two[0],
        sums_two[1],
    )
    small = jnp.concatenate([v.reshape(group, -1) for v in small], axis=1)
    grad_input = input_back(
        where, after(mine, sent), others, grad_first, w_qkv, parts_one, group
    )
    done = inward.finish(grad_input)
    sent = first.send_rest(done)
    small = jnp.concatenate([small, small], axis=0)
    small = lax.dynamic_slice_in_dim(small, own, group, axis=0)
    extra = -(-small.shape[1] // (16 * part)) * 16
    padded = jnp.pad(small, ((0, 0), (0, extra * part - small.shape[1])))
    padded = padded.reshape(group, extra, part).astype(BF16)
    done = first.finish(sent, extra=padded)
    gather_down = Gather(after(down.total().astype(BF16)[None], done))
    gather_down.step()
    gather_down.finish()
    (grad_wdown,) = widen(
        where, gather_down.parts, phases, [(True, part_rows, [(ff_rows, model_width)])]
    )
    shares = jnp.concatenate([inward.total(), first.total()], axis=0).astype(BF16)
    final = Gather(shares[None])
    final.step(gather_down.parts[3])
    final.finish(grad_wdown)
    grad_win, grad_wqkv, grad_wout, total = widen(
        where,
        final.parts,
        phases,
        [
            (False, rows, [(rows, ff_width)]),
            (False, rows, [(rows, qkv_width), (rows, model_width)]),
        ],
        extra,
    )
    total = total.reshape(-1)

    vecs, start = [], 0
    for size in sizes:
        vecs.append(total[start : start + size])
        start += size

    return (
        output_rows.reshape(tokens.shape),
        grad_input.reshape(tokens.shape),
        grad_wqkv,
        vecs[0],
        grad_wout,
        vecs[1],
        vecs[2],
        vecs[3],
        grad_win,
        vecs[4],
        grad_wdown,
        vecs[5],
        vecs[6],
        vecs[7],
    )


def solution(mesh):
    reps, group = mesh.devices.shape
    fine = Mesh(mesh.devices.reshape(reps // 2, 2, group), ALL)
    rows = P(ALL, None, None)
    matrix = P("shard", None)
    vector = P("shard")
    in_specs = (
        rows,
        P(ALL, None),
        P(ALL),
        rows,
        matrix,
        vector,
        matrix,
        vector,
        vector,
        vector,
        matrix,
        vector,
        matrix,
        vector,
        vector,
        vector,
    )
    out_specs = (
        rows,
        rows,
        matrix,
        vector,
        matrix,
        vector,
        vector,
        vector,
        matrix,
        vector,
        matrix,
        vector,
        vector,
        vector,
    )
    return jax.shard_map(
        partial(local, reps // 2, group),
        mesh=fine,
        in_specs=in_specs,
        out_specs=out_specs,
        check_vma=False,
    )
```
